32 devices in a mesh: dp: 4 (over y, x), seq: 8 (over z, core).
Axes of the slice: x: 2, y: 2, z: 4, core: 2. Of those that a mesh axis runs over, the one named last changes fastest.
Arguments:
- layer_input: bfloat16 [2, 4, 4096, 512], P(None, 'dp', 'seq'), may hold values from -6 to 6
- cotangent: bfloat16 [2, 4, 4096, 512], P(None, 'dp', 'seq'), may hold values from -6 to 6
- doc_len: int32 [2, 4, 1], P(None, 'dp'), may hold values from 2048 to 4096, as said below
- doc_offset: int32 [2, 4, 1], P(None, 'dp'), may hold values from 0 to 2048, as said below
- w_query: bfloat16 [512, 512], P(('dp', 'seq')), may hold values from -0.375 to 0.375
- w_key: bfloat16 [512, 512], P(('dp', 'seq')), may hold values from -0.375 to 0.375
- w_value: bfloat16 [512, 512], P(('dp', 'seq')), may hold values from -0.25 to 0.25
- w_out: bfloat16 [512, 512], P(('dp', 'seq')), may hold values from -1 to 1
- w_gate_attn: bfloat16 [512, 512], P(('dp', 'seq')), may hold values from -0.25 to 0.25
- w_gate_ffn: bfloat16 [512, 512], P(('dp', 'seq')), may hold values from -0.25 to 0.25
- w_in: bfloat16 [512, 2048], P(('dp', 'seq')), may hold values from -0.25 to 0.25
- w_back: bfloat16 [2048, 512], P(('dp', 'seq')), may hold values from -0.125 to 0.125
- norm_attn: bfloat16 [512], P(('dp', 'seq')), may hold values from 0.5 to 1.5
- norm_ffn: bfloat16 [512], P(('dp', 'seq')), may hold values from 0.5 to 1.5
- bias_attn: bfloat16 [512], P(('dp', 'seq')), may hold values from -3 to 3
- bias_ffn: bfloat16 [512], P(('dp', 'seq')), may hold values from -3 to 3
Outputs:
- output: bfloat16 [2, 4, 4096, 512], P(None, 'dp', 'seq')
- grad_input: float32 [2, 4, 4096, 512], P(None, 'dp', 'seq')
- grad_w_query: float32 [512, 512], P(('dp', 'seq'))
- grad_w_key: float32 [512, 512], P(('dp', 'seq'))
- grad_w_value: float32 [512, 512], P(('dp', 'seq'))
- grad_w_out: float32 [512, 512], P(('dp', 'seq'))
- grad_w_gate_attn: float32 [512, 512], P(('dp', 'seq'))
- grad_w_gate_ffn: float32 [512, 512], P(('dp', 'seq'))
- grad_w_in: float32 [512, 2048], P(('dp', 'seq'))
- grad_w_back: float32 [2048, 512], P(('dp', 'seq'))
- grad_norm_attn: float32 [512], P(('dp', 'seq'))
- grad_norm_ffn: float32 [512], P(('dp', 'seq'))
- grad_bias_attn: float32 [512], P(('dp', 'seq'))
- grad_bias_ffn: float32 [512], P(('dp', 'seq'))
The draws below stay inside these ranges and needn't reach their ends.
Inputs may be any that keep to these rules, and one draw needn't show every extreme that they name: The document of region r of a slot takes positions r * 4096 + doc_offset to r * 4096 + doc_offset + doc_len - 1 of that slot; the other positions are padding. Every draw has a document of 4096 positions and one of 2048. doc_offset + doc_len <= 4096 for every document.
All inputs are finite; a program needn't handle non-finite values.
Results may differ from the reference program's by a relative error of at most 0.018.
Values may be sent and summed in bfloat16 or wider, within the bound.
A program may use at most 192 MiB of HBM per device.

```python
import jax
import jax.numpy as jnp
from jax import lax

D = 512
HEADS = 8
HEAD_DIM = 64
FF = 2048
MICRO = 2
DOC_MIN = 2048
DOC_MAX = 4096
SLOTS = 4
SLOT = 4096
REGIONS = 1


def doc_bounds(key):
    base_key = jax.random.fold_in(key, 11)
    first_key, second_key = jax.random.split(base_key)
    grid_shape = (MICRO, SLOTS, REGIONS)
    total_docs = MICRO * SLOTS * REGIONS
    length = jax.random.randint(first_key, grid_shape, DOC_MIN, DOC_MAX + 1)
    spare_room = DOC_MAX - length
    offset = jax.random.randint(second_key, grid_shape, 0, spare_room + 1)
    doc_index = jnp.arange(total_docs).reshape(grid_shape)
    length = jnp.where(doc_index == 0, DOC_MAX, jnp.where(doc_index == total_docs - 1, DOC_MIN, length))
    offset = jnp.where(doc_index == 0, 0, jnp.where(doc_index == total_docs - 1, DOC_MAX - DOC_MIN, offset))
    return (length.astype(jnp.int32), offset.astype(jnp.int32))


def draw_doc_len(key, part):
    return doc_bounds(key)[0]


def draw_doc_offset(key, part):
    return doc_bounds(key)[1]


def steps_of(key, dims, shards, low, largest):
    factor_of = 1.0
    for position, shards_of in shards:
        draws = jax.random.uniform(jax.random.fold_in(jax.random.fold_in(key, 6), position), (shards_of,), jnp.float32, low / len(shards), largest / len(shards))
        factor_of = factor_of * jnp.repeat(jnp.exp(draws), dims[position] // shards_of).reshape((-1,) + (1,) * (len(dims) - 1 - position))
    return factor_of


def normal_values(rng, dims, scale, reach, shards=(), kind=jnp.bfloat16):
    loudness = steps_of(rng, dims, shards, -0.22, 0.18) if shards else 1.0
    array = jax.random.normal(rng, dims, jnp.float32) * scale * loudness
    return jnp.minimum(jnp.maximum(array, -reach), reach).astype(kind)


def setup_inputs(seed: int = 0) -> dict:
    arg_keys = jax.random.split(jax.random.key(seed), 17)
    layer_input = normal_values(arg_keys[0], (MICRO, SLOTS, SLOT, D), 1.0, 6.0, ((1, 4), (2, 8)))
    cotangent = normal_values(arg_keys[1], (MICRO, SLOTS, SLOT, D), 1.0, 6.0, ((1, 4), (2, 8)))
    doc_len = draw_doc_len(jax.random.fold_in(arg_keys[16], 71), 0)
    doc_offset = draw_doc_offset(jax.random.fold_in(arg_keys[16], 71), 0)
    w_query = normal_values(arg_keys[4], (D, D), (D // 2) ** -0.5, 0.375, ((0, 32),))
    w_key = normal_values(arg_keys[5], (D, D), (D // 2) ** -0.5, 0.375, ((0, 32),))
    w_value = normal_values(arg_keys[6], (D, D), D ** -0.5, 0.25, ((0, 32),))
    w_out = normal_values(arg_keys[7], (D, D), (D // 16) ** -0.5, 1.0, ((0, 32),))
    w_gate_attn = normal_values(arg_keys[8], (D, D), D ** -0.5, 0.25, ((0, 32),))
    w_gate_ffn = normal_values(arg_keys[9], (D, D), D ** -0.5, 0.25, ((0, 32),))
    w_in = normal_values(arg_keys[10], (D, FF), D ** -0.5, 0.25, ((0, 32),))
    w_back = normal_values(arg_keys[11], (FF, D), FF ** -0.5, 0.125, ((0, 32),))
    norm_attn = jnp.clip(1.0 + 0.1 * jax.random.normal(arg_keys[12], (D,), jnp.float32), 0.5, 1.5).astype(jnp.bfloat16)
    norm_ffn = jnp.clip(1.0 + 0.1 * jax.random.normal(arg_keys[13], (D,), jnp.float32), 0.5, 1.5).astype(jnp.bfloat16)
    bias_attn = normal_values(arg_keys[14], (D,), 0.5, 3.0, ((0, 32),))
    bias_ffn = normal_values(arg_keys[15], (D,), 0.5, 3.0, ((0, 32),))
    return dict(layer_input=layer_input, cotangent=cotangent, doc_len=doc_len, doc_offset=doc_offset, w_query=w_query, w_key=w_key, w_value=w_value, w_out=w_out, w_gate_attn=w_gate_attn, w_gate_ffn=w_gate_ffn, w_in=w_in, w_back=w_back, norm_attn=norm_attn, norm_ffn=norm_ffn, bias_attn=bias_attn, bias_ffn=bias_ffn)


EPS = 1e-05
exact_mode = lax.Precision.HIGHEST

@jax.custom_vjp
def low(v):
    return lax.optimization_barrier(v.astype(jnp.bfloat16)).astype(jnp.float32)

@jax.custom_vjp
def low_back(v):
    return v

def low_keep(v):
    return (low(v), None)

def low_pass(kept, grad):
    return (grad,)

def back_keep(v):
    return (v, None)

def back_low(kept, grad):
    return (low(grad),)
low.defvjp(low_keep, low_pass)
low_back.defvjp(back_keep, back_low)

def rms_norm(values, gain):
    return values * lax.rsqrt(lax.optimization_barrier(jnp.mean(values * values, -1, keepdims=True)) + EPS) * gain

def matmul(left, right):
    return jnp.dot(left, right, precision=exact_mode, preferred_element_type=jnp.float32)

def token_valid(lengths, offsets):
    positions = jnp.arange(SLOT, dtype=jnp.int32)
    region = (positions // DOC_MAX).astype(jnp.int32)
    inside = positions - region * DOC_MAX
    begins = offsets[region]
    spans = lengths[region]
    return (inside >= begins) & (inside < begins + spans)

def attend_region(inputs):
    query_r, keys_r, values_r, valid_r = inputs
    block = min(512, DOC_MAX)
    blocks = DOC_MAX // block
    positions = jnp.arange(DOC_MAX, dtype=jnp.int32)

    @jax.checkpoint
    def one_block(pieces):
        query_block, query_pos, query_live = pieces
        scores = jnp.einsum('qhd,khd->hqk', query_block, keys_r, precision=exact_mode) * HEAD_DIM ** (-0.5)
        allowed = (positions[None, :] <= query_pos[:, None]) & valid_r[None, :]
        scores = jnp.where(allowed[None], scores, -1e+30)
        weights = jax.nn.softmax(scores, axis=-1)
        result = jnp.einsum('hqk,khd->qhd', weights, values_r, precision=exact_mode)
        return result * query_live.astype(jnp.float32)[:, None, None]
    results = lax.map(one_block, (query_r.reshape(blocks, block, HEADS, HEAD_DIM), positions.reshape(blocks, block), valid_r.reshape(blocks, block)))
    return results.reshape(DOC_MAX, HEADS, HEAD_DIM)

def layer(slot_in, weights_in, valid):
    w_query, w_key, w_value, w_out, w_gate_attn, w_gate_ffn, w_in, w_back, norm_attn, norm_ffn, bias_attn, bias_ffn = weights_in
    normed_attn = low(rms_norm(slot_in, norm_attn))
    query = low_back(low(matmul(normed_attn, w_query)))
    keys = low_back(low(matmul(normed_attn, w_key)))
    values = low_back(low(matmul(normed_attn, w_value)))
    gate_attn = jax.nn.sigmoid(low_back(matmul(normed_attn, w_gate_attn) + bias_attn))
    split_shape = (REGIONS, DOC_MAX, HEADS, HEAD_DIM)
    attended = lax.map(attend_region, (query.reshape(split_shape), keys.reshape(split_shape), values.reshape(split_shape), valid.reshape(REGIONS, DOC_MAX)))
    attended = low_back(low(attended.reshape(SLOT, D)))
    branch_attn = low_back(matmul(attended, w_out))
    hidden = gate_attn * branch_attn + (1.0 - gate_attn) * slot_in
    normed_ffn = low(rms_norm(hidden, norm_ffn))
    pre = low_back(matmul(normed_ffn, w_in))
    act = low(jax.nn.gelu(pre, approximate=True))
    branch_ffn = low_back(matmul(act, w_back))
    gate_ffn = jax.nn.sigmoid(low_back(matmul(normed_ffn, w_gate_ffn) + bias_ffn))
    return gate_ffn * branch_ffn + (1.0 - gate_ffn) * hidden

def reference(layer_input, cotangent, doc_len, doc_offset, w_query, w_key, w_value, w_out, w_gate_attn, w_gate_ffn, w_in, w_back, norm_attn, norm_ffn, bias_attn, bias_ffn):
    params = tuple((item.astype(jnp.float32) for item in (w_query, w_key, w_value, w_out, w_gate_attn, w_gate_ffn, w_in, w_back, norm_attn, norm_ffn, bias_attn, bias_ffn)))
    inputs = layer_input.astype(jnp.float32).reshape(MICRO * SLOTS, SLOT, D)
    upstream = cotangent.astype(jnp.float32).reshape(MICRO * SLOTS, SLOT, D)
    lengths = doc_len.reshape(MICRO * SLOTS, REGIONS)
    offsets = doc_offset.reshape(MICRO * SLOTS, REGIONS)
    zeros = jax.tree.map(jnp.zeros_like, params)

    def per_slot(totals, item):
        slot_x, slot_cot, slot_len, slot_off = item
        valid = token_valid(slot_len, slot_off)
        result, pull = jax.vjp(lambda slot_in, weights_in: layer(slot_in, weights_in, valid), slot_x, params)
        grad_x, grad_params = pull(slot_cot)
        return (jax.tree.map(jnp.add, totals, grad_params), (result.astype(jnp.bfloat16), grad_x))
    totals, (results, grads_x) = lax.scan(per_slot, zeros, (inputs, upstream, lengths, offsets))
    return (results.reshape(MICRO, SLOTS, SLOT, D), grads_x.reshape(MICRO, SLOTS, SLOT, D), totals[0], totals[1], totals[2], totals[3], totals[4], totals[5], totals[6], totals[7], totals[8], totals[9], totals[10], totals[11])
```

```python
from functools import partial

import jax
import jax.numpy as jnp
from jax import lax
from jax.experimental import pallas as pl
from jax.experimental.pallas import tpu as pltpu
from jax.sharding import PartitionSpec as P

HEADS = 8
HEAD_DIM = 64
DOC_MAX = 4096

EPS = 1e-05
MESH = pl.DeviceIdType.MESH
BF = jnp.bfloat16
F32 = jnp.float32
VMEM_LIMIT = 66_000_000
LANES = 128
SIDE = 64
GELU_C = 0.7978845608028654
GELU_A = 0.044715
NEG = -1e30
ANY = pl.BlockSpec(memory_space=pl.ANY)
INVM = pl.BlockSpec(memory_space=pltpu.VMEM)
INSM = pl.BlockSpec(memory_space=pltpu.SMEM)


def nn(a, b):
    return lax.dot_general(a, b, (((1,), (0,)), ((), ())), preferred_element_type=F32)


def nt(a, b):
    return lax.dot_general(a, b, (((1,), (1,)), ((), ())), preferred_element_type=F32)


def tn(a, b):
    return lax.dot_general(a, b, (((0,), (0,)), ((), ())), preferred_element_type=F32)


def remote(src, dst, send, recv, dp, seq):
    return pltpu.make_async_remote_copy(
        src_ref=src, dst_ref=dst, send_sem=send, recv_sem=recv,
        device_id=(dp, seq), device_id_type=MESH,
    )


def greet(peers):
    barrier = pltpu.get_barrier_semaphore()
    for dp, seq in peers:
        pl.semaphore_signal(barrier, inc=1, device_id=(dp, seq), device_id_type=MESH)
    pl.semaphore_wait(barrier, len(peers))


def place():
    d = lax.axis_index("dp")
    j = lax.axis_index("seq")
    z = j // 2
    c = j % 2
    dx = d + 1 - 2 * (d % 2)
    dy = (d + 2) % 4
    dxy = 3 - d
    return d, j, z, c, dx, dy, dxy


CK = 4


def gather_kernel(x_ref, s_ref, xg_ref, wg_ref, xv, sv, lsem, wsend, wrecv, xsend, xrecv):
    d, j, z, c, dx, dy, dxy = place()
    g = z // 2
    pj = j + 1 - 2 * c
    za, zb, zc = z + 1 - 2 * (z % 2), (z + 2) % 4, 3 - z
    near = jnp.logical_or(z == 1, z == 2)
    far = jnp.logical_or(z == 0, z == 3)
    ja, jb, jc = 2 * za + c, 2 * zb + c, 2 * zc + c
    lx = pltpu.make_async_copy(x_ref.at[g], xv, lsem.at[0])
    ls = pltpu.make_async_copy(s_ref, sv, lsem.at[1])
    lx.start()
    ls.start()
    greet([(d, ja), (d, jb), (d, jc), (dx, j), (dy, j), (d, pj)])
    rows = xv.shape[0] // CK
    count = [0]
    waits = []

    def wcopy(slot, dp, seq, own=False):
        i = count[0]
        count[0] += 1
        copy = remote(
            s_ref if own else wg_ref.at[slot], wg_ref.at[slot], wsend.at[i], wrecv.at[slot], dp, seq
        )
        copy.start()
        waits.append(copy)

    def warrive(slot):
        remote(s_ref, wg_ref.at[slot], wsend.at[0], wrecv.at[slot], d, pj).wait_recv()

    def xcopy(k, part, block, dp, seq, src=None):
        piece = pl.ds(part * rows, rows)
        source = xg_ref.at[block, piece] if src is None else x_ref.at[src, piece]
        return remote(
            source, xg_ref.at[block, piece], xsend.at[k, part], xrecv.at[block, part], dp, seq
        )

    def xarrive(part, block):
        xcopy(0, part, block, d, pj).wait_recv()

    me = d * 8 + j
    for dp, seq in [(d, ja), (d, jb), (d, jc), (dx, j), (dy, j), (d, pj)]:
        wcopy(me, dp, seq, True)
    xwaits = []
    jn = 2 * (2 - g) + c
    for part in range(CK):
        for k, (src, seq) in enumerate([(1 - g, jn), (g, ja), (g, pj)]):
            copy = xcopy(k, part, j, d, seq, src)
            copy.start()
            xwaits.append(copy)
    lx.wait()
    ls.wait()
    ox = pltpu.make_async_copy(xv, xg_ref.at[j], lsem.at[0])
    ow = pltpu.make_async_copy(sv, wg_ref.at[me], lsem.at[1])
    ox.start()
    ow.start()

    def zarr(jz):
        slot = d * 8 + jz
        warrive(slot)
        wcopy(slot, dx, j)
        wcopy(slot, dy, j)
        wcopy(slot, d, pj)

    def xyarr(zz):
        jz = 2 * zz + c
        sx, sy = dx * 8 + jz, dy * 8 + jz
        even = zz % 2 == 0
        warrive(sx)
        wcopy(sx, d, pj)
        warrive(sy)
        wcopy(sy, d, pj)
        i = count[0]
        count[0] += 1

        def on(slot, dp):
            return remote(wg_ref.at[slot], wg_ref.at[slot], wsend.at[i], wrecv.at[slot], dp, j)

        @pl.when(even)
        def _():
            on(sx, dy).start()

        @pl.when(jnp.logical_not(even))
        def _():
            on(sy, dx).start()

        waits.append(on(sx, dy))

    zarr(ja)
    xyarr(z)
    zarr(jb)
    xyarr(za)
    zarr(jc)
    xyarr(zb)
    xyarr(zc)
    b1 = 2 * (2 - g) + c
    b2 = 2 * (3 * (1 - g)) + c
    for k, block in ((3, b1), (5, b2)):
        for part in range(CK):
            xarrive(part, block)
            copy = xcopy(k, part, block, d, pj)
            copy.start()
            xwaits.append(copy)

            @pl.when(near)
            def _():
                xcopy(k + 1, part, block, d, ja).start()

    for part in range(CK):
        xarrive(part, ja)
        copy = xcopy(7, part, ja, d, pj)
        copy.start()
        xwaits.append(copy)
    for zz in (z, za, zb, zc):
        slot = dxy * 8 + 2 * zz + c
        warrive(slot)
        wcopy(slot, d, pj)
    for dp in (d, dx, dy, dxy):
        for zz in (z, za, zb, zc):
            warrive(dp * 8 + 2 * zz + 1 - c)
    for block in (j, ja, b1, b2):
        for part in range(CK):
            xarrive(part, block + 1 - 2 * c)
    for copy in waits:
        copy.wait_send()
    for copy in xwaits:
        copy.wait_send()

    @pl.when(near)
    def _():
        for k, block in ((4, b1), (6, b2)):
            for part in range(CK):
                xcopy(k, part, block, d, ja).wait_send()

    ox.wait()
    ow.wait()


def gather(x, shard):
    _, rows, width = x.shape
    return pl.pallas_call(
        gather_kernel,
        out_shape=(
            jax.ShapeDtypeStruct((8, rows, width), BF),
            jax.ShapeDtypeStruct((32,) + shard.shape, BF),
        ),
        in_specs=[ANY, ANY],
        out_specs=(ANY, ANY),
        scratch_shapes=[
            pltpu.VMEM((rows, width), BF),
            pltpu.VMEM(shard.shape, BF),
            pltpu.SemaphoreType.DMA((2,)),
            pltpu.SemaphoreType.DMA((32,)),
            pltpu.SemaphoreType.DMA((32,)),
            pltpu.SemaphoreType.DMA((8, CK)),
            pltpu.SemaphoreType.DMA((8, CK)),
        ],
        compiler_params=pltpu.CompilerParams(collective_id=0, has_side_effects=True),
    )(x, shard)


def swap_kernel(a_ref, b_ref, av, lsem, send, recv):
    d = lax.axis_index("dp")
    j = lax.axis_index("seq")
    load = pltpu.make_async_copy(a_ref.at[j], av, lsem)
    load.start()
    peers = [(d, (j + k) % 8) for k in range(1, 8)]
    greet(peers)
    copies = []
    for k, (dp, seq) in enumerate(peers):
        copy = remote(a_ref.at[seq], b_ref.at[j], send.at[k], recv.at[k], dp, seq)
        copy.start()
        copies.append(copy)
    load.wait()
    keep = pltpu.make_async_copy(av, b_ref.at[j], lsem)
    keep.start()
    for copy in copies:
        copy.wait()
    keep.wait()


def swap(a, cid):
    return pl.pallas_call(
        swap_kernel,
        out_shape=jax.ShapeDtypeStruct(a.shape, a.dtype),
        in_specs=[ANY],
        out_specs=ANY,
        scratch_shapes=[
            pltpu.VMEM(a.shape[1:], a.dtype),
            pltpu.SemaphoreType.DMA,
            pltpu.SemaphoreType.DMA((7,)),
            pltpu.SemaphoreType.DMA((7,)),
        ],
        compiler_params=pltpu.CompilerParams(collective_id=cid, has_side_effects=True),
    )(a)


def lane_of(rows):
    return lax.broadcasted_iota(jnp.int32, (rows, LANES), 1)


def three(v):
    a = v.astype(BF).astype(F32)
    b = (v - a).astype(BF).astype(F32)
    return a, b, v - a - b


def beside(h, lane, values, parts):
    first = SIDE * (1 - h)
    own = (lane < SIDE) if h == 0 else (lane >= SIDE)
    out = jnp.where(own, values, 0.0)
    for k, part in enumerate(parts):
        if part is not None:
            out = jnp.where(lane == first + k, part, out)
    return out.astype(BF)


def attend_kernel(doc, x_ref, w_ref, gain_ref, o_ref, o32_ref, qa, ka, va):
    blocks, rows, width = x_ref.shape
    off = doc[0]
    end = off + doc[1]
    lane = lane_of(rows)
    up = lax.broadcasted_iota(jnp.int32, (rows, 1), 0)
    gain = gain_ref[...].astype(F32)

    def project(b, _):
        x = x_ref[b].astype(F32)
        n = (x * lax.rsqrt(jnp.mean(x * x, -1, keepdims=True) + EPS) * gain).astype(BF)
        p = nn(n, w_ref[...])
        pos = b * rows + up
        bad = jnp.where(jnp.logical_and(pos >= off, pos < end), 0.0, NEG)
        q = p[:, :LANES].astype(BF).astype(F32) * HEAD_DIM ** (-0.5)
        k = p[:, LANES : 2 * LANES]
        v = p[:, 2 * LANES :]
        for h in range(2):
            qa[h, b] = beside(h, lane, q, (1.0,))
            ka[h, b] = beside(h, lane, k, (bad, 1.0, 1.0, 1.0))
            va[h, b] = beside(h, lane, v, (None, 1.0, 1.0, 1.0))
        return 0

    lax.fori_loop(0, blocks, project, 0)
    first = off // rows
    last = (end - 1) // rows
    diag = lax.broadcasted_iota(jnp.int32, (rows, rows), 0) >= lax.broadcasted_iota(
        jnp.int32, (rows, rows), 1
    )

    def one(b, _):
        inside = jnp.logical_and(b >= first, b <= last)

        @pl.when(jnp.logical_not(inside))
        def _():
            o_ref[b] = jnp.zeros((rows, LANES), BF)
            o32_ref[b] = jnp.zeros((rows, LANES), F32)
            for h in range(2):
                qa[h, b] = beside(h, lane, qa[h, b].astype(F32), (1.0, NEG))

        @pl.when(inside)
        def _():
            pos = b * rows + up
            live = jnp.logical_and(pos >= off, pos < end)
            outs = []
            for h in range(2):
                q = qa[h, b]

                def step(kb, carry, masked=False):
                    m, acc = carry
                    s = nt(q, ka[h, kb])
                    if masked:
                        s = jnp.where(diag, s, NEG)
                    new = jnp.maximum(m, jnp.max(s, -1, keepdims=True))
                    p = jnp.exp(s - new).astype(BF)
                    acc = acc * jnp.exp(m - new) + nn(p, va[h, kb])
                    return new, acc

                start = (jnp.full((rows, 1), NEG, F32), jnp.zeros((rows, LANES), F32))
                m, acc = step(b, lax.fori_loop(first, b, step, start), True)
                one_at = SIDE * (1 - h) + 1
                total = acc[:, one_at : one_at + 1]
                lse = jnp.where(live, m + jnp.log(total), -NEG)
                a, bb, cc = three(lse)
                qa[h, b] = beside(h, lane, q.astype(F32), (1.0, -a, -bb, -cc))
                outs.append(jnp.where(live, acc / total, 0.0))
            out = jnp.where(lane < SIDE, outs[0], outs[1])
            o32_ref[b] = out
            o_ref[b] = out.astype(BF)

        return 0

    lax.fori_loop(0, blocks, one, 0)


def attend(doc, xg, w, gain):
    blocks, rows, width = xg.shape
    side = jax.ShapeDtypeStruct((2, blocks, rows, LANES), BF)
    return pl.pallas_call(
        attend_kernel,
        out_shape=(
            jax.ShapeDtypeStruct((blocks, rows, LANES), BF),
            jax.ShapeDtypeStruct((blocks, rows, LANES), F32),
            side, side, side,
        ),
        in_specs=[INSM, INVM, INVM, INVM],
        out_specs=(INVM,) * 5,
        compiler_params=pltpu.CompilerParams(vmem_limit_bytes=VMEM_LIMIT),
    )(doc, xg, w, gain)


def attend_back_kernel(
    doc, x_ref, w_ref, gain_ref, o32_ref, do_ref, qa, ka, va, dn_ref, dw_ref, dgain_ref, da, dq, dk, dv
):
    blocks, rows, width = x_ref.shape
    off = doc[0]
    end = off + doc[1]
    lane = lane_of(rows)
    first = off // rows
    last = (end - 1) // rows
    low = lax.broadcasted_iota(jnp.int32, (rows, rows), 0) <= lax.broadcasted_iota(
        jnp.int32, (rows, rows), 1
    )

    def prepare(b, _):
        do = do_ref[b].astype(F32)
        both = do * o32_ref[b]
        for h in range(2):
            own = (lane < SIDE) if h == 0 else (lane >= SIDE)
            delta = jnp.sum(jnp.where(own, both, 0.0), -1, keepdims=True)
            a, bb, cc = three(delta)
            da[h, b] = beside(h, lane, do, (None, -a, -bb, -cc))
            dq[h, b] = jnp.zeros((rows, LANES), F32)
            dk[h, b] = jnp.zeros((rows, LANES), F32)
            dv[h, b] = jnp.zeros((rows, LANES), F32)
        return 0

    lax.fori_loop(0, blocks, prepare, 0)

    def keys(kb, _):
        for h in range(2):
            k = ka[h, kb]
            v = va[h, kb]

            def queries(b, carry, masked=False):
                q = qa[h, b]
                do = da[h, b]
                p = jnp.exp(nt(k, q))
                if masked:
                    p = jnp.where(low, p, 0.0)
                ds = (p * nt(v, do)).astype(BF)
                dv[h, kb] += nn(p.astype(BF), do)
                dk[h, kb] += nn(ds, q)
                dq[h, b] += tn(ds, k)
                return carry

            queries(kb, 0, True)
            lax.fori_loop(kb + 1, last + 1, queries, 0)
        return 0

    lax.fori_loop(first, last + 1, keys, 0)
    gain = gain_ref[...].astype(F32)
    dw_ref[...] = jnp.zeros_like(dw_ref)
    dgain_ref[...] = jnp.zeros_like(dgain_ref)

    def finish(b, _):
        x = x_ref[b].astype(F32)
        n1 = x * lax.rsqrt(jnp.mean(x * x, -1, keepdims=True) + EPS)
        n = (n1 * gain).astype(BF)
        left = lane < SIDE
        q = jnp.where(left, dq[0, b], dq[1, b]) * HEAD_DIM ** (-0.5)
        k = jnp.where(left, dk[0, b], dk[1, b])
        v = jnp.where(left, dv[0, b], dv[1, b])
        p = jnp.concatenate([q.astype(BF), k.astype(BF), v.astype(BF)], axis=1)
        dw_ref[...] += tn(n, p)
        dn = nt(p, w_ref[...])
        dn_ref[b] = dn.astype(BF)
        dgain_ref[...] += jnp.sum(dn * n1, 0, keepdims=True)
        return 0

    lax.fori_loop(0, blocks, finish, 0)


def attend_back(doc, xg, w, gain, o32, do, qa, ka, va):
    blocks, rows, width = xg.shape
    return pl.pallas_call(
        attend_back_kernel,
        out_shape=(
            jax.ShapeDtypeStruct((blocks, rows, width), BF),
            jax.ShapeDtypeStruct((width, 3 * LANES), F32),
            jax.ShapeDtypeStruct((1, width), F32),
        ),
        in_specs=[INSM] + [INVM] * 8,
        out_specs=(INVM,) * 3,
        scratch_shapes=[
            pltpu.VMEM((2, blocks, rows, LANES), BF),
            pltpu.VMEM((2, blocks, rows, LANES), F32),
            pltpu.VMEM((2, blocks, rows, LANES), F32),
            pltpu.VMEM((2, blocks, rows, LANES), F32),
        ],
        compiler_params=pltpu.CompilerParams(vmem_limit_bytes=VMEM_LIMIT),
    )(doc, xg, w, gain, o32, do, qa, ka, va)


def token_kernel(
    x_ref, c_ref, a_ref, wg, vec, out_ref, da_ref, dh_ref, dn_ref, g_ref, v_ref,
    gp, act, g_out, g_ga, g_gf, g_in, g_back,
):
    step = pl.program_id(0)
    rows, width = x_ref.shape[1:]
    ff = gp.shape[0]
    per = width // 32

    def weight(lo):
        return wg[:, lo : lo + per, :].reshape(width, width)

    def back(k):
        n = wg.shape[0] // ff
        return wg[k * n : (k + 1) * n, 10 * per : 10 * per + ff * per, :].reshape(width, width)

    @pl.when(step == 0)
    def _():
        for ref in (g_out, g_ga, g_gf, g_in, g_back, v_ref):
            ref[...] = jnp.zeros_like(ref)

    x = x_ref[0].astype(F32)
    gain_a, gain_f = vec[0:1].astype(F32), vec[1:2].astype(F32)
    shift_a, shift_f = vec[2:3].astype(F32), vec[3:4].astype(F32)
    n1 = x * lax.rsqrt(jnp.mean(x * x, -1, keepdims=True) + EPS)
    na = (n1 * gain_a).astype(BF)
    ga = jax.nn.sigmoid(nn(na, weight(4 * per)) + shift_a)
    att = jnp.concatenate([a_ref[i] for i in range(4)], axis=1)
    br = nn(att, weight(3 * per))
    hid = ga * br + (1.0 - ga) * x
    r2 = lax.rsqrt(jnp.mean(hid * hid, -1, keepdims=True) + EPS)
    n2 = hid * r2
    nf = (n2 * gain_f).astype(BF)
    bf = jnp.zeros((rows, width), F32)
    for k in range(ff):
        pre = nn(nf, weight((6 + k) * per))
        sq = pre * pre
        t = jnp.tanh(GELU_C * pre * (1.0 + GELU_A * sq))
        half = 0.5 * (1.0 + t)
        act[k] = (pre * half).astype(BF)
        gp[k] = half + 0.5 * pre * (1.0 - t * t) * (GELU_C * (1.0 + 3.0 * GELU_A * sq))
        bf += nn(act[k], back(k))
    gf = jax.nn.sigmoid(nn(nf, weight(5 * per)) + shift_f)
    out_ref[0] = (gf * bf + (1.0 - gf) * hid).astype(BF)
    c = c_ref[0].astype(F32)
    dlf = (c * (bf - hid) * gf * (1.0 - gf)).astype(BF)
    dbf = (c * gf).astype(BF)
    dnf = nt(dlf, weight(5 * per))
    g_gf[...] += tn(nf, dlf)
    for k in range(ff):
        dpre = (nt(dbf, back(k)) * gp[k]).astype(BF)
        g_back[k] += tn(act[k], dbf)
        g_in[k] += tn(nf, dpre)
        dnf += nt(dpre, weight((6 + k) * per))
    g2 = dnf * gain_f
    dh = c * (1.0 - gf) + r2 * (g2 - n2 * jnp.mean(g2 * n2, -1, keepdims=True))
    dba = (dh * ga).astype(BF)
    dla = (dh * (br - x) * ga * (1.0 - ga)).astype(BF)
    g_out[...] += tn(att, dba)
    g_ga[...] += tn(na, dla)
    datt = nt(dba, weight(3 * per)).astype(BF)
    for i in range(4):
        da_ref[i] = datt[:, i * LANES : (i + 1) * LANES]
    dna = nt(dla, weight(4 * per))
    dh_ref[0] = dh * (1.0 - ga)
    dn_ref[0] = dna
    v_ref[0:1] += jnp.sum(dna * n1, 0, keepdims=True)
    v_ref[1:2] += jnp.sum(dnf * n2, 0, keepdims=True)
    v_ref[2:3] += jnp.sum(dla.astype(F32), 0, keepdims=True)
    v_ref[3:4] += jnp.sum(dlf.astype(F32), 0, keepdims=True)

    @pl.when(step == pl.num_programs(0) - 1)
    def _():
        def put(lo, value):
            g_ref[:, lo : lo + per, :] = value.astype(BF).reshape(32, per, width)

        put(0, g_out[...])
        put(per, g_ga[...])
        put(2 * per, g_gf[...])
        for k in range(ff):
            put((3 + k) * per, g_in[k])
            n = 32 // ff
            g_ref[k * n : (k + 1) * n, (3 + ff) * per :, :] = (
                g_back[k].astype(BF).reshape(n, ff * per, width)
            )


def tokens(x, cot, att, wg, vec):
    micro, rows, width = x.shape
    ff = 4
    per = width // 32
    tok = pl.BlockSpec((1, rows, width), lambda i: (i, 0, 0))
    head = pl.BlockSpec((4, rows, LANES), lambda i: (i, 0, 0))

    def whole(shape):
        return pl.BlockSpec(shape, lambda i: (0,) * len(shape), pipeline_mode=pl.Buffered(1))

    grads = (32, (3 + 2 * ff) * per, width)
    return pl.pallas_call(
        token_kernel,
        grid=(micro,),
        out_shape=(
            jax.ShapeDtypeStruct((micro, rows, width), BF),
            jax.ShapeDtypeStruct((4 * micro, rows, LANES), BF),
            jax.ShapeDtypeStruct((micro, rows, width), F32),
            jax.ShapeDtypeStruct((micro, rows, width), F32),
            jax.ShapeDtypeStruct(grads, BF),
            jax.ShapeDtypeStruct((8, width), F32),
        ),
        in_specs=[tok, tok, head, whole(wg.shape), whole(vec.shape)],
        out_specs=(tok, head, tok, tok, whole(grads), whole((8, width))),
        scratch_shapes=[
            pltpu.VMEM((ff, rows, width), F32),
            pltpu.VMEM((ff, rows, width), BF),
            pltpu.VMEM((width, width), F32),
            pltpu.VMEM((width, width), F32),
            pltpu.VMEM((width, width), F32),
            pltpu.VMEM((ff, width, width), F32),
            pltpu.VMEM((ff, width, width), F32),
        ],
        compiler_params=pltpu.CompilerParams(vmem_limit_bytes=VMEM_LIMIT),
    )(x, cot, att, wg, vec)


def add_into(dst, src):
    rows = dst.shape[0]
    n = rows // 16
    per = 16 * max(k for k in range(1, 9) if n % k == 0)

    def body(i, _):
        piece = pl.ds(i * per, per)
        dst[piece, :] = (dst[piece, :].astype(F32) + src[piece, :].astype(F32)).astype(BF)
        return 0

    lax.fori_loop(0, rows // per, body, 0)


def reduce_kernel(
    p_ref, g_ref, h_ref, dn_ref, gf_ref, gq_ref, gv_ref,
    acc, b1, b2, b3, b4, qs, q1, q2, hb, own,
    l1, l2, lo, s1, r1, s2, r2, s3, r3, s4, r4, ps, pr, ts, tr, us, ur, hs, hr,
):
    d, j, z, c, dx, dy, dxy = place()
    me = d * 8 + j
    g = z // 2
    pj = j + 1 - 2 * c
    za, zb, zc = z + 1 - 2 * (z % 2), (z + 2) % 4, 3 - z
    ja, jb, jc = 2 * za + c, 2 * zb + c, 2 * zc + c
    near = jnp.logical_or(z == 1, z == 2)
    far = jnp.logical_or(z == 0, z == 3)
    w3, w2, wn, wf = 3 * (1 - g), 2 - g, 1 + g, 3 * g
    order = (w3, wf, w2, wn)
    first = [(zz, dp) for zz in range(4) for dp in ((dx, dxy) if zz % 2 == 0 else (dy, dxy))]
    rest = [(zz, dp) for zz in range(4) for dp in ((d, dy) if zz % 2 == 0 else (d, dx))]

    ploads = []
    for k, zz in enumerate(order):
        copy = pltpu.make_async_copy(p_ref.at[2 * zz + c], qs.at[zz], l1.at[k])
        copy.start()
        ploads.append(copy)
    gloads = []
    for k, (zz, dp) in enumerate(first + rest):
        copy = pltpu.make_async_copy(g_ref.at[dp * 8 + 2 * zz + c], acc.at[dp * 4 + zz], l2.at[k])
        copy.start()
        gloads.append(copy)
    hload = pltpu.make_async_copy(h_ref.at[me], hb.at[me], lo.at[0])
    hload.start()

    barrier = pltpu.get_barrier_semaphore()

    def hello(k, _):
        slot = (me + k) % 32
        pl.semaphore_signal(
            barrier, inc=1, device_id=(slot // 8, slot % 8), device_id_type=MESH
        )
        return 0

    lax.fori_loop(1, 32, hello, 0)
    pl.semaphore_wait(barrier, 31)

    sent = []

    def go(copy):
        copy.start()
        sent.append(copy)

    def pcopy(zz):
        return remote(p_ref.at[2 * zz + 1 - c], q1.at[zz], ps.at[zz], pr.at[zz], d, pj)

    def gcopy(zz, dp):
        i = dp * 4 + zz
        return remote(g_ref.at[dp * 8 + 2 * zz + 1 - c], b1.at[i], s1.at[i], r1.at[i], d, pj)

    for zz in order:
        go(pcopy(zz))
    for zz, dp in first + rest:
        go(gcopy(zz, dp))

    def hcopy(k):
        slot = (me + k) % 32
        return remote(h_ref.at[slot], hb.at[me], hs.at[k], hr.at[me], slot // 8, slot % 8)

    def hstart(k, _):
        hcopy(k).start()
        return 0

    lax.fori_loop(1, 32, hstart, 0)

    def tcopy(zz):
        return remote(qs.at[zz], q2.at[zz], ts.at[zz], tr.at[zz], d, ja)

    for k, zz in enumerate(order):
        ploads[k].wait()
        pcopy(zz).wait_recv()
        add_into(qs.at[zz], q1.at[zz])
        if k == 1:

            @pl.when(near)
            def _():
                tcopy(zz).start()
        else:

            @pl.when(far)
            def _():
                tcopy(zz).start()

    def stage2(zz, dp):
        i = dp * 4 + zz
        to = dx if zz % 2 == 0 else dy
        return remote(acc.at[i], b2.at[i], s2.at[i], r2.at[i], to, j)

    def stage3(zz):
        to = dy if zz % 2 == 0 else dx
        return remote(acc.at[to * 4 + zz], b3.at[zz], s3.at[zz], r3.at[zz], to, j)

    def stage4(k, zz, jz):
        return remote(acc.at[d * 4 + zz], b4.at[z], s4.at[k], r4.at[z], d, jz)

    def ucopy(k, zz):
        return remote(qs.at[zz], dn_ref.at[g], us.at[k], ur.at[0], d, 2 * zz + c)

    def pass_on(k, zz):
        @pl.when(near)
        def _():
            tcopy(zz).wait_recv()
            add_into(qs.at[zz], q2.at[zz])
            ucopy(k, zz).start()

    for k, (zz, dp) in enumerate(first):
        gloads[k].wait()
        gcopy(zz, dp).wait_recv()
        add_into(acc.at[dp * 4 + zz], b1.at[dp * 4 + zz])
        go(stage2(zz, dp))
    for k, (zz, dp) in enumerate(rest):
        gloads[len(first) + k].wait()
        gcopy(zz, dp).wait_recv()
        add_into(acc.at[dp * 4 + zz], b1.at[dp * 4 + zz])
    pass_on(0, w3)
    for pick in (1, 0):
        for zz in range(4):
            dp = (d, dy if zz % 2 == 0 else dx)[pick]
            stage2(zz, dp).wait_recv()
            add_into(acc.at[dp * 4 + zz], b2.at[dp * 4 + zz])
            if pick:
                go(stage3(zz))
    for zz in range(4):
        stage3(zz).wait_recv()
        add_into(acc.at[d * 4 + zz], b3.at[zz])
    for k, (zz, jz) in enumerate(((za, ja), (zb, jb), (zc, jc))):
        go(stage4(k, zz, jz))
    pass_on(1, w2)
    tcopy(z).wait_recv()

    def mine(i, _):
        piece = pl.ds(i * 128, 128)
        own[piece, :] = (qs[z, piece, :].astype(F32) + q2[z, piece, :].astype(F32)).astype(BF)
        return 0

    lax.fori_loop(0, own.shape[0] // 128, mine, 0)
    keep = pltpu.make_async_copy(own, dn_ref.at[g], lo.at[1])
    keep.start()
    for zz in (za, zb, zc):
        remote(acc.at[0], b4.at[zz], s4.at[0], r4.at[zz], d, ja).wait_recv()
    gf_ref[...] = (
        acc[d * 4 + z].astype(F32)
        + b4[za].astype(F32) + b4[zb].astype(F32) + b4[zc].astype(F32)
    )
    hload.wait()

    def harrive(k, _):
        slot = (me + k) % 32
        remote(h_ref.at[0], hb.at[slot], hs.at[0], hr.at[slot], d, pj).wait_recv()
        return 0

    lax.fori_loop(1, 32, harrive, 0)
    per = gq_ref.shape[1]
    total = jnp.zeros(gv_ref.shape, F32)
    for hi in range(4):
        part = jnp.zeros((per, 3 * LANES), F32)
        for k in range(8):
            slot = (k // 2) * 8 + (k % 2) * 4 + hi
            part += hb[slot, :per].astype(F32)
            total += hb[slot, per:].astype(F32)
        for m in range(3):
            gq_ref[m, :, hi * LANES : (hi + 1) * LANES] = part[:, m * LANES : (m + 1) * LANES]
    gv_ref[...] = total
    ucopy(0, w3).wait_recv()
    for copy in sent:
        copy.wait_send()

    def hsent(k, _):
        hcopy(k).wait_send()
        return 0

    lax.fori_loop(1, 32, hsent, 0)

    @pl.when(near)
    def _():
        tcopy(wf).wait_send()
        ucopy(0, w3).wait_send()
        ucopy(1, w2).wait_send()

    @pl.when(far)
    def _():
        for zz in (w3, w2, wn):
            tcopy(zz).wait_send()

    keep.wait()


def reduce(p, grads, h):
    blocks, rows, width = p.shape
    g = grads.shape[1:]
    per = h.shape[1] // 2
    dma = pltpu.SemaphoreType.DMA
    return pl.pallas_call(
        reduce_kernel,
        out_shape=(
            jax.ShapeDtypeStruct((2, rows, width), BF),
            jax.ShapeDtypeStruct(g, F32),
            jax.ShapeDtypeStruct((3, per, width), F32),
            jax.ShapeDtypeStruct((per, 3 * LANES), F32),
        ),
        in_specs=[ANY, ANY, ANY],
        out_specs=(ANY, INVM, INVM, INVM),
        scratch_shapes=[
            pltpu.VMEM((16,) + g, BF),
            pltpu.VMEM((16,) + g, BF),
            pltpu.VMEM((16,) + g, BF),
            pltpu.VMEM((4,) + g, BF),
            pltpu.VMEM((4,) + g, BF),
            pltpu.VMEM((4, rows, width), BF),
            pltpu.VMEM((4, rows, width), BF),
            pltpu.VMEM((4, rows, width), BF),
            pltpu.VMEM((32,) + h.shape[1:], BF),
            pltpu.VMEM((rows, width), BF),
            dma((4,)), dma((16,)), dma((2,)),
            dma((16,)), dma((16,)), dma((16,)), dma((16,)), dma((4,)), dma((4,)), dma((4,)), dma((4,)),
            dma((4,)), dma((4,)), dma((4,)), dma((4,)), dma((2,)), dma((1,)), dma((32,)), dma((32,)),
        ],
        compiler_params=pltpu.CompilerParams(
            collective_id=3, has_side_effects=True, vmem_limit_bytes=VMEM_LIMIT
        ),
    )(p, grads, h)


def by_heads(
    layer_input, cotangent, doc_len, doc_offset,
    w_query, w_key, w_value, w_out, w_gate_attn, w_gate_ffn, w_in, w_back,
    norm_attn, norm_ffn, bias_attn, bias_ffn,
):
    micro, _, rows, width = layer_input.shape
    per = w_query.shape[0]
    ff = w_in.shape[1] // width
    j = lax.axis_index("seq")
    g = j // 4
    hi = j % 4
    x = layer_input[:, 0]
    cot = cotangent[:, 0]
    vec = jnp.stack([norm_attn, norm_ffn, bias_attn, bias_ffn])
    shard = jnp.concatenate(
        [w_query, w_key, w_value, w_out, w_gate_attn, w_gate_ffn]
        + [w_in[:, k * width : (k + 1) * width] for k in range(ff)]
        + [w_back, jnp.pad(vec, ((0, 12), (0, width - per)))]
    )
    xg, wg = gather(x, shard)
    vecs = wg[:, -16:-12, :per].transpose(1, 0, 2).reshape(4, width)
    w = lax.dynamic_slice(wg, (0, 0, hi * LANES), (32, 3 * per, LANES))
    w = w.reshape(32, 3, per, LANES).transpose(0, 2, 1, 3).reshape(width, 3 * LANES)
    doc = jnp.stack([doc_offset[g, 0, 0], doc_len[g, 0, 0]])
    gain = vecs[0:1]
    o, o32, qa, ka, va = attend(doc, xg, w, gain)
    att = swap(o, 1)
    out, datt, dh, dna, grads, sums = tokens(x, cot, att, wg, vecs)
    do = swap(datt, 2)
    dn, dw, dgain = attend_back(doc, xg, w, gain, o32, do, qa, ka, va)
    sums = jnp.concatenate([sums[0:1] + dgain, sums[1:4]]).reshape(4, 32, per).transpose(1, 0, 2)
    sums = jnp.pad(sums, ((0, 0), (0, per - 4), (0, 3 * LANES - per)))
    h = jnp.concatenate([dw.reshape(32, per, 3 * LANES), sums], axis=1).astype(BF)
    dn, gf, gq, gv = reduce(dn, grads, h)
    x32 = x.astype(F32)
    r1 = lax.rsqrt(jnp.mean(x32 * x32, -1, keepdims=True) + EPS)
    n1 = x32 * r1
    g1 = (dna + dn.astype(F32)) * gain.astype(F32)
    grad = dh + r1 * (g1 - n1 * jnp.mean(g1 * n1, -1, keepdims=True))
    return (
        out[:, None],
        grad[:, None],
        gq[0], gq[1], gq[2],
        gf[:per], gf[per : 2 * per], gf[2 * per : 3 * per],
        gf[3 * per : (3 + ff) * per].reshape(ff, per, width).transpose(1, 0, 2).reshape(per, ff * width),
        gf[(3 + ff) * per :],
        gv[0, :per], gv[1, :per], gv[2, :per], gv[3, :per],
    )


def from_behind(x, axis, by):
    count = lax.axis_size(axis)
    pairs = [(i, i + by) for i in range(count) if 0 <= i + by < count]
    return lax.ppermute(x, axis, pairs)


def passed_along(value, axis, steps):
    count = lax.axis_size(axis)
    pairs = [(source, (source + steps) % count) for source in range(count)]
    return lax.ppermute(value, axis, pairs)


def rms_norm(values, gain):
    return values * lax.rsqrt(jnp.mean(values * values, -1, keepdims=True) + EPS) * gain


def dense(left, right):
    return jnp.dot(left, right, preferred_element_type=jnp.float32)


def dense_tn(left, right):
    return lax.dot_general(
        left, right, (((0,), (0,)), ((), ())), preferred_element_type=jnp.float32
    )


def dense_nt(left, right):
    return lax.dot_general(
        left, right, (((1,), (1,)), ((), ())), preferred_element_type=jnp.float32
    )


def layout_of(lengths, offsets, source, rows, filler):
    positions = source * rows + jnp.arange(rows, dtype=jnp.int32)
    region = positions // DOC_MAX
    inside = positions - region * DOC_MAX
    members = (region[:, None] == jnp.arange(lengths.shape[1], dtype=jnp.int32)[None, :]).astype(
        jnp.int32
    )
    begins = jnp.sum(members[None] * offsets[:, None, :], axis=2)
    spans = jnp.sum(members[None] * lengths[:, None, :], axis=2)
    inside_doc = (inside[None] >= begins) & (inside[None] < begins + spans)
    labels = jnp.where(inside_doc, region[None], filler)
    return (positions, labels, inside_doc)


def allowed_pairs(query_side, key_side):
    same_doc = query_side[1][:, :, None] == key_side[1][:, None, :]
    causal = key_side[0][None, None, :] <= query_side[0][None, :, None]
    return same_doc & causal


def absorb(carry, query, key_piece, value_piece, allowed):
    run_max, run_sum, totals = carry
    scores = jnp.einsum(
        "mqhd,mkhd->mhqk", query, key_piece, preferred_element_type=jnp.float32
    ) * HEAD_DIM ** (-0.5)
    scores = jnp.where(allowed[:, None], scores, -1e30)
    new_max = jnp.maximum(run_max, jnp.max(scores, axis=-1))
    factor = jnp.exp(run_max - new_max)
    weights = jnp.where(allowed[:, None], jnp.exp(scores - new_max[..., None]), 0.0)
    run_sum = run_sum * factor + jnp.sum(weights, axis=-1)
    totals = totals * factor[..., None] + jnp.einsum(
        "mhqk,mkhd->mhqd", weights, value_piece.astype(jnp.float32)
    )
    return (new_max, run_sum, totals)


def hop_grads(query, grad_att, lse, delta, key_piece, value_piece, allowed):
    scores = jnp.einsum(
        "mqhd,mkhd->mhqk", query, key_piece, preferred_element_type=jnp.float32
    ) * HEAD_DIM ** (-0.5)
    probs = jnp.where(allowed[:, None], jnp.exp(scores - lse[..., None]), 0.0)
    grad_value = jnp.einsum("mhqk,mqhd->mkhd", probs, grad_att.astype(jnp.float32))
    grad_probs = jnp.einsum(
        "mqhd,mkhd->mhqk", grad_att, value_piece, preferred_element_type=jnp.float32
    )
    grad_scores = probs * (grad_probs - delta[..., None]) * HEAD_DIM ** (-0.5)
    grad_query = jnp.einsum("mhqk,mkhd->mqhd", grad_scores, key_piece.astype(jnp.float32))
    grad_key = jnp.einsum("mhqk,mqhd->mkhd", grad_scores, query.astype(jnp.float32))
    return (grad_query, grad_key, grad_value)


def shards(
    layer_input,
    cotangent,
    doc_len,
    doc_offset,
    w_query,
    w_key,
    w_value,
    w_out,
    w_gate_attn,
    w_gate_ffn,
    w_in,
    w_back,
    norm_attn,
    norm_ffn,
    bias_attn,
    bias_ffn,
):
    gathered = (
        lax.all_gather(w_query, ("dp", "seq"), axis=0, tiled=True),
        lax.all_gather(w_key, ("dp", "seq"), axis=0, tiled=True),
        lax.all_gather(w_value, ("dp", "seq"), axis=0, tiled=True),
        lax.all_gather(w_out, ("dp", "seq"), axis=0, tiled=True),
        lax.all_gather(w_gate_attn, ("dp", "seq"), axis=0, tiled=True),
        lax.all_gather(w_gate_ffn, ("dp", "seq"), axis=0, tiled=True),
        lax.all_gather(w_in, ("dp", "seq"), axis=0, tiled=True),
        lax.all_gather(w_back, ("dp", "seq"), axis=0, tiled=True),
        lax.all_gather(norm_attn, ("dp", "seq"), axis=0, tiled=True),
        lax.all_gather(norm_ffn, ("dp", "seq"), axis=0, tiled=True),
        lax.all_gather(bias_attn, ("dp", "seq"), axis=0, tiled=True),
        lax.all_gather(bias_ffn, ("dp", "seq"), axis=0, tiled=True),
    )
    (
        full_query,
        full_key,
        full_value,
        full_out,
        full_gate_attn,
        full_gate_ffn,
        full_in,
        full_back,
        gain_attn,
        gain_ffn,
        shift_attn,
        shift_ffn,
    ) = gathered
    micro = layer_input.shape[0]
    rows = layer_input.shape[2]
    width = layer_input.shape[3]
    tokens = micro * rows
    nseq = lax.axis_size("seq")
    me_index = lax.axis_index("seq")
    hops = min(max(DOC_MAX // rows, 1), nseq) - 1
    lengths = doc_len[:, 0]
    offsets = doc_offset[:, 0]

    def key_side(source):
        positions, labels, _ = layout_of(lengths, offsets, source, rows, -2)
        return (positions, labels)

    own_layout = layout_of(lengths, offsets, me_index, rows, -1)
    query_side = (own_layout[0], own_layout[1])
    own_keys = key_side(me_index)
    inputs = layer_input[:, 0].reshape(tokens, width).astype(jnp.float32)
    normed_attn, pull_attn = jax.vjp(rms_norm, inputs, gain_attn.astype(jnp.float32))
    normed_low = normed_attn.astype(jnp.bfloat16)
    query = dense(normed_low, full_query).astype(jnp.bfloat16)
    keys = dense(normed_low, full_key).astype(jnp.bfloat16)
    values = dense(normed_low, full_value).astype(jnp.bfloat16)
    gate_attn = jax.nn.sigmoid(dense(normed_low, full_gate_attn) + shift_attn.astype(jnp.float32))
    head_shape = (micro, rows, HEADS, HEAD_DIM)
    query_h = query.reshape(head_shape)
    keys_h = keys.reshape(head_shape)
    values_h = values.reshape(head_shape)
    start_carry = (
        jnp.full((micro, HEADS, rows), -1e30, jnp.float32),
        jnp.zeros((micro, HEADS, rows), jnp.float32),
        jnp.zeros((micro, HEADS, rows, HEAD_DIM), jnp.float32),
    )
    carry = absorb(start_carry, query_h, keys_h, values_h, allowed_pairs(query_side, own_keys))

    def forward_hop(hop, state):
        pieces, inner = state
        pieces = from_behind((pieces[0], pieces[1]), "seq", 1)
        source = me_index - hop
        inner = absorb(
            inner, query_h, pieces[0], pieces[1], allowed_pairs(query_side, key_side(source))
        )
        return (pieces, inner)

    _, (run_max, run_sum, totals) = lax.fori_loop(
        1, hops + 1, forward_hop, ((keys_h, values_h), carry)
    )
    live = own_layout[2][:, None, :]
    safe_sum = jnp.where(live, run_sum, 1.0)
    attended_h = jnp.where(live[..., None], totals / safe_sum[..., None], 0.0)
    lse = jnp.where(live, run_max + jnp.log(safe_sum), 0.0)
    attended32 = attended_h.transpose(0, 2, 1, 3).reshape(tokens, width)
    attended = attended32.astype(jnp.bfloat16)
    branch_attn = dense(attended, full_out)
    hidden = gate_attn * branch_attn + (1.0 - gate_attn) * inputs
    normed_ffn, pull_ffn = jax.vjp(rms_norm, hidden, gain_ffn.astype(jnp.float32))
    normed_ffn_low = normed_ffn.astype(jnp.bfloat16)
    pre = dense(normed_ffn_low, full_in)
    act32, pull_gelu = jax.vjp(partial(jax.nn.gelu, approximate=True), pre)
    act = act32.astype(jnp.bfloat16)
    branch_ffn = dense(act, full_back)
    gate_ffn = jax.nn.sigmoid(dense(normed_ffn_low, full_gate_ffn) + shift_ffn.astype(jnp.float32))
    output = gate_ffn * branch_ffn + (1.0 - gate_ffn) * hidden
    again = (
        lax.all_gather(w_query, ("dp", "seq"), axis=0, tiled=True),
        lax.all_gather(w_key, ("dp", "seq"), axis=0, tiled=True),
        lax.all_gather(w_value, ("dp", "seq"), axis=0, tiled=True),
        lax.all_gather(w_out, ("dp", "seq"), axis=0, tiled=True),
        lax.all_gather(w_gate_attn, ("dp", "seq"), axis=0, tiled=True),
        lax.all_gather(w_gate_ffn, ("dp", "seq"), axis=0, tiled=True),
        lax.all_gather(w_in, ("dp", "seq"), axis=0, tiled=True),
        lax.all_gather(w_back, ("dp", "seq"), axis=0, tiled=True),
        lax.all_gather(norm_attn, ("dp", "seq"), axis=0, tiled=True),
        lax.all_gather(norm_ffn, ("dp", "seq"), axis=0, tiled=True),
        lax.all_gather(bias_attn, ("dp", "seq"), axis=0, tiled=True),
        lax.all_gather(bias_ffn, ("dp", "seq"), axis=0, tiled=True),
    )
    (
        back_query,
        back_key,
        back_value,
        back_out,
        back_gate_attn,
        back_gate_ffn,
        back_in,
        back_back,
        _,
        _,
        _,
        _,
    ) = again
    upstream = cotangent[:, 0].reshape(tokens, width).astype(jnp.float32)
    d_logit_ffn = (upstream * (branch_ffn - hidden) * gate_ffn * (1.0 - gate_ffn)).astype(
        jnp.bfloat16
    )
    d_branch_ffn = (upstream * gate_ffn).astype(jnp.bfloat16)
    grad_back = dense_tn(act, d_branch_ffn)
    (d_pre32,) = pull_gelu(dense_nt(d_branch_ffn, back_back))
    d_pre = d_pre32.astype(jnp.bfloat16)
    grad_in = dense_tn(normed_ffn_low, d_pre)
    grad_gate_ffn = dense_tn(normed_ffn_low, d_logit_ffn)
    grad_bias_ffn = jnp.sum(d_logit_ffn.astype(jnp.float32), axis=0)
    d_normed_ffn = dense_nt(d_pre, back_in) + dense_nt(d_logit_ffn, back_gate_ffn)
    d_hidden_norm, grad_gain_ffn = pull_ffn(d_normed_ffn)
    d_hidden = upstream * (1.0 - gate_ffn) + d_hidden_norm
    d_branch_attn = (d_hidden * gate_attn).astype(jnp.bfloat16)
    d_logit_attn = (d_hidden * (branch_attn - inputs) * gate_attn * (1.0 - gate_attn)).astype(
        jnp.bfloat16
    )
    grad_out = dense_tn(attended, d_branch_attn)
    d_attended = dense_nt(d_branch_attn, back_out).astype(jnp.bfloat16)
    grad_att = d_attended.reshape(head_shape)
    delta = jnp.einsum(
        "mqhd,mqhd->mhq", grad_att.astype(jnp.float32), attended32.reshape(head_shape)
    )
    first_q, first_k, first_v = hop_grads(
        query_h, grad_att, lse, delta, keys_h, values_h, allowed_pairs(query_side, own_keys)
    )

    def backward_hop(hop, state):
        pieces, moving, grad_q = state
        pieces = from_behind((pieces[0], pieces[1]), "seq", 1)
        moving = (
            passed_along(moving[0].astype(jnp.bfloat16), "seq", 1).astype(jnp.float32),
            passed_along(moving[1].astype(jnp.bfloat16), "seq", 1).astype(jnp.float32),
        )
        source = me_index - hop
        step_q, step_k, step_v = hop_grads(
            query_h,
            grad_att,
            lse,
            delta,
            pieces[0],
            pieces[1],
            allowed_pairs(query_side, key_side(source)),
        )
        return (pieces, (moving[0] + step_k, moving[1] + step_v), grad_q + step_q)

    _, moving, grad_q = lax.fori_loop(
        1, hops + 1, backward_hop, ((keys_h, values_h), (first_k, first_v), first_q)
    )
    moving = (
        passed_along(moving[0].astype(jnp.bfloat16), "seq", -hops).astype(jnp.float32),
        passed_along(moving[1].astype(jnp.bfloat16), "seq", -hops).astype(jnp.float32),
    )
    grad_k, grad_v = moving
    d_query = grad_q.reshape(tokens, width).astype(jnp.bfloat16)
    d_key = grad_k.reshape(tokens, width).astype(jnp.bfloat16)
    d_value = grad_v.reshape(tokens, width).astype(jnp.bfloat16)
    grad_query = dense_tn(normed_low, d_query)
    grad_key = dense_tn(normed_low, d_key)
    grad_value = dense_tn(normed_low, d_value)
    grad_gate_attn = dense_tn(normed_low, d_logit_attn)
    grad_bias_attn = jnp.sum(d_logit_attn.astype(jnp.float32), axis=0)
    d_normed_attn = (
        dense_nt(d_query, back_query)
        + dense_nt(d_key, back_key)
        + dense_nt(d_value, back_value)
        + dense_nt(d_logit_attn, back_gate_attn)
    )
    d_inputs_norm, grad_gain_attn = pull_attn(d_normed_attn)
    grad_input = d_hidden * (1.0 - gate_attn) + d_inputs_norm
    owned = (
        lax.psum_scatter(grad_query, ("dp", "seq"), scatter_dimension=0, tiled=True),
        lax.psum_scatter(grad_key, ("dp", "seq"), scatter_dimension=0, tiled=True),
        lax.psum_scatter(grad_value, ("dp", "seq"), scatter_dimension=0, tiled=True),
        lax.psum_scatter(grad_out, ("dp", "seq"), scatter_dimension=0, tiled=True),
        lax.psum_scatter(grad_gate_attn, ("dp", "seq"), scatter_dimension=0, tiled=True),
        lax.psum_scatter(grad_gate_ffn, ("dp", "seq"), scatter_dimension=0, tiled=True),
        lax.psum_scatter(grad_in, ("dp", "seq"), scatter_dimension=0, tiled=True),
        lax.psum_scatter(grad_back, ("dp", "seq"), scatter_dimension=0, tiled=True),
        lax.psum_scatter(grad_gain_attn, ("dp", "seq"), scatter_dimension=0, tiled=True),
        lax.psum_scatter(grad_gain_ffn, ("dp", "seq"), scatter_dimension=0, tiled=True),
        lax.psum_scatter(grad_bias_attn, ("dp", "seq"), scatter_dimension=0, tiled=True),
        lax.psum_scatter(grad_bias_ffn, ("dp", "seq"), scatter_dimension=0, tiled=True),
    )
    return (
        output.reshape(micro, 1, rows, width).astype(jnp.bfloat16),
        grad_input.reshape(micro, 1, rows, width),
        owned[0],
        owned[1],
        owned[2],
        owned[3],
        owned[4],
        owned[5],
        owned[6],
        owned[7],
        owned[8],
        owned[9],
        owned[10],
        owned[11],
    )


def solution(mesh):
    placed = (
        P(None, "dp", "seq", None),
        P(None, "dp", "seq", None),
        P(None, "dp", None),
        P(None, "dp", None),
        P(("dp", "seq"), None),
        P(("dp", "seq"), None),
        P(("dp", "seq"), None),
        P(("dp", "seq"), None),
        P(("dp", "seq"), None),
        P(("dp", "seq"), None),
        P(("dp", "seq"), None),
        P(("dp", "seq"), None),
        P(("dp", "seq")),
        P(("dp", "seq")),
        P(("dp", "seq")),
        P(("dp", "seq")),
    )
    def pick(layer_input, *others):
        micro, _, rows, width = layer_input.shape
        fits = (
            dict(mesh.shape) == {"dp": 4, "seq": 8}
            and micro == 2
            and others[1].shape[2] == 1
            and width == HEADS * HEAD_DIM
            and width == 4 * LANES
            and rows % 128 == 0
            and others[10].shape == (width // 8, width)
        )
        return (by_heads if fits else shards)(layer_input, *others)

    return jax.shard_map(
        pick,
        mesh=mesh,
        in_specs=placed,
        out_specs=(
            P(None, "dp", "seq", None),
            P(None, "dp", "seq", None),
            P(("dp", "seq"), None),
            P(("dp", "seq"), None),
            P(("dp", "seq"), None),
            P(("dp", "seq"), None),
            P(("dp", "seq"), None),
            P(("dp", "seq"), None),
            P(("dp", "seq"), None),
            P(("dp", "seq"), None),
            P(("dp", "seq")),
            P(("dp", "seq")),
            P(("dp", "seq")),
            P(("dp", "seq")),
        ),
        check_vma=False,
    )
```

```python
from functools import partial

import jax
import jax.numpy as jnp
from jax import lax
from jax.experimental import pallas as pl
from jax.experimental.pallas import tpu as pltpu
from jax.sharding import PartitionSpec as P

HEADS = 8
HEAD_DIM = 64
DOC_MAX = 4096

EPS = 1e-05
MESH = pl.DeviceIdType.MESH
BF = jnp.bfloat16
F32 = jnp.float32
VMEM_LIMIT = 66_000_000
LANES = 128
SIDE = 64
GELU_C = 0.7978845608028654
GELU_A = 0.044715
NEG = -1e30
ANY = pl.BlockSpec(memory_space=pl.ANY)
INVM = pl.BlockSpec(memory_space=pltpu.VMEM)
INSM = pl.BlockSpec(memory_space=pltpu.SMEM)


def nn(a, b):
    return lax.dot_general(a, b, (((1,), (0,)), ((), ())), preferred_element_type=F32)


def nt(a, b):
    return lax.dot_general(a, b, (((1,), (1,)), ((), ())), preferred_element_type=F32)


def tn(a, b):
    return lax.dot_general(a, b, (((0,), (0,)), ((), ())), preferred_element_type=F32)


def remote(src, dst, send, recv, dp, seq):
    return pltpu.make_async_remote_copy(
        src_ref=src, dst_ref=dst, send_sem=send, recv_sem=recv,
        device_id=(dp, seq), device_id_type=MESH,
    )


def greet(peers):
    barrier = pltpu.get_barrier_semaphore()
    for dp, seq in peers:
        pl.semaphore_signal(barrier, inc=1, device_id=(dp, seq), device_id_type=MESH)
    pl.semaphore_wait(barrier, len(peers))


def place():
    d = lax.axis_index("dp")
    j = lax.axis_index("seq")
    z = j // 2
    c = j % 2
    dx = d + 1 - 2 * (d % 2)
    dy = (d + 2) % 4
    dxy = 3 - d
    return d, j, z, c, dx, dy, dxy


CK = 4


def gather_kernel(x_ref, s_ref, xg_ref, wg_ref, xv, sv, lsem, wsend, wrecv, xsend, xrecv):
    d, j, z, c, dx, dy, dxy = place()
    g = z // 2
    pj = j + 1 - 2 * c
    za, zb, zc = z + 1 - 2 * (z % 2), (z + 2) % 4, 3 - z
    near = jnp.logical_or(z == 1, z == 2)
    far = jnp.logical_or(z == 0, z == 3)
    ja, jb, jc = 2 * za + c, 2 * zb + c, 2 * zc + c
    lx = pltpu.make_async_copy(x_ref.at[g], xv, lsem.at[0])
    ls = pltpu.make_async_copy(s_ref, sv, lsem.at[1])
    lx.start()
    ls.start()
    greet([(d, ja), (d, jb), (d, jc), (dx, j), (dy, j), (d, pj)])
    rows = xv.shape[0] // CK
    count = [0]
    waits = []

    def wcopy(slot, dp, seq, own=False):
        i = count[0]
        count[0] += 1
        copy = remote(
            s_ref if own else wg_ref.at[slot], wg_ref.at[slot], wsend.at[i], wrecv.at[slot], dp, seq
        )
        copy.start()
        waits.append(copy)

    def warrive(slot):
        remote(s_ref, wg_ref.at[slot], wsend.at[0], wrecv.at[slot], d, pj).wait_recv()

    def xcopy(k, part, block, dp, seq, src=None):
        piece = pl.ds(part * rows, rows)
        source = xg_ref.at[block, piece] if src is None else x_ref.at[src, piece]
        return remote(
            source, xg_ref.at[block, piece], xsend.at[k, part], xrecv.at[block, part], dp, seq
        )

    def xarrive(part, block):
        xcopy(0, part, block, d, pj).wait_recv()

    me = d * 8 + j
    for dp, seq in [(d, ja), (d, jb), (d, jc), (dx, j), (dy, j), (d, pj)]:
        wcopy(me, dp, seq, True)
    xwaits = []
    jn = 2 * (2 - g) + c
    for part in range(CK):
        for k, (src, seq) in enumerate([(1 - g, jn), (g, ja), (g, pj)]):
            copy = xcopy(k, part, j, d, seq, src)
            copy.start()
            xwaits.append(copy)
    lx.wait()
    ls.wait()
    ox = pltpu.make_async_copy(xv, xg_ref.at[j], lsem.at[0])
    ow = pltpu.make_async_copy(sv, wg_ref.at[me], lsem.at[1])
    ox.start()
    ow.start()

    def zarr(jz):
        slot = d * 8 + jz
        warrive(slot)
        wcopy(slot, dx, j)
        wcopy(slot, dy, j)
        wcopy(slot, d, pj)

    def xyarr(zz):
        jz = 2 * zz + c
        sx, sy = dx * 8 + jz, dy * 8 + jz
        even = zz % 2 == 0
        warrive(sx)
        wcopy(sx, d, pj)
        warrive(sy)
        wcopy(sy, d, pj)
        i = count[0]
        count[0] += 1

        def on(slot, dp):
            return remote(wg_ref.at[slot], wg_ref.at[slot], wsend.at[i], wrecv.at[slot], dp, j)

        @pl.when(even)
        def _():
            on(sx, dy).start()

        @pl.when(jnp.logical_not(even))
        def _():
            on(sy, dx).start()

        waits.append(on(sx, dy))

    zarr(ja)
    xyarr(z)
    zarr(jb)
    xyarr(za)
    zarr(jc)
    xyarr(zb)
    xyarr(zc)
    b1 = 2 * (2 - g) + c
    b2 = 2 * (3 * (1 - g)) + c
    for k, block in ((3, b1), (5, b2)):
        for part in range(CK):
            xarrive(part, block)
            copy = xcopy(k, part, block, d, pj)
            copy.start()
            xwaits.append(copy)

            @pl.when(near)
            def _():
                xcopy(k + 1, part, block, d, ja).start()

    for part in range(CK):
        xarrive(part, ja)
        copy = xcopy(7, part, ja, d, pj)
        copy.start()
        xwaits.append(copy)
    for zz in (z, za, zb, zc):
        slot = dxy * 8 + 2 * zz + c
        warrive(slot)
        wcopy(slot, d, pj)
    for dp in (d, dx, dy, dxy):
        for zz in (z, za, zb, zc):
            warrive(dp * 8 + 2 * zz + 1 - c)
    for block in (j, ja, b1, b2):
        for part in range(CK):
            xarrive(part, block + 1 - 2 * c)
    for copy in waits:
        copy.wait_send()
    for copy in xwaits:
        copy.wait_send()

    @pl.when(near)
    def _():
        for k, block in ((4, b1), (6, b2)):
            for part in range(CK):
                xcopy(k, part, block, d, ja).wait_send()

    ox.wait()
    ow.wait()


def gather(x, shard):
    _, rows, width = x.shape
    return pl.pallas_call(
        gather_kernel,
        out_shape=(
            jax.ShapeDtypeStruct((8, rows, width), BF),
            jax.ShapeDtypeStruct((32,) + shard.shape, BF),
        ),
        in_specs=[ANY, ANY],
        out_specs=(ANY, ANY),
        scratch_shapes=[
            pltpu.VMEM((rows, width), BF),
            pltpu.VMEM(shard.shape, BF),
            pltpu.SemaphoreType.DMA((2,)),
            pltpu.SemaphoreType.DMA((32,)),
            pltpu.SemaphoreType.DMA((32,)),
            pltpu.SemaphoreType.DMA((8, CK)),
            pltpu.SemaphoreType.DMA((8, CK)),
        ],
        compiler_params=pltpu.CompilerParams(collective_id=0, has_side_effects=True),
    )(x, shard)


def swap_kernel(a_ref, b_ref, av, lsem, send, recv):
    d = lax.axis_index("dp")
    j = lax.axis_index("seq")
    load = pltpu.make_async_copy(a_ref.at[j], av, lsem)
    load.start()
    peers = [(d, (j + k) % 8) for k in range(1, 8)]
    greet(peers)
    copies = []
    for k, (dp, seq) in enumerate(peers):
        copy = remote(a_ref.at[seq], b_ref.at[j], send.at[k], recv.at[k], dp, seq)
        copy.start()
        copies.append(copy)
    load.wait()
    keep = pltpu.make_async_copy(av, b_ref.at[j], lsem)
    keep.start()
    for copy in copies:
        copy.wait()
    keep.wait()


def swap(a, cid):
    return pl.pallas_call(
        swap_kernel,
        out_shape=jax.ShapeDtypeStruct(a.shape, a.dtype),
        in_specs=[ANY],
        out_specs=ANY,
        scratch_shapes=[
            pltpu.VMEM(a.shape[1:], a.dtype),
            pltpu.SemaphoreType.DMA,
            pltpu.SemaphoreType.DMA((7,)),
            pltpu.SemaphoreType.DMA((7,)),
        ],
        compiler_params=pltpu.CompilerParams(collective_id=cid, has_side_effects=True),
    )(a)


LOG2E = 1.4426950408889634


def lane_of(rows):
    return lax.broadcasted_iota(jnp.int32, (rows, LANES), 1)


def three(v):
    a = v.astype(BF).astype(F32)
    b = (v - a).astype(BF).astype(F32)
    return a, b, v - a - b


def beside(h, lane, values, parts):
    first = SIDE * (1 - h)
    own = (lane < SIDE) if h == 0 else (lane >= SIDE)
    out = jnp.where(own, values, 0.0)
    for k, part in enumerate(parts):
        if part is not None:
            out = jnp.where(lane == first + k, part, out)
    return out.astype(BF)


def upper(rows):
    return lax.broadcasted_iota(jnp.int32, (rows, rows), 0) <= lax.broadcasted_iota(
        jnp.int32, (rows, rows), 1
    )


def attend_kernel(doc, x_ref, w_ref, gain_ref, o_ref, o32_ref, qa, ka, va, vt):
    blocks, rows, width = x_ref.shape
    off = doc[0]
    end = off + doc[1]
    lane = lane_of(rows)
    up = lax.broadcasted_iota(jnp.int32, (rows, 1), 0)
    along = lax.broadcasted_iota(jnp.int32, (1, rows), 1)
    gain = gain_ref[...].astype(F32)
    tall = lax.broadcasted_iota(jnp.int32, (16, rows), 0)
    ones = jnp.where(tall == 0, 1.0, 0.0).astype(BF)

    def project(b, _):
        x = x_ref[b].astype(F32)
        n = (x * lax.rsqrt(jnp.mean(x * x, -1, keepdims=True) + EPS) * gain).astype(BF)
        p = nn(n, w_ref[...])
        pos = b * rows + up
        bad = jnp.where(jnp.logical_and(pos >= off, pos < end), 0.0, NEG)
        q = p[:, :LANES] * (HEAD_DIM ** (-0.5) * LOG2E)
        k = p[:, LANES : 2 * LANES]
        v = p[:, 2 * LANES :]
        for h in range(2):
            qa[h, b] = beside(h, lane, q, (1.0,))
            ka[h, b] = beside(h, lane, k, (bad, 1.0, 1.0, 1.0))
            va[h, b] = beside(h, lane, v, (None, 1.0, 1.0, 1.0))
        turned = v.astype(BF).T
        for h in range(2):
            vt[h, b, :SIDE] = turned[h * SIDE : (h + 1) * SIDE]
            vt[h, b, SIDE:] = ones
        return 0

    lax.fori_loop(0, blocks, project, 0)
    keep = upper(rows)
    sub = lax.broadcasted_iota(jnp.int32, (LANES, rows), 0)

    def one(b, _):
        pos = b * rows + along
        live = jnp.logical_and(pos >= off, pos < end)

        def score(h, kb, masked):
            s = nt(ka[h, kb], qa[h, b])
            return jnp.where(keep, s, NEG) if masked else s

        def step(kb, carry, masked=False):
            ss = [score(h, kb, masked) for h in range(2)]
            new = [jnp.maximum(carry[h][0], jnp.max(ss[h], 0, keepdims=True)) for h in range(2)]
            ps = [jnp.exp2(ss[h] - new[h]).astype(BF) for h in range(2)]
            return tuple(
                (new[h], carry[h][1] * jnp.exp2(carry[h][0] - new[h]) + nn(vt[h, kb], ps[h])) for h in range(2)
            )

        start = ((jnp.full((1, rows), NEG, F32), jnp.zeros((SIDE + 16, rows), F32)),) * 2
        done = step(b, lax.fori_loop(0, b, step, start), True)
        m = [v[0] for v in done]
        acc = [v[1] for v in done]
        outs = []
        for h in range(2):
            total = acc[h][SIDE : SIDE + 1]
            lse = jnp.where(live, m[h] + jnp.log2(total), -NEG)
            own = jnp.where(live, acc[h][:SIDE] / total, 0.0)
            parts = three(lse)
            side = jnp.zeros((SIDE, rows), F32)
            for k in range(3):
                side = jnp.where(sub[:SIDE] == k + 1, -parts[k], side)
            both = (own, side) if h == 0 else (side, own)
            out = jnp.concatenate(both, axis=0).T
            first = SIDE * (1 - h)
            aug = jnp.logical_and(lane > first, lane < first + 4)
            qa[h, b] = jnp.where(aug, out, qa[h, b].astype(F32)).astype(BF)
            outs.append(out)
        out = jnp.where(lane < SIDE, outs[0], outs[1])
        o32_ref[b] = out
        o_ref[b] = out.astype(BF)
        return 0

    lax.fori_loop(0, blocks, one, 0)


def attend(doc, xg, w, gain):
    blocks, rows, width = xg.shape
    side = jax.ShapeDtypeStruct((2, blocks, rows, LANES), BF)
    return pl.pallas_call(
        attend_kernel,
        out_shape=(
            jax.ShapeDtypeStruct((blocks, rows, LANES), BF),
            jax.ShapeDtypeStruct((blocks, rows, LANES), F32),
            side, side, side,
        ),
        in_specs=[INSM, INVM, INVM, INVM],
        out_specs=(INVM,) * 5,
        scratch_shapes=[pltpu.VMEM((2, blocks, SIDE + 16, rows), BF)],
        compiler_params=pltpu.CompilerParams(vmem_limit_bytes=VMEM_LIMIT),
        name="attend",
    )(doc, xg, w, gain)


def token_kernel(
    x_ref, c_ref, a_ref, wg, vec, out_ref, da_ref, dh_ref, dn_ref, g_ref, v_ref,
    gp, act, g_out, g_ga, g_gf, g_in, g_back,
):
    step = pl.program_id(0)
    rows, width = x_ref.shape[1:]
    ff = gp.shape[0]
    per = width // 32

    def weight(lo):
        return wg[:, lo : lo + per, :].reshape(width, width)

    def back(k):
        n = wg.shape[0] // ff
        return wg[k * n : (k + 1) * n, 10 * per : 10 * per + ff * per, :].reshape(width, width)

    @pl.when(step == 0)
    def _():
        for ref in (g_out, g_ga, g_gf, g_in, g_back, v_ref):
            ref[...] = jnp.zeros_like(ref)

    x = x_ref[0].astype(F32)
    gain_a, gain_f = vec[0:1].astype(F32), vec[1:2].astype(F32)
    shift_a, shift_f = vec[2:3].astype(F32), vec[3:4].astype(F32)
    n1 = x * lax.rsqrt(jnp.mean(x * x, -1, keepdims=True) + EPS)
    na = (n1 * gain_a).astype(BF)
    ga = jax.nn.sigmoid(nn(na, weight(4 * per)) + shift_a)
    att = jnp.concatenate([a_ref[i] for i in range(4)], axis=1)
    br = nn(att, weight(3 * per))
    hid = ga * br + (1.0 - ga) * x
    r2 = lax.rsqrt(jnp.mean(hid * hid, -1, keepdims=True) + EPS)
    n2 = hid * r2
    nf = (n2 * gain_f).astype(BF)
    bf = jnp.zeros((rows, width), F32)
    for k in range(ff):
        pre = nn(nf, weight((6 + k) * per))
        sq = pre * pre
        t = jnp.tanh(GELU_C * pre * (1.0 + GELU_A * sq))
        half = 0.5 * (1.0 + t)
        act[k] = (pre * half).astype(BF)
        gp[k] = half + 0.5 * pre * (1.0 - t * t) * (GELU_C * (1.0 + 3.0 * GELU_A * sq))
        bf += nn(act[k], back(k))
    gf = jax.nn.sigmoid(nn(nf, weight(5 * per)) + shift_f)
    out_ref[0] = (gf * bf + (1.0 - gf) * hid).astype(BF)
    c = c_ref[0].astype(F32)
    dlf = (c * (bf - hid) * gf * (1.0 - gf)).astype(BF)
    dbf = (c * gf).astype(BF)
    dnf = nt(dlf, weight(5 * per))
    g_gf[...] += tn(nf, dlf)
    for k in range(ff):
        dpre = (nt(dbf, back(k)) * gp[k]).astype(BF)
        g_back[k] += tn(act[k], dbf)
        g_in[k] += tn(nf, dpre)
        dnf += nt(dpre, weight((6 + k) * per))
    g2 = dnf * gain_f
    dh = c * (1.0 - gf) + r2 * (g2 - n2 * jnp.mean(g2 * n2, -1, keepdims=True))
    dba = (dh * ga).astype(BF)
    dla = (dh * (br - x) * ga * (1.0 - ga)).astype(BF)
    g_out[...] += tn(att, dba)
    g_ga[...] += tn(na, dla)
    datt = nt(dba, weight(3 * per)).astype(BF)
    for i in range(4):
        da_ref[i] = datt[:, i * LANES : (i + 1) * LANES]
    dna = nt(dla, weight(4 * per))
    dh_ref[0] = dh * (1.0 - ga)
    dn_ref[0] = dna
    v_ref[0:1] += jnp.sum(dna * n1, 0, keepdims=True)
    v_ref[1:2] += jnp.sum(dnf * n2, 0, keepdims=True)
    v_ref[2:3] += jnp.sum(dla.astype(F32), 0, keepdims=True)
    v_ref[3:4] += jnp.sum(dlf.astype(F32), 0, keepdims=True)

    @pl.when(step == pl.num_programs(0) - 1)
    def _():
        def put(lo, value):
            g_ref[:, lo : lo + per, :] = value.astype(BF).reshape(32, per, width)

        put(0, g_out[...])
        put(per, g_ga[...])
        put(2 * per, g_gf[...])
        for k in range(ff):
            put((3 + k) * per, g_in[k])
            n = 32 // ff
            g_ref[k * n : (k + 1) * n, (3 + ff) * per :, :] = (
                g_back[k].astype(BF).reshape(n, ff * per, width)
            )


def tokens(x, cot, att, wg, vec):
    micro, rows, width = x.shape
    ff = 4
    per = width // 32
    tok = pl.BlockSpec((1, rows, width), lambda i: (i, 0, 0))
    head = pl.BlockSpec((4, rows, LANES), lambda i: (i, 0, 0))

    def whole(shape):
        return pl.BlockSpec(shape, lambda i: (0,) * len(shape), pipeline_mode=pl.Buffered(1))

    grads = (32, (3 + 2 * ff) * per, width)
    return pl.pallas_call(
        token_kernel,
        grid=(micro,),
        out_shape=(
            jax.ShapeDtypeStruct((micro, rows, width), BF),
            jax.ShapeDtypeStruct((4 * micro, rows, LANES), BF),
            jax.ShapeDtypeStruct((micro, rows, width), F32),
            jax.ShapeDtypeStruct((micro, rows, width), F32),
            jax.ShapeDtypeStruct(grads, BF),
            jax.ShapeDtypeStruct((8, width), F32),
        ),
        in_specs=[tok, tok, head, whole(wg.shape), whole(vec.shape)],
        out_specs=(tok, head, tok, tok, whole(grads), whole((8, width))),
        scratch_shapes=[
            pltpu.VMEM((ff, rows, width), F32),
            pltpu.VMEM((ff, rows, width), BF),
            pltpu.VMEM((width, width), F32),
            pltpu.VMEM((width, width), F32),
            pltpu.VMEM((width, width), F32),
            pltpu.VMEM((ff, width, width), F32),
            pltpu.VMEM((ff, width, width), F32),
        ],
        compiler_params=pltpu.CompilerParams(vmem_limit_bytes=VMEM_LIMIT),
    )(x, cot, att, wg, vec)


def add_into(dst, src):
    rows = dst.shape[0]
    n = rows // 16
    per = 16 * max(k for k in range(1, 9) if n % k == 0)

    def body(i, _):
        piece = pl.ds(i * per, per)
        dst[piece, :] = (dst[piece, :].astype(F32) + src[piece, :].astype(F32)).astype(BF)
        return 0

    lax.fori_loop(0, rows // per, body, 0)


def attend_back_kernel(
    x_ref, w_ref, gain_ref, o32_ref, do_ref, qa, ka, va, sum_ref, g_ref,
    dn_ref, gf_ref, gq_ref, gv_ref,
    da, qt, kt, dot, dq, dk, dv, dw, pb, hs_buf, vs_buf,
    acc, b1, b2, b3, b4, q1, q2, hb, vb, own,
    l2, lo, s1, r1, s2, r2, s3, r3, s4, r4, ps, pr, ts, tr, us, ur, hs, hr, vs, vr,
):
    blocks, rows, width = x_ref.shape
    per = width // 32
    d, j, z, c, dx, dy, dxy = place()
    me = d * 8 + j
    g = z // 2
    pj = j + 1 - 2 * c
    za, zb, zc = z + 1 - 2 * (z % 2), (z + 2) % 4, 3 - z
    ja, jb, jc = 2 * za + c, 2 * zb + c, 2 * zc + c
    near = jnp.logical_or(z == 1, z == 2)
    far = jnp.logical_or(z == 0, z == 3)
    w3, w2, wn, wf = 3 * (1 - g), 2 - g, 1 + g, 3 * g
    first = [(zz, dp) for zz in range(4) for dp in ((dx, dxy) if zz % 2 == 0 else (dy, dxy))]
    rest = [(zz, dp) for zz in range(4) for dp in ((d, dy) if zz % 2 == 0 else (d, dx))]

    gloads = []
    for k, (zz, dp) in enumerate(first + rest):
        copy = pltpu.make_async_copy(g_ref.at[dp * 8 + 2 * zz + c], acc.at[dp * 4 + zz], l2.at[k])
        copy.start()
        gloads.append(copy)

    barrier = pltpu.get_barrier_semaphore()

    def hello(k, _):
        slot = (me + k) % 32
        pl.semaphore_signal(
            barrier, inc=1, device_id=(slot // 8, slot % 8), device_id_type=MESH
        )
        return 0

    lax.fori_loop(1, 32, hello, 0)
    pl.semaphore_wait(barrier, 31)

    def gcopy(zz, dp):
        i = dp * 4 + zz
        return remote(g_ref.at[dp * 8 + 2 * zz + 1 - c], b1.at[i], s1.at[i], r1.at[i], d, pj)

    def stage2(zz, dp):
        i = dp * 4 + zz
        to = dx if zz % 2 == 0 else dy
        return remote(acc.at[i], b2.at[i], s2.at[i], r2.at[i], to, j)

    def stage3(zz):
        to = dy if zz % 2 == 0 else dx
        return remote(acc.at[to * 4 + zz], b3.at[zz], s3.at[zz], r3.at[zz], to, j)

    def stage4(k, zz, jz):
        return remote(acc.at[d * 4 + zz], b4.at[z], s4.at[k], r4.at[z], d, jz)

    def pcopy(zz):
        return remote(pb.at[2 * zz + 1 - c], q1.at[zz], ps.at[zz], pr.at[zz], d, pj)

    def tcopy(zz):
        return remote(pb.at[2 * zz + c], q2.at[zz], ts.at[zz], tr.at[zz], d, ja)

    def ucopy(k, zz):
        return remote(pb.at[2 * zz + c], dn_ref.at[g], us.at[k], ur.at[0], d, 2 * zz + c)

    def hcopy(k):
        slot = (me + k) % 32
        return remote(hs_buf.at[slot], hb.at[me], hs.at[k], hr.at[me], slot // 8, slot % 8)

    def vcopy(k):
        slot = (me + k) % 32
        return remote(vs_buf, vb.at[me], vs.at[k], vr.at[me], slot // 8, slot % 8)

    for zz, dp in first + rest:
        gcopy(zz, dp).start()

    def sums1():
        for k, (zz, dp) in enumerate(first + rest):
            gloads[k].wait()
            gcopy(zz, dp).wait_recv()
            add_into(acc.at[dp * 4 + zz], b1.at[dp * 4 + zz])
            if k < len(first):
                stage2(zz, dp).start()

    def sums2():
        for pick in (1, 0):
            for zz in range(4):
                dp = (d, dy if zz % 2 == 0 else dx)[pick]
                stage2(zz, dp).wait_recv()
                add_into(acc.at[dp * 4 + zz], b2.at[dp * 4 + zz])
                if pick:
                    stage3(zz).start()

    def sums3():
        for zz in range(4):
            stage3(zz).wait_recv()
            add_into(acc.at[d * 4 + zz], b3.at[zz])
        for k, (zz, jz) in enumerate(((za, ja), (zb, jb), (zc, jc))):
            stage4(k, zz, jz).start()

    def both_cores(zz):
        pcopy(zz).wait_recv()
        add_into(pb.at[2 * zz + c], q1.at[zz])

    def pass_on(k, zz):
        @pl.when(near)
        def _():
            tcopy(zz).wait_recv()
            add_into(pb.at[2 * zz + c], q2.at[zz])
            ucopy(k, zz).start()

    def to_near(zz):
        @pl.when(far)
        def _():
            tcopy(zz).start()

    def event0():
        both_cores(w3)
        to_near(w3)

    def event1():
        both_cores(w2)
        to_near(w2)
        pass_on(0, w3)

    def event2():
        both_cores(wn)
        to_near(wn)
        pass_on(1, w2)

    events = {(0, 3): sums1, (1, 4): sums2, (2, 0): event0, (2, 3): sums3, (4, 0): event1, (6, 0): event2}

    lane = lane_of(rows)
    low = upper(rows)
    left = lane < SIDE

    def prepare(b, _):
        do = do_ref[b].astype(F32)
        both = do * o32_ref[b]
        for h in range(2):
            mine = left if h == 0 else jnp.logical_not(left)
            delta = jnp.sum(jnp.where(mine, both, 0.0), -1, keepdims=True)
            a, bb, cc = three(delta)
            da[h, b] = beside(h, lane, do, (None, -a, -bb, -cc))
        qt[b] = jnp.where(left, qa[0, b], qa[1, b]).T
        kt[b] = jnp.where(left, ka[0, b], ka[1, b]).T
        dot[b] = do_ref[b].T
        dq[b] = jnp.zeros((LANES, rows), F32)
        dk[b] = jnp.zeros((LANES, rows), F32)
        dv[b] = jnp.zeros((LANES, rows), F32)
        return 0

    lax.fori_loop(0, blocks, prepare, 0)
    gain = gain_ref[...].astype(F32)
    dw[...] = jnp.zeros_like(dw)
    vs_buf[...] = sum_ref[...]

    def finish(b):
        x = x_ref[b].astype(F32)
        n1 = x * lax.rsqrt(jnp.mean(x * x, -1, keepdims=True) + EPS)
        n = (n1 * gain).astype(BF)
        q = (dq[b] * HEAD_DIM ** (-0.5)).astype(BF)
        k = (dk[b] * (1.0 / LOG2E)).astype(BF)
        pt = jnp.concatenate([q, k, dv[b].astype(BF)], axis=0)
        dw[...] += nn(pt, n)
        dn = nt(pt.T, w_ref[...])
        pb[b] = dn.astype(BF)
        vs_buf[0:1] += jnp.sum(dn * n1, 0, keepdims=True)

    def pair(kb, b, masked=False):
        for h in range(2):
            part = slice(h * SIDE, (h + 1) * SIDE)
            p = jnp.exp2(nt(ka[h, kb], qa[h, b]))
            if masked:
                p = jnp.where(low, p, 0.0)
            ds = (p * nt(va[h, kb], da[h, b])).astype(BF)
            dv[kb, part] += nt(dot[b, part], p.astype(BF))
            dk[kb, part] += nt(qt[b, part], ds)
            dq[b, part] += nn(kt[kb, part], ds)

    def outer(i, _):
        o = g * i + (1 - g) * (blocks - 1 - i)
        pair(o, o, True)

        def inner(t, _):
            pair(g * o + (1 - g) * (o - 1 - t), g * (o + 1 + t) + (1 - g) * o)
            for (ei, et), event in events.items():
                pl.when(jnp.logical_and(i == ei, t == et))(event)
            return 0

        lax.fori_loop(0, blocks - 1 - i, inner, 0)
        finish(o)

        @pl.when(o % 2 != c)
        def _():
            pcopy(o // 2).start()

        return 0

    lax.fori_loop(0, blocks, outer, 0)
    wide = dw[...].T.astype(BF)
    hs_buf[...] = wide.reshape(32, per, 3 * LANES)
    keep_h = pltpu.make_async_copy(hs_buf.at[me], hb.at[me], lo.at[0])
    keep_v = pltpu.make_async_copy(vs_buf, vb.at[me], lo.at[1])
    keep_h.start()
    keep_v.start()

    def hstart(k, _):
        hcopy(k).start()
        vcopy(k).start()
        return 0

    both_cores(wf)

    @pl.when(near)
    def _():
        tcopy(wf).start()

    lax.fori_loop(1, 32, hstart, 0)
    for zz in (za, zb, zc):
        remote(acc.at[0], b4.at[zz], s4.at[0], r4.at[zz], d, ja).wait_recv()
    gf_ref[...] = (
        acc[d * 4 + z].astype(F32)
        + b4[za].astype(F32) + b4[zb].astype(F32) + b4[zc].astype(F32)
    )
    keep_h.wait()
    keep_v.wait()

    def harrive(k, _):
        slot = (me + k) % 32
        remote(hs_buf.at[0], hb.at[slot], hs.at[0], hr.at[slot], d, pj).wait_recv()
        remote(vs_buf, vb.at[slot], vs.at[0], vr.at[slot], d, pj).wait_recv()
        return 0

    lax.fori_loop(1, 32, harrive, 0)
    total = jnp.zeros(gv_ref.shape, F32)
    for hi in range(4):
        part = jnp.zeros((per, 3 * LANES), F32)
        for k in range(8):
            slot = (k // 2) * 8 + (k % 2) * 4 + hi
            part += hb[slot].astype(F32)
            total += vb[slot]
        for m in range(3):
            gq_ref[m, :, hi * LANES : (hi + 1) * LANES] = part[:, m * LANES : (m + 1) * LANES]
    gv_ref[...] = total
    tcopy(z).wait_recv()

    def mine(i, _):
        piece = pl.ds(i * 128, 128)
        own[piece, :] = (pb[j, piece, :].astype(F32) + q2[z, piece, :].astype(F32)).astype(BF)
        return 0

    lax.fori_loop(0, rows // 128, mine, 0)
    keep = pltpu.make_async_copy(own, dn_ref.at[g], lo.at[2])
    keep.start()
    ucopy(0, w3).wait_recv()
    for zz, dp in first + rest:
        gcopy(zz, dp).wait_send()
    for zz, dp in first:
        stage2(zz, dp).wait_send()
    for zz in range(4):
        stage3(zz).wait_send()
        pcopy(zz).wait_send()
    for k, (zz, jz) in enumerate(((za, ja), (zb, jb), (zc, jc))):
        stage4(k, zz, jz).wait_send()

    def hsent(k, _):
        hcopy(k).wait_send()
        vcopy(k).wait_send()
        return 0

    lax.fori_loop(1, 32, hsent, 0)

    @pl.when(near)
    def _():
        tcopy(wf).wait_send()
        ucopy(0, w3).wait_send()
        ucopy(1, w2).wait_send()

    @pl.when(far)
    def _():
        for zz in (w3, w2, wn):
            tcopy(zz).wait_send()

    keep.wait()


def attend_back(xg, w, gain, o32, do, qa, ka, va, sums, grads):
    blocks, rows, width = xg.shape
    g = grads.shape[1:]
    per = width // 32
    dma = pltpu.SemaphoreType.DMA
    turned = pltpu.VMEM((blocks, LANES, rows), BF)
    total = pltpu.VMEM((blocks, LANES, rows), F32)
    return pl.pallas_call(
        attend_back_kernel,
        out_shape=(
            jax.ShapeDtypeStruct((2, rows, width), BF),
            jax.ShapeDtypeStruct(g, F32),
            jax.ShapeDtypeStruct((3, per, width), F32),
            jax.ShapeDtypeStruct(sums.shape, F32),
        ),
        in_specs=[INVM] * 9 + [ANY],
        out_specs=(ANY, INVM, INVM, INVM),
        scratch_shapes=[
            pltpu.VMEM((2, blocks, rows, LANES), BF), turned, turned, turned, total, total, total,
            pltpu.VMEM((3 * LANES, width), F32),
            pltpu.VMEM((blocks, rows, width), BF),
            pltpu.VMEM((32, per, 3 * LANES), BF),
            pltpu.VMEM(sums.shape, F32),
            pltpu.VMEM((16,) + g, BF),
            pltpu.VMEM((16,) + g, BF),
            pltpu.VMEM((16,) + g, BF),
            pltpu.VMEM((4,) + g, BF),
            pltpu.VMEM((4,) + g, BF),
            pltpu.VMEM((4, rows, width), BF),
            pltpu.VMEM((4, rows, width), BF),
            pltpu.VMEM((32, per, 3 * LANES), BF),
            pltpu.VMEM((32,) + sums.shape, F32),
            pltpu.VMEM((rows, width), BF),
            dma((16,)), dma((3,)),
            dma((16,)), dma((16,)), dma((16,)), dma((16,)), dma((4,)), dma((4,)), dma((4,)), dma((4,)),
            dma((4,)), dma((4,)), dma((4,)), dma((4,)), dma((2,)), dma((1,)),
            dma((32,)), dma((32,)), dma((32,)), dma((32,)),
        ],
        compiler_params=pltpu.CompilerParams(
            collective_id=3, has_side_effects=True, vmem_limit_bytes=VMEM_LIMIT
        ),
        name="attend_back",
    )(xg, w, gain, o32, do, qa, ka, va, sums, grads)


def by_heads(
    layer_input, cotangent, doc_len, doc_offset,
    w_query, w_key, w_value, w_out, w_gate_attn, w_gate_ffn, w_in, w_back,
    norm_attn, norm_ffn, bias_attn, bias_ffn,
):
    micro, _, rows, width = layer_input.shape
    per = w_query.shape[0]
    ff = w_in.shape[1] // width
    j = lax.axis_index("seq")
    g = j // 4
    hi = j % 4
    x = layer_input[:, 0]
    cot = cotangent[:, 0]
    vec = jnp.stack([norm_attn, norm_ffn, bias_attn, bias_ffn])
    shard = jnp.concatenate(
        [w_query, w_key, w_value, w_out, w_gate_attn, w_gate_ffn]
        + [w_in[:, k * width : (k + 1) * width] for k in range(ff)]
        + [w_back, jnp.pad(vec, ((0, 12), (0, width - per)))]
    )
    xg, wg = gather(x, shard)
    vecs = wg[:, -16:-12, :per].transpose(1, 0, 2).reshape(4, width)
    w = lax.dynamic_slice(wg, (0, 0, hi * LANES), (32, 3 * per, LANES))
    w = w.reshape(32, 3, per, LANES).transpose(0, 2, 1, 3).reshape(width, 3 * LANES)
    doc = jnp.stack([doc_offset[g, 0, 0], doc_len[g, 0, 0]])
    gain = vecs[0:1]
    o, o32, qa, ka, va = attend(doc, xg, w, gain)
    att = swap(o, 1)
    out, datt, dh, dna, grads, sums = tokens(x, cot, att, wg, vecs)
    do = swap(datt, 2)
    dn, gf, gq, gv = attend_back(xg, w, gain, o32, do, qa, ka, va, sums, grads)
    x32 = x.astype(F32)
    r1 = lax.rsqrt(jnp.mean(x32 * x32, -1, keepdims=True) + EPS)
    n1 = x32 * r1
    g1 = (dna + dn.astype(F32)) * gain.astype(F32)
    grad = dh + r1 * (g1 - n1 * jnp.mean(g1 * n1, -1, keepdims=True))
    gv = lax.dynamic_slice(gv, (0, (lax.axis_index("dp") * 8 + j) * per), (4, per))
    return (
        out[:, None],
        grad[:, None],
        gq[0], gq[1], gq[2],
        gf[:per], gf[per : 2 * per], gf[2 * per : 3 * per],
        gf[3 * per : (3 + ff) * per].reshape(ff, per, width).transpose(1, 0, 2).reshape(per, ff * width),
        gf[(3 + ff) * per :],
        gv[0], gv[1], gv[2], gv[3],
    )


def from_behind(x, axis, by):
    count = lax.axis_size(axis)
    pairs = [(i, i + by) for i in range(count) if 0 <= i + by < count]
    return lax.ppermute(x, axis, pairs)


def passed_along(value, axis, steps):
    count = lax.axis_size(axis)
    pairs = [(source, (source + steps) % count) for source in range(count)]
    return lax.ppermute(value, axis, pairs)


def rms_norm(values, gain):
    return values * lax.rsqrt(jnp.mean(values * values, -1, keepdims=True) + EPS) * gain


def dense(left, right):
    return jnp.dot(left, right, preferred_element_type=jnp.float32)


def dense_tn(left, right):
    return lax.dot_general(
        left, right, (((0,), (0,)), ((), ())), preferred_element_type=jnp.float32
    )


def dense_nt(left, right):
    return lax.dot_general(
        left, right, (((1,), (1,)), ((), ())), preferred_element_type=jnp.float32
    )


def layout_of(lengths, offsets, source, rows, filler):
    positions = source * rows + jnp.arange(rows, dtype=jnp.int32)
    region = positions // DOC_MAX
    inside = positions - region * DOC_MAX
    members = (region[:, None] == jnp.arange(lengths.shape[1], dtype=jnp.int32)[None, :]).astype(
        jnp.int32
    )
    begins = jnp.sum(members[None] * offsets[:, None, :], axis=2)
    spans = jnp.sum(members[None] * lengths[:, None, :], axis=2)
    inside_doc = (inside[None] >= begins) & (inside[None] < begins + spans)
    labels = jnp.where(inside_doc, region[None], filler)
    return (positions, labels, inside_doc)


def allowed_pairs(query_side, key_side):
    same_doc = query_side[1][:, :, None] == key_side[1][:, None, :]
    causal = key_side[0][None, None, :] <= query_side[0][None, :, None]
    return same_doc & causal


def absorb(carry, query, key_piece, value_piece, allowed):
    run_max, run_sum, totals = carry
    scores = jnp.einsum(
        "mqhd,mkhd->mhqk", query, key_piece, preferred_element_type=jnp.float32
    ) * HEAD_DIM ** (-0.5)
    scores = jnp.where(allowed[:, None], scores, -1e30)
    new_max = jnp.maximum(run_max, jnp.max(scores, axis=-1))
    factor = jnp.exp(run_max - new_max)
    weights = jnp.where(allowed[:, None], jnp.exp(scores - new_max[..., None]), 0.0)
    run_sum = run_sum * factor + jnp.sum(weights, axis=-1)
    totals = totals * factor[..., None] + jnp.einsum(
        "mhqk,mkhd->mhqd", weights, value_piece.astype(jnp.float32)
    )
    return (new_max, run_sum, totals)


def hop_grads(query, grad_att, lse, delta, key_piece, value_piece, allowed):
    scores = jnp.einsum(
        "mqhd,mkhd->mhqk", query, key_piece, preferred_element_type=jnp.float32
    ) * HEAD_DIM ** (-0.5)
    probs = jnp.where(allowed[:, None], jnp.exp(scores - lse[..., None]), 0.0)
    grad_value = jnp.einsum("mhqk,mqhd->mkhd", probs, grad_att.astype(jnp.float32))
    grad_probs = jnp.einsum(
        "mqhd,mkhd->mhqk", grad_att, value_piece, preferred_element_type=jnp.float32
    )
    grad_scores = probs * (grad_probs - delta[..., None]) * HEAD_DIM ** (-0.5)
    grad_query = jnp.einsum("mhqk,mkhd->mqhd", grad_scores, key_piece.astype(jnp.float32))
    grad_key = jnp.einsum("mhqk,mqhd->mkhd", grad_scores, query.astype(jnp.float32))
    return (grad_query, grad_key, grad_value)


def shards(
    layer_input,
    cotangent,
    doc_len,
    doc_offset,
    w_query,
    w_key,
    w_value,
    w_out,
    w_gate_attn,
    w_gate_ffn,
    w_in,
    w_back,
    norm_attn,
    norm_ffn,
    bias_attn,
    bias_ffn,
):
    gathered = (
        lax.all_gather(w_query, ("dp", "seq"), axis=0, tiled=True),
        lax.all_gather(w_key, ("dp", "seq"), axis=0, tiled=True),
        lax.all_gather(w_value, ("dp", "seq"), axis=0, tiled=True),
        lax.all_gather(w_out, ("dp", "seq"), axis=0, tiled=True),
        lax.all_gather(w_gate_attn, ("dp", "seq"), axis=0, tiled=True),
        lax.all_gather(w_gate_ffn, ("dp", "seq"), axis=0, tiled=True),
        lax.all_gather(w_in, ("dp", "seq"), axis=0, tiled=True),
        lax.all_gather(w_back, ("dp", "seq"), axis=0, tiled=True),
        lax.all_gather(norm_attn, ("dp", "seq"), axis=0, tiled=True),
        lax.all_gather(norm_ffn, ("dp", "seq"), axis=0, tiled=True),
        lax.all_gather(bias_attn, ("dp", "seq"), axis=0, tiled=True),
        lax.all_gather(bias_ffn, ("dp", "seq"), axis=0, tiled=True),
    )
    (
        full_query,
        full_key,
        full_value,
        full_out,
        full_gate_attn,
        full_gate_ffn,
        full_in,
        full_back,
        gain_attn,
        gain_ffn,
        shift_attn,
        shift_ffn,
    ) = gathered
    micro = layer_input.shape[0]
    rows = layer_input.shape[2]
    width = layer_input.shape[3]
    tokens = micro * rows
    nseq = lax.axis_size("seq")
    me_index = lax.axis_index("seq")
    hops = min(max(DOC_MAX // rows, 1), nseq) - 1
    lengths = doc_len[:, 0]
    offsets = doc_offset[:, 0]

    def key_side(source):
        positions, labels, _ = layout_of(lengths, offsets, source, rows, -2)
        return (positions, labels)

    own_layout = layout_of(lengths, offsets, me_index, rows, -1)
    query_side = (own_layout[0], own_layout[1])
    own_keys = key_side(me_index)
    inputs = layer_input[:, 0].reshape(tokens, width).astype(jnp.float32)
    normed_attn, pull_attn = jax.vjp(rms_norm, inputs, gain_attn.astype(jnp.float32))
    normed_low = normed_attn.astype(jnp.bfloat16)
    query = dense(normed_low, full_query).astype(jnp.bfloat16)
    keys = dense(normed_low, full_key).astype(jnp.bfloat16)
    values = dense(normed_low, full_value).astype(jnp.bfloat16)
    gate_attn = jax.nn.sigmoid(dense(normed_low, full_gate_attn) + shift_attn.astype(jnp.float32))
    head_shape = (micro, rows, HEADS, HEAD_DIM)
    query_h = query.reshape(head_shape)
    keys_h = keys.reshape(head_shape)
    values_h = values.reshape(head_shape)
    start_carry = (
        jnp.full((micro, HEADS, rows), -1e30, jnp.float32),
        jnp.zeros((micro, HEADS, rows), jnp.float32),
        jnp.zeros((micro, HEADS, rows, HEAD_DIM), jnp.float32),
    )
    carry = absorb(start_carry, query_h, keys_h, values_h, allowed_pairs(query_side, own_keys))

    def forward_hop(hop, state):
        pieces, inner = state
        pieces = from_behind((pieces[0], pieces[1]), "seq", 1)
        source = me_index - hop
        inner = absorb(
            inner, query_h, pieces[0], pieces[1], allowed_pairs(query_side, key_side(source))
        )
        return (pieces, inner)

    _, (run_max, run_sum, totals) = lax.fori_loop(
        1, hops + 1, forward_hop, ((keys_h, values_h), carry)
    )
    live = own_layout[2][:, None, :]
    safe_sum = jnp.where(live, run_sum, 1.0)
    attended_h = jnp.where(live[..., None], totals / safe_sum[..., None], 0.0)
    lse = jnp.where(live, run_max + jnp.log(safe_sum), 0.0)
    attended32 = attended_h.transpose(0, 2, 1, 3).reshape(tokens, width)
    attended = attended32.astype(jnp.bfloat16)
    branch_attn = dense(attended, full_out)
    hidden = gate_attn * branch_attn + (1.0 - gate_attn) * inputs
    normed_ffn, pull_ffn = jax.vjp(rms_norm, hidden, gain_ffn.astype(jnp.float32))
    normed_ffn_low = normed_ffn.astype(jnp.bfloat16)
    pre = dense(normed_ffn_low, full_in)
    act32, pull_gelu = jax.vjp(partial(jax.nn.gelu, approximate=True), pre)
    act = act32.astype(jnp.bfloat16)
    branch_ffn = dense(act, full_back)
    gate_ffn = jax.nn.sigmoid(dense(normed_ffn_low, full_gate_ffn) + shift_ffn.astype(jnp.float32))
    output = gate_ffn * branch_ffn + (1.0 - gate_ffn) * hidden
    again = (
        lax.all_gather(w_query, ("dp", "seq"), axis=0, tiled=True),
        lax.all_gather(w_key, ("dp", "seq"), axis=0, tiled=True),
        lax.all_gather(w_value, ("dp", "seq"), axis=0, tiled=True),
        lax.all_gather(w_out, ("dp", "seq"), axis=0, tiled=True),
        lax.all_gather(w_gate_attn, ("dp", "seq"), axis=0, tiled=True),
        lax.all_gather(w_gate_ffn, ("dp", "seq"), axis=0, tiled=True),
        lax.all_gather(w_in, ("dp", "seq"), axis=0, tiled=True),
        lax.all_gather(w_back, ("dp", "seq"), axis=0, tiled=True),
        lax.all_gather(norm_attn, ("dp", "seq"), axis=0, tiled=True),
        lax.all_gather(norm_ffn, ("dp", "seq"), axis=0, tiled=True),
        lax.all_gather(bias_attn, ("dp", "seq"), axis=0, tiled=True),
        lax.all_gather(bias_ffn, ("dp", "seq"), axis=0, tiled=True),
    )
    (
        back_query,
        back_key,
        back_value,
        back_out,
        back_gate_attn,
        back_gate_ffn,
        back_in,
        back_back,
        _,
        _,
        _,
        _,
    ) = again
    upstream = cotangent[:, 0].reshape(tokens, width).astype(jnp.float32)
    d_logit_ffn = (upstream * (branch_ffn - hidden) * gate_ffn * (1.0 - gate_ffn)).astype(
        jnp.bfloat16
    )
    d_branch_ffn = (upstream * gate_ffn).astype(jnp.bfloat16)
    grad_back = dense_tn(act, d_branch_ffn)
    (d_pre32,) = pull_gelu(dense_nt(d_branch_ffn, back_back))
    d_pre = d_pre32.astype(jnp.bfloat16)
    grad_in = dense_tn(normed_ffn_low, d_pre)
    grad_gate_ffn = dense_tn(normed_ffn_low, d_logit_ffn)
    grad_bias_ffn = jnp.sum(d_logit_ffn.astype(jnp.float32), axis=0)
    d_normed_ffn = dense_nt(d_pre, back_in) + dense_nt(d_logit_ffn, back_gate_ffn)
    d_hidden_norm, grad_gain_ffn = pull_ffn(d_normed_ffn)
    d_hidden = upstream * (1.0 - gate_ffn) + d_hidden_norm
    d_branch_attn = (d_hidden * gate_attn).astype(jnp.bfloat16)
    d_logit_attn = (d_hidden * (branch_attn - inputs) * gate_attn * (1.0 - gate_attn)).astype(
        jnp.bfloat16
    )
    grad_out = dense_tn(attended, d_branch_attn)
    d_attended = dense_nt(d_branch_attn, back_out).astype(jnp.bfloat16)
    grad_att = d_attended.reshape(head_shape)
    delta = jnp.einsum(
        "mqhd,mqhd->mhq", grad_att.astype(jnp.float32), attended32.reshape(head_shape)
    )
    first_q, first_k, first_v = hop_grads(
        query_h, grad_att, lse, delta, keys_h, values_h, allowed_pairs(query_side, own_keys)
    )

    def backward_hop(hop, state):
        pieces, moving, grad_q = state
        pieces = from_behind((pieces[0], pieces[1]), "seq", 1)
        moving = (
            passed_along(moving[0].astype(jnp.bfloat16), "seq", 1).astype(jnp.float32),
            passed_along(moving[1].astype(jnp.bfloat16), "seq", 1).astype(jnp.float32),
        )
        source = me_index - hop
        step_q, step_k, step_v = hop_grads(
            query_h,
            grad_att,
            lse,
            delta,
            pieces[0],
            pieces[1],
            allowed_pairs(query_side, key_side(source)),
        )
        return (pieces, (moving[0] + step_k, moving[1] + step_v), grad_q + step_q)

    _, moving, grad_q = lax.fori_loop(
        1, hops + 1, backward_hop, ((keys_h, values_h), (first_k, first_v), first_q)
    )
    moving = (
        passed_along(moving[0].astype(jnp.bfloat16), "seq", -hops).astype(jnp.float32),
        passed_along(moving[1].astype(jnp.bfloat16), "seq", -hops).astype(jnp.float32),
    )
    grad_k, grad_v = moving
    d_query = grad_q.reshape(tokens, width).astype(jnp.bfloat16)
    d_key = grad_k.reshape(tokens, width).astype(jnp.bfloat16)
    d_value = grad_v.reshape(tokens, width).astype(jnp.bfloat16)
    grad_query = dense_tn(normed_low, d_query)
    grad_key = dense_tn(normed_low, d_key)
    grad_value = dense_tn(normed_low, d_value)
    grad_gate_attn = dense_tn(normed_low, d_logit_attn)
    grad_bias_attn = jnp.sum(d_logit_attn.astype(jnp.float32), axis=0)
    d_normed_attn = (
        dense_nt(d_query, back_query)
        + dense_nt(d_key, back_key)
        + dense_nt(d_value, back_value)
        + dense_nt(d_logit_attn, back_gate_attn)
    )
    d_inputs_norm, grad_gain_attn = pull_attn(d_normed_attn)
    grad_input = d_hidden * (1.0 - gate_attn) + d_inputs_norm
    owned = (
        lax.psum_scatter(grad_query, ("dp", "seq"), scatter_dimension=0, tiled=True),
        lax.psum_scatter(grad_key, ("dp", "seq"), scatter_dimension=0, tiled=True),
        lax.psum_scatter(grad_value, ("dp", "seq"), scatter_dimension=0, tiled=True),
        lax.psum_scatter(grad_out, ("dp", "seq"), scatter_dimension=0, tiled=True),
        lax.psum_scatter(grad_gate_attn, ("dp", "seq"), scatter_dimension=0, tiled=True),
        lax.psum_scatter(grad_gate_ffn, ("dp", "seq"), scatter_dimension=0, tiled=True),
        lax.psum_scatter(grad_in, ("dp", "seq"), scatter_dimension=0, tiled=True),
        lax.psum_scatter(grad_back, ("dp", "seq"), scatter_dimension=0, tiled=True),
        lax.psum_scatter(grad_gain_attn, ("dp", "seq"), scatter_dimension=0, tiled=True),
        lax.psum_scatter(grad_gain_ffn, ("dp", "seq"), scatter_dimension=0, tiled=True),
        lax.psum_scatter(grad_bias_attn, ("dp", "seq"), scatter_dimension=0, tiled=True),
        lax.psum_scatter(grad_bias_ffn, ("dp", "seq"), scatter_dimension=0, tiled=True),
    )
    return (
        output.reshape(micro, 1, rows, width).astype(jnp.bfloat16),
        grad_input.reshape(micro, 1, rows, width),
        owned[0],
        owned[1],
        owned[2],
        owned[3],
        owned[4],
        owned[5],
        owned[6],
        owned[7],
        owned[8],
        owned[9],
        owned[10],
        owned[11],
    )


def solution(mesh):
    placed = (
        P(None, "dp", "seq", None),
        P(None, "dp", "seq", None),
        P(None, "dp", None),
        P(None, "dp", None),
        P(("dp", "seq"), None),
        P(("dp", "seq"), None),
        P(("dp", "seq"), None),
        P(("dp", "seq"), None),
        P(("dp", "seq"), None),
        P(("dp", "seq"), None),
        P(("dp", "seq"), None),
        P(("dp", "seq"), None),
        P(("dp", "seq")),
        P(("dp", "seq")),
        P(("dp", "seq")),
        P(("dp", "seq")),
    )
    def pick(layer_input, *others):
        micro, _, rows, width = layer_input.shape
        fits = (
            dict(mesh.shape) == {"dp": 4, "seq": 8}
            and micro == 2
            and others[1].shape[2] == 1
            and width == HEADS * HEAD_DIM
            and width == 4 * LANES
            and rows % 128 == 0
            and others[10].shape == (width // 8, width)
        )
        return (by_heads if fits else shards)(layer_input, *others)

    return jax.shard_map(
        pick,
        mesh=mesh,
        in_specs=placed,
        out_specs=(
            P(None, "dp", "seq", None),
            P(None, "dp", "seq", None),
            P(("dp", "seq"), None),
            P(("dp", "seq"), None),
            P(("dp", "seq"), None),
            P(("dp", "seq"), None),
            P(("dp", "seq"), None),
            P(("dp", "seq"), None),
            P(("dp", "seq"), None),
            P(("dp", "seq"), None),
            P(("dp", "seq")),
            P(("dp", "seq")),
            P(("dp", "seq")),
            P(("dp", "seq")),
        ),
        check_vma=False,
    )
```

```python
from functools import partial

import jax
import jax.numpy as jnp
from jax import lax
from jax.experimental import pallas as pl
from jax.experimental.pallas import tpu as pltpu
from jax.sharding import PartitionSpec as P

HEADS = 8
HEAD_DIM = 64
DOC_MAX = 4096

EPS = 1e-05
MESH = pl.DeviceIdType.MESH
BF = jnp.bfloat16
F32 = jnp.float32
VMEM_LIMIT = 66_000_000
LANES = 128
SIDE = 64
GELU_C = 0.7978845608028654
GELU_A = 0.044715
NEG = -1e30
ANY = pl.BlockSpec(memory_space=pl.ANY)
INVM = pl.BlockSpec(memory_space=pltpu.VMEM)
INSM = pl.BlockSpec(memory_space=pltpu.SMEM)


def nn(a, b):
    return lax.dot_general(a, b, (((1,), (0,)), ((), ())), preferred_element_type=F32)


def nt(a, b):
    return lax.dot_general(a, b, (((1,), (1,)), ((), ())), preferred_element_type=F32)


def tn(a, b):
    return lax.dot_general(a, b, (((0,), (0,)), ((), ())), preferred_element_type=F32)


def remote(src, dst, send, recv, dp, seq):
    return pltpu.make_async_remote_copy(
        src_ref=src, dst_ref=dst, send_sem=send, recv_sem=recv,
        device_id=(dp, seq), device_id_type=MESH,
    )


def greet(peers):
    barrier = pltpu.get_barrier_semaphore()
    for dp, seq in peers:
        pl.semaphore_signal(barrier, inc=1, device_id=(dp, seq), device_id_type=MESH)
    pl.semaphore_wait(barrier, len(peers))


def place():
    d = lax.axis_index("dp")
    j = lax.axis_index("seq")
    z = j // 2
    c = j % 2
    dx = d + 1 - 2 * (d % 2)
    dy = (d + 2) % 4
    dxy = 3 - d
    return d, j, z, c, dx, dy, dxy


CK = 4


class Spread:
    def __init__(self, dst, send, recv):
        self.dst, self.send, self.recv = dst, send, recv
        self.at = place()
        self.count = 0
        self.sent = []
        d, j, z, c, dx, dy, dxy = self.at
        self.pj = j + 1 - 2 * c
        self.lines = (z, z + 1 - 2 * (z % 2), (z + 2) % 4, 3 - z)
        self.slots = {
            dp: [where * 8 + 2 * zz + c for zz in self.lines]
            for dp, where in (("d", d), ("x", dx), ("y", dy), ("xy", dxy))
        }

    def make(self, slot, i, dp, seq, src=None):
        return remote(
            self.dst.at[slot] if src is None else src, self.dst.at[slot],
            self.send.at[i], self.recv.at[slot], dp, seq,
        )

    def put(self, slot, dp, seq, src=None):
        i = self.count
        self.count += 1
        self.make(slot, i, dp, seq, src).start()
        self.sent.append((slot, i))

    def arrive(self, slot):
        self.make(slot, 0, self.at[0], self.pj).wait_recv()

    def in_plane(self, src):
        d, j, z, c, dx, dy, dxy = self.at
        for dp, seq in ((dx, j), (dy, j), (d, self.pj)):
            self.put(self.slots["d"][0], dp, seq, src)

    def along(self, srcs):
        d, j, z, c, dx, dy, dxy = self.at
        for zz, src in zip(self.lines[1:], srcs):
            self.put(self.slots["d"][0], d, 2 * zz + c, src)

    def from_line(self, k):
        d, j, z, c, dx, dy, dxy = self.at
        slot = self.slots["d"][k]
        self.arrive(slot)
        for dp, seq in ((dx, j), (dy, j), (d, self.pj)):
            self.put(slot, dp, seq)

    def from_plane(self, k):
        d, j, z, c, dx, dy, dxy = self.at
        sx, sy = self.slots["x"][k], self.slots["y"][k]
        for slot in (sx, sy):
            self.arrive(slot)
            self.put(slot, d, self.pj)
        even = self.lines[k] % 2 == 0
        i = self.count
        self.count += 1
        self.sent.append((sx, i))

        @pl.when(even)
        def _():
            self.make(sx, i, dy, j).start()

        @pl.when(jnp.logical_not(even))
        def _():
            self.make(sy, i, dx, j).start()

    def from_corner(self):
        for slot in self.slots["xy"]:
            self.arrive(slot)
            self.put(slot, self.at[0], self.pj)

    def from_core(self):
        c = self.at[3]
        for slots in self.slots.values():
            for slot in slots:
                self.arrive(slot + 1 - 2 * c)

    def wait_sent(self):
        for slot, i in self.sent:
            self.make(slot, i, self.at[0], self.pj).wait_send()


LOG2E = 1.4426950408889634


def lane_of(rows):
    return lax.broadcasted_iota(jnp.int32, (rows, LANES), 1)


def three(v):
    a = v.astype(BF).astype(F32)
    b = (v - a).astype(BF).astype(F32)
    return a, b, v - a - b


def beside(h, lane, values, parts):
    first = SIDE * (1 - h)
    own = (lane < SIDE) if h == 0 else (lane >= SIDE)
    out = jnp.where(own, values, 0.0)
    for k, part in enumerate(parts):
        if part is not None:
            out = jnp.where(lane == first + k, part, out)
    return out.astype(BF)


def upper(rows):
    return lax.broadcasted_iota(jnp.int32, (rows, rows), 0) <= lax.broadcasted_iota(
        jnp.int32, (rows, rows), 1
    )


def front_kernel(
    doc_len, doc_off, x_ref, wq, wk, wv, wo, wga, wgf, win, wback, small_ref,
    xg, wg, w_ref, vec_ref, att, o32_ref, qa, ka, va,
    hv, hg, sv, vt, top, acc, ov,
    lsem, xsem, hsend, hrecv, wsend, wrecv, xsend, xrecv, ssend, srecv,
):
    blocks, rows, width = xg.shape
    per = wq.shape[0]
    half = width // 2
    d, j, z, c, dx, dy, dxy = place()
    me = d * 8 + j
    g = z // 2
    pj = j + 1 - 2 * c
    za, zb, zc = z + 1 - 2 * (z % 2), (z + 2) % 4, 3 - z
    ja = 2 * za + c
    near = jnp.logical_or(z == 1, z == 2)
    far = jnp.logical_or(z == 0, z == 3)
    loads = []
    pieces = [(m, hv.at[k * per : (k + 1) * per]) for k, m in enumerate((wq, wk, wv))]
    pieces += [(m, sv.at[k * per : (k + 1) * per]) for k, m in enumerate((wo, wga, wgf))]
    ff = win.shape[1] // width
    for k in range(ff):
        pieces.append((win.at[:, k * width : (k + 1) * width], sv.at[(3 + k) * per : (4 + k) * per]))
    pieces.append((wback, sv.at[(3 + ff) * per :]))
    for k, (src, dst) in enumerate(pieces):
        loads.append(pltpu.make_async_copy(src, dst, lsem.at[k]))
        loads[-1].start()
    own = pltpu.make_async_copy(x_ref.at[g], xg.at[j], xsem)
    own.start()
    lanes = lax.broadcasted_iota(jnp.int32, (LANES, half), 1)
    subs = lax.broadcasted_iota(jnp.int32, (LANES, half), 0)
    spots = [
        nn(small_ref[...], jnp.where(lanes + k * half == me * per + subs, 1.0, 0.0).astype(BF)) for k in range(2)
    ]
    row = lax.broadcasted_iota(jnp.int32, (16, half), 0)
    tile = jnp.where(row < 4, spots[0], spots[1]).astype(BF)
    hv[3 * per :, :half] = tile
    hv[3 * per :, half:] = tile
    for k in range(3):
        loads[k].wait()
    greet([(d, (j + k) % 8) for k in range(1, 8)] + [(dx, j), (dy, j)])

    heads = Spread(hg, hsend, hrecv)
    weights = Spread(wg, wsend, wrecv)

    def side(zz):
        return hv.at[:, pl.ds(pl.multiple_of(half * (zz % 2), half), half)]

    heads.along([side(zz) for zz in (za, zb, zc)])
    heads.in_plane(side(z))

    def xcopy(k, part, block, dp, seq, src=None):
        piece = pl.ds(part * (rows // CK), rows // CK)
        source = xg.at[block, piece] if src is None else x_ref.at[src, piece]
        return remote(source, xg.at[block, piece], xsend.at[k, part], xrecv.at[block, part], dp, seq)

    def xarrive(block):
        for part in range(CK):
            xcopy(0, part, block, d, pj).wait_recv()

    jn = 2 * (2 - g) + c
    for part in range(CK):
        xcopy(0, part, j, d, ja, g).start()
        xcopy(1, part, j, d, pj, g).start()
    for part in range(CK):
        xcopy(2, part, j, d, jn, 1 - g).start()
    hg[me] = jnp.where(z % 2 == 0, hv[:, :half], hv[:, half:])
    for copy in loads[3:]:
        copy.wait()
    keep = pltpu.make_async_copy(sv, wg.at[me], lsem.at[0])
    keep.start()
    weights.in_plane(sv)

    heads.from_line(1)
    heads.from_plane(0)
    heads.from_line(2)
    heads.from_plane(1)
    heads.from_line(3)
    heads.from_plane(2)
    heads.from_plane(3)
    heads.from_corner()
    heads.from_core()

    vecs = jnp.zeros((16, half), F32)
    for k in range(32):
        vecs += hg[k, 3 * per :].astype(F32)
    for k in range(2):
        vec_ref[:, k * half : (k + 1) * half] = vecs[4 * k : 4 * k + 4]
    for k in range(3):
        both = hg[:, k * per : (k + 1) * per, :]
        picked = jnp.where(c == 0, both[:, :, :LANES], both[:, :, LANES:])
        w_ref[:, k * LANES : (k + 1) * LANES] = picked.reshape(width, LANES)

    off = doc_off[g, 0, 0]
    end = off + doc_len[g, 0, 0]
    lane = lane_of(rows)
    up = lax.broadcasted_iota(jnp.int32, (rows, 1), 0)
    along = lax.broadcasted_iota(jnp.int32, (1, rows), 1)
    tall = lax.broadcasted_iota(jnp.int32, (16, rows), 0)
    ones = jnp.where(tall == 0, 1.0, 0.0).astype(BF)

    def project(b):
        x = xg[b].astype(F32)
        n = (x * lax.rsqrt(jnp.mean(x * x, -1, keepdims=True) + EPS) * vec_ref[0:1]).astype(BF)
        p = nn(n, w_ref[...])
        pos = b * rows + up
        bad = jnp.where(jnp.logical_and(pos >= off, pos < end), 0.0, NEG)
        q = p[:, :LANES] * (HEAD_DIM ** (-0.5) * LOG2E)
        k = p[:, LANES : 2 * LANES]
        v = p[:, 2 * LANES :]
        for h in range(2):
            qa[h, b] = beside(h, lane, q, (1.0,))
            ka[h, b] = beside(h, lane, k, (bad, 1.0, 1.0, 1.0))
            va[h, b] = beside(h, lane, v, (None, 1.0, 1.0, 1.0))
        turned = v.astype(BF).T
        for h in range(2):
            vt[h, b, :SIDE] = turned[h * SIDE : (h + 1) * SIDE]
            vt[h, b, SIDE:] = ones

    def project_two(base):
        def body(k, _):
            project(base + k)
            return 0

        lax.fori_loop(0, 2, body, 0)

    z1 = 2 - g
    z2 = 3 * (1 - g)
    b1, b2 = 2 * z1 + c, 2 * z2 + c
    own.wait()
    xarrive(pj)
    project_two(2 * z)
    for part in range(CK):
        xcopy(0, part, ja, d, pj).wait_recv()
        xcopy(3, part, ja, d, pj).start()

        @pl.when(near)
        def _():
            xcopy(0, part, b1, d, pj).wait_recv()
            xcopy(6, part, b1, d, ja).start()
            xcopy(4, part, b1, d, pj).start()

    xarrive(ja + 1 - 2 * c)
    project_two(2 * za)

    keep_low = upper(rows)
    sub = lax.broadcasted_iota(jnp.int32, (SIDE, rows), 0)

    def scores(q, k):
        return [nt(ka[h, k], qa[h, q]) for h in range(2)]

    def first(q):
        ss = [jnp.where(keep_low, s, NEG) for s in scores(q, q)]
        new = [jnp.max(s, 0, keepdims=True) for s in ss]
        ps = [jnp.exp2(s - n).astype(BF) for s, n in zip(ss, new)]
        for h in range(2):
            top[h, q] = new[h]
            acc[h, q] = nn(vt[h, q], ps[h])

    def pair(q, k):
        ss = scores(q, k)
        old = [top[h, q] for h in range(2)]
        new = [jnp.maximum(old[h], jnp.max(ss[h], 0, keepdims=True)) for h in range(2)]
        ps = [jnp.exp2(ss[h] - new[h]).astype(BF) for h in range(2)]
        for h in range(2):
            top[h, q] = new[h]
            acc[h, q] = acc[h, q] * jnp.exp2(old[h] - new[h]) + nn(vt[h, k], ps[h])

    def acopy(q):
        return remote(ov.at[q], att.at[j], ssend.at[q], srecv.at[j], d, q)

    def finish(b):
        pos = b * rows + along
        live = jnp.logical_and(pos >= off, pos < end)
        outs = []
        for h in range(2):
            total = acc[h, b, SIDE : SIDE + 1]
            lse = jnp.where(live, top[h, b] + jnp.log2(total), -NEG)
            mine = jnp.where(live, acc[h, b, :SIDE] / total, 0.0)
            parts = three(lse)
            beyond = jnp.zeros((SIDE, rows), F32)
            for k in range(3):
                beyond = jnp.where(sub == k + 1, -parts[k], beyond)
            both = (mine, beyond) if h == 0 else (beyond, mine)
            out = jnp.concatenate(both, axis=0).T
            start = SIDE * (1 - h)
            aug = jnp.logical_and(lane > start, lane < start + 4)
            qa[h, b] = jnp.where(aug, out, qa[h, b].astype(F32)).astype(BF)
            outs.append(out)
        out = jnp.where(lane < SIDE, outs[0], outs[1])
        o32_ref[b] = out
        ov[b] = out.astype(BF)

        @pl.when(b != j)
        def _():
            acopy(b).start()

    def outer(i, _):
        @pl.when(i == 4)
        def _():
            @pl.when(near)
            def _():
                for part in range(CK):
                    xcopy(0, part, b2, d, pj).wait_recv()
                    xcopy(7, part, b2, d, ja).start()
                    xcopy(5, part, b2, d, pj).start()

            @pl.when(far)
            def _():
                for part in range(CK):
                    xcopy(0, part, b1, d, pj).wait_recv()
                    xcopy(4, part, b1, d, pj).start()

            weights.along([sv] * 3)
            weights.from_plane(0)
            xarrive(b1 + 1 - 2 * c)

        @pl.when(i == 6)
        def _():
            @pl.when(far)
            def _():
                for part in range(CK):
                    xcopy(0, part, b2, d, pj).wait_recv()
                    xcopy(5, part, b2, d, pj).start()

            xarrive(b2 + 1 - 2 * c)

        @pl.when(jnp.logical_or(i == 4, i == 6))
        def _():
            project_two(2 * (z1 + (z2 - z1) * ((i - 4) // 2)))

        o = (1 - g) * i + g * (blocks - 1 - i)
        first(o)
        last = jnp.logical_and(g == 1, i == blocks - 1)
        pl.when(last)(lambda: finish(o))

        def inner(t, _):
            q = (1 - g) * o + g * (o + 1 + t)
            pair(q, (1 - g) * (o - 1 - t) + g * o)
            pl.when(jnp.logical_or(last, jnp.logical_and(g == 0, t == i - 1)))(lambda: finish(q))

            @pl.when(jnp.logical_and(i == blocks - 1, t == 3))
            def _():
                for k in range(1, 4):
                    weights.from_line(k)

            return 0

        lax.fori_loop(0, i, inner, 0)
        pl.when(jnp.logical_and(g == 0, i == 0))(lambda: finish(o))
        return 0

    lax.fori_loop(0, blocks, outer, 0)
    att[j] = ov[j]
    for k in range(1, 4):
        weights.from_plane(k)
    weights.from_corner()
    weights.from_core()
    for k in range(1, 8):
        q = (j + k) % 8
        remote(ov.at[q], att.at[q], ssend.at[q], srecv.at[q], d, q).wait_recv()
    heads.wait_sent()
    weights.wait_sent()
    for k in range(6):
        for part in range(CK):
            xcopy(k, part, j, d, pj).wait_send()

    @pl.when(near)
    def _():
        for k in (6, 7):
            for part in range(CK):
                xcopy(k, part, j, d, pj).wait_send()

    for k in range(1, 8):
        acopy((j + k) % 8).wait_send()
    keep.wait()


def front(doc_len, doc_off, x, mats, small):
    _, rows, width = x.shape
    per = mats[0].shape[0]
    blocks = 8
    tall = sum(m.shape[0] * (m.shape[1] // width) for m in mats[3:])
    side = jax.ShapeDtypeStruct((2, blocks, rows, LANES), BF)
    dma = pltpu.SemaphoreType.DMA
    return pl.pallas_call(
        front_kernel,
        out_shape=(
            jax.ShapeDtypeStruct((blocks, rows, width), BF),
            jax.ShapeDtypeStruct((32, tall, width), BF),
            jax.ShapeDtypeStruct((width, 3 * LANES), BF),
            jax.ShapeDtypeStruct((4, width), F32),
            jax.ShapeDtypeStruct((blocks, rows, LANES), BF),
            jax.ShapeDtypeStruct((blocks, rows, LANES), F32),
            side, side, side,
        ),
        in_specs=[INSM, INSM] + [ANY] * 9 + [INVM],
        out_specs=(INVM, ANY) + (INVM,) * 7,
        scratch_shapes=[
            pltpu.VMEM((3 * per + 16, width), BF),
            pltpu.VMEM((32, 3 * per + 16, width // 2), BF),
            pltpu.VMEM((tall, width), BF),
            pltpu.VMEM((2, blocks, SIDE + 16, rows), BF),
            pltpu.VMEM((2, blocks, 1, rows), F32),
            pltpu.VMEM((2, blocks, SIDE + 16, rows), F32),
            pltpu.VMEM((blocks, rows, LANES), BF),
            dma((12,)), dma, dma((32,)), dma((32,)), dma((32,)), dma((32,)),
            dma((8, CK)), dma((8, CK)), dma((8,)), dma((8,)),
        ],
        compiler_params=pltpu.CompilerParams(
            collective_id=0, has_side_effects=True, vmem_limit_bytes=VMEM_LIMIT
        ),
        name="front",
    )(doc_len, doc_off, x, *mats, small)


def swap_kernel(a_ref, b_ref, av, lsem, send, recv):
    d = lax.axis_index("dp")
    j = lax.axis_index("seq")
    load = pltpu.make_async_copy(a_ref.at[j], av, lsem)
    load.start()
    peers = [(d, (j + k) % 8) for k in range(1, 8)]
    greet(peers)
    copies = []
    for k, (dp, seq) in enumerate(peers):
        copy = remote(a_ref.at[seq], b_ref.at[j], send.at[k], recv.at[k], dp, seq)
        copy.start()
        copies.append(copy)
    load.wait()
    keep = pltpu.make_async_copy(av, b_ref.at[j], lsem)
    keep.start()
    for copy in copies:
        copy.wait()
    keep.wait()


def swap(a, cid):
    return pl.pallas_call(
        swap_kernel,
        out_shape=jax.ShapeDtypeStruct(a.shape, a.dtype),
        in_specs=[ANY],
        out_specs=ANY,
        scratch_shapes=[
            pltpu.VMEM(a.shape[1:], a.dtype),
            pltpu.SemaphoreType.DMA,
            pltpu.SemaphoreType.DMA((7,)),
            pltpu.SemaphoreType.DMA((7,)),
        ],
        compiler_params=pltpu.CompilerParams(collective_id=cid, has_side_effects=True),
    )(a)


def token_kernel(
    x_ref, c_ref, a_ref, wg, vec, out_ref, da_ref, dh_ref, dn_ref, g_ref, v_ref,
    gp, act, g_out, g_ga, g_gf, g_in, g_back,
):
    step = pl.program_id(0)
    rows, width = x_ref.shape[1:]
    ff = gp.shape[0]
    per = width // 32

    def weight(lo):
        return wg[:, lo : lo + per, :].reshape(width, width)

    def back(k):
        n = wg.shape[0] // ff
        return wg[k * n : (k + 1) * n, 7 * per : 7 * per + ff * per, :].reshape(width, width)

    @pl.when(step == 0)
    def _():
        for ref in (g_out, g_ga, g_gf, g_in, g_back, v_ref):
            ref[...] = jnp.zeros_like(ref)

    x = x_ref[0].astype(F32)
    gain_a, gain_f = vec[0:1].astype(F32), vec[1:2].astype(F32)
    shift_a, shift_f = vec[2:3].astype(F32), vec[3:4].astype(F32)
    n1 = x * lax.rsqrt(jnp.mean(x * x, -1, keepdims=True) + EPS)
    na = (n1 * gain_a).astype(BF)
    ga = jax.nn.sigmoid(nn(na, weight(per)) + shift_a)
    att = jnp.concatenate([a_ref[i] for i in range(4)], axis=1)
    br = nn(att, weight(0))
    hid = ga * br + (1.0 - ga) * x
    r2 = lax.rsqrt(jnp.mean(hid * hid, -1, keepdims=True) + EPS)
    n2 = hid * r2
    nf = (n2 * gain_f).astype(BF)
    bf = jnp.zeros((rows, width), F32)
    for k in range(ff):
        pre = nn(nf, weight((3 + k) * per))
        sq = pre * pre
        t = jnp.tanh(GELU_C * pre * (1.0 + GELU_A * sq))
        half = 0.5 * (1.0 + t)
        act[k] = (pre * half).astype(BF)
        gp[k] = half + 0.5 * pre * (1.0 - t * t) * (GELU_C * (1.0 + 3.0 * GELU_A * sq))
        bf += nn(act[k], back(k))
    gf = jax.nn.sigmoid(nn(nf, weight(2 * per)) + shift_f)
    out_ref[0] = (gf * bf + (1.0 - gf) * hid).astype(BF)
    c = c_ref[0].astype(F32)
    dlf = (c * (bf - hid) * gf * (1.0 - gf)).astype(BF)
    dbf = (c * gf).astype(BF)
    dnf = nt(dlf, weight(2 * per))
    g_gf[...] += tn(nf, dlf)
    for k in range(ff):
        dpre = (nt(dbf, back(k)) * gp[k]).astype(BF)
        g_back[k] += tn(act[k], dbf)
        g_in[k] += tn(nf, dpre)
        dnf += nt(dpre, weight((3 + k) * per))
    g2 = dnf * gain_f
    dh = c * (1.0 - gf) + r2 * (g2 - n2 * jnp.mean(g2 * n2, -1, keepdims=True))
    dba = (dh * ga).astype(BF)
    dla = (dh * (br - x) * ga * (1.0 - ga)).astype(BF)
    g_out[...] += tn(att, dba)
    g_ga[...] += tn(na, dla)
    datt = nt(dba, weight(0)).astype(BF)
    for i in range(4):
        da_ref[i] = datt[:, i * LANES : (i + 1) * LANES]
    dna = nt(dla, weight(per))
    dh_ref[0] = dh * (1.0 - ga)
    dn_ref[0] = dna
    v_ref[0:1] += jnp.sum(dna * n1, 0, keepdims=True)
    v_ref[1:2] += jnp.sum(dnf * n2, 0, keepdims=True)
    v_ref[2:3] += jnp.sum(dla.astype(F32), 0, keepdims=True)
    v_ref[3:4] += jnp.sum(dlf.astype(F32), 0, keepdims=True)

    @pl.when(step == pl.num_programs(0) - 1)
    def _():
        def put(lo, value):
            g_ref[:, lo : lo + per, :] = value.astype(BF).reshape(32, per, width)

        put(0, g_out[...])
        put(per, g_ga[...])
        put(2 * per, g_gf[...])
        for k in range(ff):
            put((3 + k) * per, g_in[k])
            n = 32 // ff
            g_ref[k * n : (k + 1) * n, (3 + ff) * per :, :] = (
                g_back[k].astype(BF).reshape(n, ff * per, width)
            )


def tokens(x, cot, att, wg, vec):
    micro, rows, width = x.shape
    ff = 4
    per = width // 32
    tok = pl.BlockSpec((1, rows, width), lambda i: (i, 0, 0))
    head = pl.BlockSpec((4, rows, LANES), lambda i: (i, 0, 0))

    def whole(shape):
        return pl.BlockSpec(shape, lambda i: (0,) * len(shape), pipeline_mode=pl.Buffered(1))

    grads = (32, (3 + 2 * ff) * per, width)
    return pl.pallas_call(
        token_kernel,
        grid=(micro,),
        out_shape=(
            jax.ShapeDtypeStruct((micro, rows, width), BF),
            jax.ShapeDtypeStruct((4 * micro, rows, LANES), BF),
            jax.ShapeDtypeStruct((micro, rows, width), F32),
            jax.ShapeDtypeStruct((micro, rows, width), F32),
            jax.ShapeDtypeStruct(grads, BF),
            jax.ShapeDtypeStruct((8, width), F32),
        ),
        in_specs=[tok, tok, head, whole(wg.shape), whole(vec.shape)],
        out_specs=(tok, head, tok, tok, whole(grads), whole((8, width))),
        scratch_shapes=[
            pltpu.VMEM((ff, rows, width), F32),
            pltpu.VMEM((ff, rows, width), BF),
            pltpu.VMEM((width, width), F32),
            pltpu.VMEM((width, width), F32),
            pltpu.VMEM((width, width), F32),
            pltpu.VMEM((ff, width, width), F32),
            pltpu.VMEM((ff, width, width), F32),
        ],
        compiler_params=pltpu.CompilerParams(vmem_limit_bytes=VMEM_LIMIT),
    )(x, cot, att, wg, vec)


def add_into(dst, src):
    rows = dst.shape[0]
    n = rows // 16
    per = 16 * max(k for k in range(1, 9) if n % k == 0)

    def body(i, _):
        piece = pl.ds(i * per, per)
        dst[piece, :] = (dst[piece, :].astype(F32) + src[piece, :].astype(F32)).astype(BF)
        return 0

    lax.fori_loop(0, rows // per, body, 0)


def attend_back_kernel(
    x_ref, w_ref, gain_ref, o32_ref, do_ref, qa, ka, va, sum_ref, g_ref,
    dn_ref, gf_ref, gq_ref, gv_ref,
    da, qt, kt, dot, dq, dk, dv, dw, pb, hs_buf, vs_buf,
    acc, b1, b2, b3, b4, q1, q2, hb, vb, own,
    l2, lo, s1, r1, s2, r2, s3, r3, s4, r4, ps, pr, ts, tr, us, ur, hs, hr, vs, vr,
):
    blocks, rows, width = x_ref.shape
    per = width // 32
    d, j, z, c, dx, dy, dxy = place()
    me = d * 8 + j
    g = z // 2
    pj = j + 1 - 2 * c
    za, zb, zc = z + 1 - 2 * (z % 2), (z + 2) % 4, 3 - z
    ja, jb, jc = 2 * za + c, 2 * zb + c, 2 * zc + c
    near = jnp.logical_or(z == 1, z == 2)
    far = jnp.logical_or(z == 0, z == 3)
    w3, w2, wn, wf = 3 * (1 - g), 2 - g, 1 + g, 3 * g
    first = [(zz, dp) for zz in range(4) for dp in ((dx, dxy) if zz % 2 == 0 else (dy, dxy))]
    rest = [(zz, dp) for zz in range(4) for dp in ((d, dy) if zz % 2 == 0 else (d, dx))]

    gloads = []
    for k, (zz, dp) in enumerate(first + rest):
        copy = pltpu.make_async_copy(g_ref.at[dp * 8 + 2 * zz + c], acc.at[dp * 4 + zz], l2.at[k])
        copy.start()
        gloads.append(copy)

    barrier = pltpu.get_barrier_semaphore()

    def hello(k, _):
        slot = (me + k) % 32
        pl.semaphore_signal(
            barrier, inc=1, device_id=(slot // 8, slot % 8), device_id_type=MESH
        )
        return 0

    lax.fori_loop(1, 32, hello, 0)
    pl.semaphore_wait(barrier, 31)

    def gcopy(zz, dp):
        i = dp * 4 + zz
        return remote(g_ref.at[dp * 8 + 2 * zz + 1 - c], b1.at[i], s1.at[i], r1.at[i], d, pj)

    def stage2(zz, dp):
        i = dp * 4 + zz
        to = dx if zz % 2 == 0 else dy
        return remote(acc.at[i], b2.at[i], s2.at[i], r2.at[i], to, j)

    def stage3(zz):
        to = dy if zz % 2 == 0 else dx
        return remote(acc.at[to * 4 + zz], b3.at[zz], s3.at[zz], r3.at[zz], to, j)

    def stage4(k, zz, jz):
        return remote(acc.at[d * 4 + zz], b4.at[z], s4.at[k], r4.at[z], d, jz)

    def pcopy(zz):
        return remote(pb.at[2 * zz + 1 - c], q1.at[zz], ps.at[zz], pr.at[zz], d, pj)

    def tcopy(zz):
        return remote(pb.at[2 * zz + c], q2.at[zz], ts.at[zz], tr.at[zz], d, ja)

    def ucopy(k, zz):
        return remote(pb.at[2 * zz + c], dn_ref.at[g], us.at[k], ur.at[0], d, 2 * zz + c)

    def hcopy(k):
        slot = (me + k) % 32
        return remote(hs_buf.at[slot], hb.at[me], hs.at[k], hr.at[me], slot // 8, slot % 8)

    def vcopy(k):
        slot = (me + k) % 32
        return remote(vs_buf, vb.at[me], vs.at[k], vr.at[me], slot // 8, slot % 8)

    for zz, dp in first + rest:
        gcopy(zz, dp).start()

    def sums1():
        for k, (zz, dp) in enumerate(first + rest):
            gloads[k].wait()
            gcopy(zz, dp).wait_recv()
            add_into(acc.at[dp * 4 + zz], b1.at[dp * 4 + zz])
            if k < len(first):
                stage2(zz, dp).start()

    def sums2():
        for pick in (1, 0):
            for zz in range(4):
                dp = (d, dy if zz % 2 == 0 else dx)[pick]
                stage2(zz, dp).wait_recv()
                add_into(acc.at[dp * 4 + zz], b2.at[dp * 4 + zz])
                if pick:
                    stage3(zz).start()

    def sums3():
        for zz in range(4):
            stage3(zz).wait_recv()
            add_into(acc.at[d * 4 + zz], b3.at[zz])
        for k, (zz, jz) in enumerate(((za, ja), (zb, jb), (zc, jc))):
            stage4(k, zz, jz).start()

    def both_cores(zz):
        pcopy(zz).wait_recv()
        add_into(pb.at[2 * zz + c], q1.at[zz])

    def pass_on(k, zz):
        @pl.when(near)
        def _():
            tcopy(zz).wait_recv()
            add_into(pb.at[2 * zz + c], q2.at[zz])
            ucopy(k, zz).start()

    def to_near(zz):
        @pl.when(far)
        def _():
            tcopy(zz).start()

    def event0():
        both_cores(w3)
        to_near(w3)

    def event1():
        both_cores(w2)
        to_near(w2)
        pass_on(0, w3)

    def event2():
        both_cores(wn)
        to_near(wn)
        pass_on(1, w2)

    events = {(0, 3): sums1, (1, 4): sums2, (2, 0): event0, (2, 3): sums3, (4, 0): event1, (6, 0): event2}

    lane = lane_of(rows)
    low = upper(rows)
    left = lane < SIDE

    def prepare(b, _):
        do = do_ref[b].astype(F32)
        both = do * o32_ref[b]
        for h in range(2):
            mine = left if h == 0 else jnp.logical_not(left)
            delta = jnp.sum(jnp.where(mine, both, 0.0), -1, keepdims=True)
            a, bb, cc = three(delta)
            da[h, b] = beside(h, lane, do, (None, -a, -bb, -cc))
        qt[b] = jnp.where(left, qa[0, b], qa[1, b]).T
        kt[b] = jnp.where(left, ka[0, b], ka[1, b]).T
        dot[b] = do_ref[b].T
        dq[b] = jnp.zeros((LANES, rows), F32)
        dk[b] = jnp.zeros((LANES, rows), F32)
        dv[b] = jnp.zeros((LANES, rows), F32)
        return 0

    lax.fori_loop(0, blocks, prepare, 0)
    gain = gain_ref[...].astype(F32)
    dw[...] = jnp.zeros_like(dw)
    vs_buf[...] = sum_ref[...]

    def finish(b):
        x = x_ref[b].astype(F32)
        n1 = x * lax.rsqrt(jnp.mean(x * x, -1, keepdims=True) + EPS)
        n = (n1 * gain).astype(BF)
        q = (dq[b] * HEAD_DIM ** (-0.5)).astype(BF)
        k = (dk[b] * (1.0 / LOG2E)).astype(BF)
        pt = jnp.concatenate([q, k, dv[b].astype(BF)], axis=0)
        dw[...] += nn(pt, n)
        dn = nt(pt.T, w_ref[...])
        pb[b] = dn.astype(BF)
        vs_buf[0:1] += jnp.sum(dn * n1, 0, keepdims=True)

    def pair(kb, b, masked=False):
        for h in range(2):
            part = slice(h * SIDE, (h + 1) * SIDE)
            p = jnp.exp2(nt(ka[h, kb], qa[h, b]))
            if masked:
                p = jnp.where(low, p, 0.0)
            ds = (p * nt(va[h, kb], da[h, b])).astype(BF)
            dv[kb, part] += nt(dot[b, part], p.astype(BF))
            dk[kb, part] += nt(qt[b, part], ds)
            dq[b, part] += nn(kt[kb, part], ds)

    def outer(i, _):
        o = g * i + (1 - g) * (blocks - 1 - i)
        pair(o, o, True)

        def inner(t, _):
            pair(g * o + (1 - g) * (o - 1 - t), g * (o + 1 + t) + (1 - g) * o)
            for (ei, et), event in events.items():
                pl.when(jnp.logical_and(i == ei, t == et))(event)
            return 0

        lax.fori_loop(0, blocks - 1 - i, inner, 0)
        finish(o)

        @pl.when(o % 2 != c)
        def _():
            pcopy(o // 2).start()

        return 0

    lax.fori_loop(0, blocks, outer, 0)
    wide = dw[...].T.astype(BF)
    hs_buf[...] = wide.reshape(32, per, 3 * LANES)
    keep_h = pltpu.make_async_copy(hs_buf.at[me], hb.at[me], lo.at[0])
    keep_v = pltpu.make_async_copy(vs_buf, vb.at[me], lo.at[1])
    keep_h.start()
    keep_v.start()

    def hstart(k, _):
        hcopy(k).start()
        vcopy(k).start()
        return 0

    both_cores(wf)

    @pl.when(near)
    def _():
        tcopy(wf).start()

    lax.fori_loop(1, 32, hstart, 0)
    for zz in (za, zb, zc):
        remote(acc.at[0], b4.at[zz], s4.at[0], r4.at[zz], d, ja).wait_recv()
    gf_ref[...] = (
        acc[d * 4 + z].astype(F32)
        + b4[za].astype(F32) + b4[zb].astype(F32) + b4[zc].astype(F32)
    )
    keep_h.wait()
    keep_v.wait()

    def harrive(k, _):
        slot = (me + k) % 32
        remote(hs_buf.at[0], hb.at[slot], hs.at[0], hr.at[slot], d, pj).wait_recv()
        remote(vs_buf, vb.at[slot], vs.at[0], vr.at[slot], d, pj).wait_recv()
        return 0

    lax.fori_loop(1, 32, harrive, 0)
    total = jnp.zeros(gv_ref.shape, F32)
    for hi in range(4):
        part = jnp.zeros((per, 3 * LANES), F32)
        for k in range(8):
            slot = (k // 2) * 8 + (k % 2) * 4 + hi
            part += hb[slot].astype(F32)
            total += vb[slot]
        for m in range(3):
            gq_ref[m, :, hi * LANES : (hi + 1) * LANES] = part[:, m * LANES : (m + 1) * LANES]
    gv_ref[...] = total
    tcopy(z).wait_recv()

    def mine(i, _):
        piece = pl.ds(i * 128, 128)
        own[piece, :] = (pb[j, piece, :].astype(F32) + q2[z, piece, :].astype(F32)).astype(BF)
        return 0

    lax.fori_loop(0, rows // 128, mine, 0)
    keep = pltpu.make_async_copy(own, dn_ref.at[g], lo.at[2])
    keep.start()
    ucopy(0, w3).wait_recv()
    for zz, dp in first + rest:
        gcopy(zz, dp).wait_send()
    for zz, dp in first:
        stage2(zz, dp).wait_send()
    for zz in range(4):
        stage3(zz).wait_send()
        pcopy(zz).wait_send()
    for k, (zz, jz) in enumerate(((za, ja), (zb, jb), (zc, jc))):
        stage4(k, zz, jz).wait_send()

    def hsent(k, _):
        hcopy(k).wait_send()
        vcopy(k).wait_send()
        return 0

    lax.fori_loop(1, 32, hsent, 0)

    @pl.when(near)
    def _():
        tcopy(wf).wait_send()
        ucopy(0, w3).wait_send()
        ucopy(1, w2).wait_send()

    @pl.when(far)
    def _():
        for zz in (w3, w2, wn):
            tcopy(zz).wait_send()

    keep.wait()


def attend_back(xg, w, gain, o32, do, qa, ka, va, sums, grads):
    blocks, rows, width = xg.shape
    g = grads.shape[1:]
    per = width // 32
    dma = pltpu.SemaphoreType.DMA
    turned = pltpu.VMEM((blocks, LANES, rows), BF)
    total = pltpu.VMEM((blocks, LANES, rows), F32)
    return pl.pallas_call(
        attend_back_kernel,
        out_shape=(
            jax.ShapeDtypeStruct((2, rows, width), BF),
            jax.ShapeDtypeStruct(g, F32),
            jax.ShapeDtypeStruct((3, per, width), F32),
            jax.ShapeDtypeStruct(sums.shape, F32),
        ),
        in_specs=[INVM] * 9 + [ANY],
        out_specs=(ANY, INVM, INVM, INVM),
        scratch_shapes=[
            pltpu.VMEM((2, blocks, rows, LANES), BF), turned, turned, turned, total, total, total,
            pltpu.VMEM((3 * LANES, width), F32),
            pltpu.VMEM((blocks, rows, width), BF),
            pltpu.VMEM((32, per, 3 * LANES), BF),
            pltpu.VMEM(sums.shape, F32),
            pltpu.VMEM((16,) + g, BF),
            pltpu.VMEM((16,) + g, BF),
            pltpu.VMEM((16,) + g, BF),
            pltpu.VMEM((4,) + g, BF),
            pltpu.VMEM((4,) + g, BF),
            pltpu.VMEM((4, rows, width), BF),
            pltpu.VMEM((4, rows, width), BF),
            pltpu.VMEM((32, per, 3 * LANES), BF),
            pltpu.VMEM((32,) + sums.shape, F32),
            pltpu.VMEM((rows, width), BF),
            dma((16,)), dma((3,)),
            dma((16,)), dma((16,)), dma((16,)), dma((16,)), dma((4,)), dma((4,)), dma((4,)), dma((4,)),
            dma((4,)), dma((4,)), dma((4,)), dma((4,)), dma((2,)), dma((1,)),
            dma((32,)), dma((32,)), dma((32,)), dma((32,)),
        ],
        compiler_params=pltpu.CompilerParams(
            collective_id=3, has_side_effects=True, vmem_limit_bytes=VMEM_LIMIT
        ),
        name="attend_back",
    )(xg, w, gain, o32, do, qa, ka, va, sums, grads)


def by_heads(
    layer_input, cotangent, doc_len, doc_offset,
    w_query, w_key, w_value, w_out, w_gate_attn, w_gate_ffn, w_in, w_back,
    norm_attn, norm_ffn, bias_attn, bias_ffn,
):
    micro, _, rows, width = layer_input.shape
    per = w_query.shape[0]
    ff = w_in.shape[1] // width
    j = lax.axis_index("seq")
    x = layer_input[:, 0]
    cot = cotangent[:, 0]
    small = jnp.pad(
        jnp.stack([norm_attn, norm_ffn, bias_attn, bias_ffn] * 2), ((0, 8), (0, LANES - per))
    )
    mats = (w_query, w_key, w_value, w_out, w_gate_attn, w_gate_ffn, w_in, w_back)
    xg, wg, w, vecs, att, o32, qa, ka, va = front(doc_len, doc_offset, x, mats, small)
    gain = vecs[0:1]
    out, datt, dh, dna, grads, sums = tokens(x, cot, att, wg, vecs)
    do = swap(datt, 2)
    dn, gf, gq, gv = attend_back(xg, w, gain, o32, do, qa, ka, va, sums, grads)
    x32 = x.astype(F32)
    r1 = lax.rsqrt(jnp.mean(x32 * x32, -1, keepdims=True) + EPS)
    n1 = x32 * r1
    g1 = (dna + dn.astype(F32)) * gain.astype(F32)
    grad = dh + r1 * (g1 - n1 * jnp.mean(g1 * n1, -1, keepdims=True))
    gv = lax.dynamic_slice(gv, (0, (lax.axis_index("dp") * 8 + j) * per), (4, per))
    return (
        out[:, None],
        grad[:, None],
        gq[0], gq[1], gq[2],
        gf[:per], gf[per : 2 * per], gf[2 * per : 3 * per],
        gf[3 * per : (3 + ff) * per].reshape(ff, per, width).transpose(1, 0, 2).reshape(per, ff * width),
        gf[(3 + ff) * per :],
        gv[0], gv[1], gv[2], gv[3],
    )


def from_behind(x, axis, by):
    count = lax.axis_size(axis)
    pairs = [(i, i + by) for i in range(count) if 0 <= i + by < count]
    return lax.ppermute(x, axis, pairs)


def passed_along(value, axis, steps):
    count = lax.axis_size(axis)
    pairs = [(source, (source + steps) % count) for source in range(count)]
    return lax.ppermute(value, axis, pairs)


def rms_norm(values, gain):
    return values * lax.rsqrt(jnp.mean(values * values, -1, keepdims=True) + EPS) * gain


def dense(left, right):
    return jnp.dot(left, right, preferred_element_type=jnp.float32)


def dense_tn(left, right):
    return lax.dot_general(
        left, right, (((0,), (0,)), ((), ())), preferred_element_type=jnp.float32
    )


def dense_nt(left, right):
    return lax.dot_general(
        left, right, (((1,), (1,)), ((), ())), preferred_element_type=jnp.float32
    )


def layout_of(lengths, offsets, source, rows, filler):
    positions = source * rows + jnp.arange(rows, dtype=jnp.int32)
    region = positions // DOC_MAX
    inside = positions - region * DOC_MAX
    members = (region[:, None] == jnp.arange(lengths.shape[1], dtype=jnp.int32)[None, :]).astype(
        jnp.int32
    )
    begins = jnp.sum(members[None] * offsets[:, None, :], axis=2)
    spans = jnp.sum(members[None] * lengths[:, None, :], axis=2)
    inside_doc = (inside[None] >= begins) & (inside[None] < begins + spans)
    labels = jnp.where(inside_doc, region[None], filler)
    return (positions, labels, inside_doc)


def allowed_pairs(query_side, key_side):
    same_doc = query_side[1][:, :, None] == key_side[1][:, None, :]
    causal = key_side[0][None, None, :] <= query_side[0][None, :, None]
    return same_doc & causal


def absorb(carry, query, key_piece, value_piece, allowed):
    run_max, run_sum, totals = carry
    scores = jnp.einsum(
        "mqhd,mkhd->mhqk", query, key_piece, preferred_element_type=jnp.float32
    ) * HEAD_DIM ** (-0.5)
    scores = jnp.where(allowed[:, None], scores, -1e30)
    new_max = jnp.maximum(run_max, jnp.max(scores, axis=-1))
    factor = jnp.exp(run_max - new_max)
    weights = jnp.where(allowed[:, None], jnp.exp(scores - new_max[..., None]), 0.0)
    run_sum = run_sum * factor + jnp.sum(weights, axis=-1)
    totals = totals * factor[..., None] + jnp.einsum(
        "mhqk,mkhd->mhqd", weights, value_piece.astype(jnp.float32)
    )
    return (new_max, run_sum, totals)


def hop_grads(query, grad_att, lse, delta, key_piece, value_piece, allowed):
    scores = jnp.einsum(
        "mqhd,mkhd->mhqk", query, key_piece, preferred_element_type=jnp.float32
    ) * HEAD_DIM ** (-0.5)
    probs = jnp.where(allowed[:, None], jnp.exp(scores - lse[..., None]), 0.0)
    grad_value = jnp.einsum("mhqk,mqhd->mkhd", probs, grad_att.astype(jnp.float32))
    grad_probs = jnp.einsum(
        "mqhd,mkhd->mhqk", grad_att, value_piece, preferred_element_type=jnp.float32
    )
    grad_scores = probs * (grad_probs - delta[..., None]) * HEAD_DIM ** (-0.5)
    grad_query = jnp.einsum("mhqk,mkhd->mqhd", grad_scores, key_piece.astype(jnp.float32))
    grad_key = jnp.einsum("mhqk,mqhd->mkhd", grad_scores, query.astype(jnp.float32))
    return (grad_query, grad_key, grad_value)


def shards(
    layer_input,
    cotangent,
    doc_len,
    doc_offset,
    w_query,
    w_key,
    w_value,
    w_out,
    w_gate_attn,
    w_gate_ffn,
    w_in,
    w_back,
    norm_attn,
    norm_ffn,
    bias_attn,
    bias_ffn,
):
    gathered = (
        lax.all_gather(w_query, ("dp", "seq"), axis=0, tiled=True),
        lax.all_gather(w_key, ("dp", "seq"), axis=0, tiled=True),
        lax.all_gather(w_value, ("dp", "seq"), axis=0, tiled=True),
        lax.all_gather(w_out, ("dp", "seq"), axis=0, tiled=True),
        lax.all_gather(w_gate_attn, ("dp", "seq"), axis=0, tiled=True),
        lax.all_gather(w_gate_ffn, ("dp", "seq"), axis=0, tiled=True),
        lax.all_gather(w_in, ("dp", "seq"), axis=0, tiled=True),
        lax.all_gather(w_back, ("dp", "seq"), axis=0, tiled=True),
        lax.all_gather(norm_attn, ("dp", "seq"), axis=0, tiled=True),
        lax.all_gather(norm_ffn, ("dp", "seq"), axis=0, tiled=True),
        lax.all_gather(bias_attn, ("dp", "seq"), axis=0, tiled=True),
        lax.all_gather(bias_ffn, ("dp", "seq"), axis=0, tiled=True),
    )
    (
        full_query,
        full_key,
        full_value,
        full_out,
        full_gate_attn,
        full_gate_ffn,
        full_in,
        full_back,
        gain_attn,
        gain_ffn,
        shift_attn,
        shift_ffn,
    ) = gathered
    micro = layer_input.shape[0]
    rows = layer_input.shape[2]
    width = layer_input.shape[3]
    tokens = micro * rows
    nseq = lax.axis_size("seq")
    me_index = lax.axis_index("seq")
    hops = min(max(DOC_MAX // rows, 1), nseq) - 1
    lengths = doc_len[:, 0]
    offsets = doc_offset[:, 0]

    def key_side(source):
        positions, labels, _ = layout_of(lengths, offsets, source, rows, -2)
        return (positions, labels)

    own_layout = layout_of(lengths, offsets, me_index, rows, -1)
    query_side = (own_layout[0], own_layout[1])
    own_keys = key_side(me_index)
    inputs = layer_input[:, 0].reshape(tokens, width).astype(jnp.float32)
    normed_attn, pull_attn = jax.vjp(rms_norm, inputs, gain_attn.astype(jnp.float32))
    normed_low = normed_attn.astype(jnp.bfloat16)
    query = dense(normed_low, full_query).astype(jnp.bfloat16)
    keys = dense(normed_low, full_key).astype(jnp.bfloat16)
    values = dense(normed_low, full_value).astype(jnp.bfloat16)
    gate_attn = jax.nn.sigmoid(dense(normed_low, full_gate_attn) + shift_attn.astype(jnp.float32))
    head_shape = (micro, rows, HEADS, HEAD_DIM)
    query_h = query.reshape(head_shape)
    keys_h = keys.reshape(head_shape)
    values_h = values.reshape(head_shape)
    start_carry = (
        jnp.full((micro, HEADS, rows), -1e30, jnp.float32),
        jnp.zeros((micro, HEADS, rows), jnp.float32),
        jnp.zeros((micro, HEADS, rows, HEAD_DIM), jnp.float32),
    )
    carry = absorb(start_carry, query_h, keys_h, values_h, allowed_pairs(query_side, own_keys))

    def forward_hop(hop, state):
        pieces, inner = state
        pieces = from_behind((pieces[0], pieces[1]), "seq", 1)
        source = me_index - hop
        inner = absorb(
            inner, query_h, pieces[0], pieces[1], allowed_pairs(query_side, key_side(source))
        )
        return (pieces, inner)

    _, (run_max, run_sum, totals) = lax.fori_loop(
        1, hops + 1, forward_hop, ((keys_h, values_h), carry)
    )
    live = own_layout[2][:, None, :]
    safe_sum = jnp.where(live, run_sum, 1.0)
    attended_h = jnp.where(live[..., None], totals / safe_sum[..., None], 0.0)
    lse = jnp.where(live, run_max + jnp.log(safe_sum), 0.0)
    attended32 = attended_h.transpose(0, 2, 1, 3).reshape(tokens, width)
    attended = attended32.astype(jnp.bfloat16)
    branch_attn = dense(attended, full_out)
    hidden = gate_attn * branch_attn + (1.0 - gate_attn) * inputs
    normed_ffn, pull_ffn = jax.vjp(rms_norm, hidden, gain_ffn.astype(jnp.float32))
    normed_ffn_low = normed_ffn.astype(jnp.bfloat16)
    pre = dense(normed_ffn_low, full_in)
    act32, pull_gelu = jax.vjp(partial(jax.nn.gelu, approximate=True), pre)
    act = act32.astype(jnp.bfloat16)
    branch_ffn = dense(act, full_back)
    gate_ffn = jax.nn.sigmoid(dense(normed_ffn_low, full_gate_ffn) + shift_ffn.astype(jnp.float32))
    output = gate_ffn * branch_ffn + (1.0 - gate_ffn) * hidden
    again = (
        lax.all_gather(w_query, ("dp", "seq"), axis=0, tiled=True),
        lax.all_gather(w_key, ("dp", "seq"), axis=0, tiled=True),
        lax.all_gather(w_value, ("dp", "seq"), axis=0, tiled=True),
        lax.all_gather(w_out, ("dp", "seq"), axis=0, tiled=True),
        lax.all_gather(w_gate_attn, ("dp", "seq"), axis=0, tiled=True),
        lax.all_gather(w_gate_ffn, ("dp", "seq"), axis=0, tiled=True),
        lax.all_gather(w_in, ("dp", "seq"), axis=0, tiled=True),
        lax.all_gather(w_back, ("dp", "seq"), axis=0, tiled=True),
        lax.all_gather(norm_attn, ("dp", "seq"), axis=0, tiled=True),
        lax.all_gather(norm_ffn, ("dp", "seq"), axis=0, tiled=True),
        lax.all_gather(bias_attn, ("dp", "seq"), axis=0, tiled=True),
        lax.all_gather(bias_ffn, ("dp", "seq"), axis=0, tiled=True),
    )
    (
        back_query,
        back_key,
        back_value,
        back_out,
        back_gate_attn,
        back_gate_ffn,
        back_in,
        back_back,
        _,
        _,
        _,
        _,
    ) = again
    upstream = cotangent[:, 0].reshape(tokens, width).astype(jnp.float32)
    d_logit_ffn = (upstream * (branch_ffn - hidden) * gate_ffn * (1.0 - gate_ffn)).astype(
        jnp.bfloat16
    )
    d_branch_ffn = (upstream * gate_ffn).astype(jnp.bfloat16)
    grad_back = dense_tn(act, d_branch_ffn)
    (d_pre32,) = pull_gelu(dense_nt(d_branch_ffn, back_back))
    d_pre = d_pre32.astype(jnp.bfloat16)
    grad_in = dense_tn(normed_ffn_low, d_pre)
    grad_gate_ffn = dense_tn(normed_ffn_low, d_logit_ffn)
    grad_bias_ffn = jnp.sum(d_logit_ffn.astype(jnp.float32), axis=0)
    d_normed_ffn = dense_nt(d_pre, back_in) + dense_nt(d_logit_ffn, back_gate_ffn)
    d_hidden_norm, grad_gain_ffn = pull_ffn(d_normed_ffn)
    d_hidden = upstream * (1.0 - gate_ffn) + d_hidden_norm
    d_branch_attn = (d_hidden * gate_attn).astype(jnp.bfloat16)
    d_logit_attn = (d_hidden * (branch_attn - inputs) * gate_attn * (1.0 - gate_attn)).astype(
        jnp.bfloat16
    )
    grad_out = dense_tn(attended, d_branch_attn)
    d_attended = dense_nt(d_branch_attn, back_out).astype(jnp.bfloat16)
    grad_att = d_attended.reshape(head_shape)
    delta = jnp.einsum(
        "mqhd,mqhd->mhq", grad_att.astype(jnp.float32), attended32.reshape(head_shape)
    )
    first_q, first_k, first_v = hop_grads(
        query_h, grad_att, lse, delta, keys_h, values_h, allowed_pairs(query_side, own_keys)
    )

    def backward_hop(hop, state):
        pieces, moving, grad_q = state
        pieces = from_behind((pieces[0], pieces[1]), "seq", 1)
        moving = (
            passed_along(moving[0].astype(jnp.bfloat16), "seq", 1).astype(jnp.float32),
            passed_along(moving[1].astype(jnp.bfloat16), "seq", 1).astype(jnp.float32),
        )
        source = me_index - hop
        step_q, step_k, step_v = hop_grads(
            query_h,
            grad_att,
            lse,
            delta,
            pieces[0],
            pieces[1],
            allowed_pairs(query_side, key_side(source)),
        )
        return (pieces, (moving[0] + step_k, moving[1] + step_v), grad_q + step_q)

    _, moving, grad_q = lax.fori_loop(
        1, hops + 1, backward_hop, ((keys_h, values_h), (first_k, first_v), first_q)
    )
    moving = (
        passed_along(moving[0].astype(jnp.bfloat16), "seq", -hops).astype(jnp.float32),
        passed_along(moving[1].astype(jnp.bfloat16), "seq", -hops).astype(jnp.float32),
    )
    grad_k, grad_v = moving
    d_query = grad_q.reshape(tokens, width).astype(jnp.bfloat16)
    d_key = grad_k.reshape(tokens, width).astype(jnp.bfloat16)
    d_value = grad_v.reshape(tokens, width).astype(jnp.bfloat16)
    grad_query = dense_tn(normed_low, d_query)
    grad_key = dense_tn(normed_low, d_key)
    grad_value = dense_tn(normed_low, d_value)
    grad_gate_attn = dense_tn(normed_low, d_logit_attn)
    grad_bias_attn = jnp.sum(d_logit_attn.astype(jnp.float32), axis=0)
    d_normed_attn = (
        dense_nt(d_query, back_query)
        + dense_nt(d_key, back_key)
        + dense_nt(d_value, back_value)
        + dense_nt(d_logit_attn, back_gate_attn)
    )
    d_inputs_norm, grad_gain_attn = pull_attn(d_normed_attn)
    grad_input = d_hidden * (1.0 - gate_attn) + d_inputs_norm
    owned = (
        lax.psum_scatter(grad_query, ("dp", "seq"), scatter_dimension=0, tiled=True),
        lax.psum_scatter(grad_key, ("dp", "seq"), scatter_dimension=0, tiled=True),
        lax.psum_scatter(grad_value, ("dp", "seq"), scatter_dimension=0, tiled=True),
        lax.psum_scatter(grad_out, ("dp", "seq"), scatter_dimension=0, tiled=True),
        lax.psum_scatter(grad_gate_attn, ("dp", "seq"), scatter_dimension=0, tiled=True),
        lax.psum_scatter(grad_gate_ffn, ("dp", "seq"), scatter_dimension=0, tiled=True),
        lax.psum_scatter(grad_in, ("dp", "seq"), scatter_dimension=0, tiled=True),
        lax.psum_scatter(grad_back, ("dp", "seq"), scatter_dimension=0, tiled=True),
        lax.psum_scatter(grad_gain_attn, ("dp", "seq"), scatter_dimension=0, tiled=True),
        lax.psum_scatter(grad_gain_ffn, ("dp", "seq"), scatter_dimension=0, tiled=True),
        lax.psum_scatter(grad_bias_attn, ("dp", "seq"), scatter_dimension=0, tiled=True),
        lax.psum_scatter(grad_bias_ffn, ("dp", "seq"), scatter_dimension=0, tiled=True),
    )
    return (
        output.reshape(micro, 1, rows, width).astype(jnp.bfloat16),
        grad_input.reshape(micro, 1, rows, width),
        owned[0],
        owned[1],
        owned[2],
        owned[3],
        owned[4],
        owned[5],
        owned[6],
        owned[7],
        owned[8],
        owned[9],
        owned[10],
        owned[11],
    )


def solution(mesh):
    placed = (
        P(None, "dp", "seq", None),
        P(None, "dp", "seq", None),
        P(None, "dp", None),
        P(None, "dp", None),
        P(("dp", "seq"), None),
        P(("dp", "seq"), None),
        P(("dp", "seq"), None),
        P(("dp", "seq"), None),
        P(("dp", "seq"), None),
        P(("dp", "seq"), None),
        P(("dp", "seq"), None),
        P(("dp", "seq"), None),
        P(("dp", "seq")),
        P(("dp", "seq")),
        P(("dp", "seq")),
        P(("dp", "seq")),
    )
    def pick(layer_input, *others):
        micro, _, rows, width = layer_input.shape
        fits = (
            dict(mesh.shape) == {"dp": 4, "seq": 8}
            and micro == 2
            and others[1].shape[2] == 1
            and width == HEADS * HEAD_DIM
            and width == 4 * LANES
            and rows % 128 == 0
            and others[10].shape == (width // 8, width)
        )
        return (by_heads if fits else shards)(layer_input, *others)

    return jax.shard_map(
        pick,
        mesh=mesh,
        in_specs=placed,
        out_specs=(
            P(None, "dp", "seq", None),
            P(None, "dp", "seq", None),
            P(("dp", "seq"), None),
            P(("dp", "seq"), None),
            P(("dp", "seq"), None),
            P(("dp", "seq"), None),
            P(("dp", "seq"), None),
            P(("dp", "seq"), None),
            P(("dp", "seq"), None),
            P(("dp", "seq"), None),
            P(("dp", "seq")),
            P(("dp", "seq")),
            P(("dp", "seq")),
            P(("dp", "seq")),
        ),
        check_vma=False,
    )
```

```python
from functools import partial

import jax
import jax.numpy as jnp
from jax import lax
from jax.experimental import pallas as pl
from jax.experimental.pallas import tpu as pltpu
from jax.sharding import PartitionSpec as P

HEADS = 8
HEAD_DIM = 64
DOC_MAX = 4096

EPS = 1e-05
MESH = pl.DeviceIdType.MESH
BF = jnp.bfloat16
F32 = jnp.float32
VMEM_LIMIT = 66_000_000
LANES = 128
SIDE = 64
GELU_C = 0.7978845608028654
GELU_A = 0.044715
NEG = -1e30
ANY = pl.BlockSpec(memory_space=pl.ANY)
INVM = pl.BlockSpec(memory_space=pltpu.VMEM)
INSM = pl.BlockSpec(memory_space=pltpu.SMEM)


def nn(a, b):
    return lax.dot_general(a, b, (((1,), (0,)), ((), ())), preferred_element_type=F32)


def nt(a, b):
    return lax.dot_general(a, b, (((1,), (1,)), ((), ())), preferred_element_type=F32)


def tn(a, b):
    return lax.dot_general(a, b, (((0,), (0,)), ((), ())), preferred_element_type=F32)


def remote(src, dst, send, recv, dp, seq):
    return pltpu.make_async_remote_copy(
        src_ref=src, dst_ref=dst, send_sem=send, recv_sem=recv,
        device_id=(dp, seq), device_id_type=MESH,
    )


def greet(peers):
    barrier = pltpu.get_barrier_semaphore()
    for dp, seq in peers:
        pl.semaphore_signal(barrier, inc=1, device_id=(dp, seq), device_id_type=MESH)
    pl.semaphore_wait(barrier, len(peers))


def place():
    d = lax.axis_index("dp")
    j = lax.axis_index("seq")
    z = j // 2
    c = j % 2
    dx = d + 1 - 2 * (d % 2)
    dy = (d + 2) % 4
    dxy = 3 - d
    return d, j, z, c, dx, dy, dxy


CK = 4


class Spread:
    def __init__(self, dst, send, recv):
        self.dst, self.send, self.recv = dst, send, recv
        self.at = place()
        self.count = 0
        self.sent = []
        d, j, z, c, dx, dy, dxy = self.at
        self.pj = j + 1 - 2 * c
        self.lines = (z, z + 1 - 2 * (z % 2), (z + 2) % 4, 3 - z)
        self.slots = {
            dp: [where * 8 + 2 * zz + c for zz in self.lines]
            for dp, where in (("d", d), ("x", dx), ("y", dy), ("xy", dxy))
        }

    def make(self, slot, i, dp, seq, src=None):
        return remote(
            self.dst.at[slot] if src is None else src, self.dst.at[slot],
            self.send.at[i], self.recv.at[slot], dp, seq,
        )

    def put(self, slot, dp, seq, src=None):
        i = self.count
        self.count += 1
        self.make(slot, i, dp, seq, src).start()
        self.sent.append((slot, i))

    def arrive(self, slot):
        self.make(slot, 0, self.at[0], self.pj).wait_recv()

    def in_plane(self, src):
        d, j, z, c, dx, dy, dxy = self.at
        for dp, seq in ((dx, j), (dy, j), (d, self.pj)):
            self.put(self.slots["d"][0], dp, seq, src)

    def along(self, srcs):
        d, j, z, c, dx, dy, dxy = self.at
        for zz, src in zip(self.lines[1:], srcs):
            self.put(self.slots["d"][0], d, 2 * zz + c, src)

    def from_line(self, k):
        d, j, z, c, dx, dy, dxy = self.at
        slot = self.slots["d"][k]
        self.arrive(slot)
        for dp, seq in ((dx, j), (dy, j), (d, self.pj)):
            self.put(slot, dp, seq)

    def from_plane(self, k):
        d, j, z, c, dx, dy, dxy = self.at
        sx, sy = self.slots["x"][k], self.slots["y"][k]
        for slot in (sx, sy):
            self.arrive(slot)
            self.put(slot, d, self.pj)
        even = self.lines[k] % 2 == 0
        i = self.count
        self.count += 1
        self.sent.append((sx, i))

        @pl.when(even)
        def _():
            self.make(sx, i, dy, j).start()

        @pl.when(jnp.logical_not(even))
        def _():
            self.make(sy, i, dx, j).start()

    def from_corner(self):
        for slot in self.slots["xy"]:
            self.arrive(slot)
            self.put(slot, self.at[0], self.pj)

    def from_core(self):
        c = self.at[3]
        for slots in self.slots.values():
            for slot in slots:
                self.arrive(slot + 1 - 2 * c)

    def wait_sent(self):
        for slot, i in self.sent:
            self.make(slot, i, self.at[0], self.pj).wait_send()


LOG2E = 1.4426950408889634


def lane_of(rows):
    return lax.broadcasted_iota(jnp.int32, (rows, LANES), 1)


def three(v):
    a = v.astype(BF).astype(F32)
    b = (v - a).astype(BF).astype(F32)
    return a, b, v - a - b


def beside(h, lane, values, parts):
    first = SIDE * (1 - h)
    own = (lane < SIDE) if h == 0 else (lane >= SIDE)
    out = jnp.where(own, values, 0.0)
    for k, part in enumerate(parts):
        if part is not None:
            out = jnp.where(lane == first + k, part, out)
    return out.astype(BF)


def upper(rows):
    return lax.broadcasted_iota(jnp.int32, (rows, rows), 0) <= lax.broadcasted_iota(
        jnp.int32, (rows, rows), 1
    )


def front_kernel(
    doc_len, doc_off, x_ref, wq, wk, wv, wo, wga, wgf, win, wback, small_ref,
    xg, wg, w_ref, vec_ref, att, o32_ref, qa, ka, va,
    hv, hg, sv, vt, top, acc, ov,
    lsem, xsem, hsend, hrecv, wsend, wrecv, xsend, xrecv, ssend, srecv,
):
    blocks, rows, width = xg.shape
    per = wq.shape[0]
    d, j, z, c, dx, dy, dxy = place()
    me = d * 8 + j
    g = z // 2
    pj = j + 1 - 2 * c
    za, zb, zc = z + 1 - 2 * (z % 2), (z + 2) % 4, 3 - z
    ja = 2 * za + c
    near = jnp.logical_or(z == 1, z == 2)
    far = jnp.logical_or(z == 0, z == 3)
    loads = []
    pieces = [(m, hv.at[k * per : (k + 1) * per]) for k, m in enumerate((wq, wk, wv))]
    pieces += [(m, sv.at[k * per : (k + 1) * per]) for k, m in enumerate((wo, wga, wgf))]
    ff = win.shape[1] // width
    for k in range(ff):
        pieces.append((win.at[:, k * width : (k + 1) * width], sv.at[(3 + k) * per : (4 + k) * per]))
    pieces.append((wback, sv.at[(3 + ff) * per :]))
    for k, (src, dst) in enumerate(pieces):
        loads.append(pltpu.make_async_copy(src, dst, lsem.at[k]))
        loads[-1].start()
    own = pltpu.make_async_copy(x_ref.at[g], xg.at[j], xsem)
    own.start()
    lanes = lax.broadcasted_iota(jnp.int32, (LANES, LANES), 1)
    subs = lax.broadcasted_iota(jnp.int32, (LANES, LANES), 0)
    row = lax.broadcasted_iota(jnp.int32, (16, LANES), 0)
    tile = jnp.zeros((16, LANES), F32)
    for k in range(4):
        spot = jnp.where(lanes + k * LANES == me * per + subs, 1.0, 0.0).astype(BF)
        tile = jnp.where(row // 4 == k, nn(small_ref[...], spot), tile)
    for k in range(4):
        hv[3 * per :, k * LANES : (k + 1) * LANES] = tile.astype(BF)
    for k in range(3):
        loads[k].wait()
    greet([(d, (j + k) % 8) for k in range(1, 8)] + [(dx, j), (dy, j), (dxy, j)])

    weights = Spread(wg, wsend, wrecv)

    def mine(seq):
        return hv.at[:, pl.ds(pl.multiple_of(LANES * (seq % 4), LANES), LANES)]

    def hcopy(k):
        seq = (j + k) % 8
        return remote(mine(seq), hg.at[me], hsend.at[k], hrecv.at[j], d, seq)

    def lcopy(k, dp):
        line = hg.at[pl.ds(d * 8, 8)]
        return remote(line, line, hsend.at[8 + k], hrecv.at[8 + k], dp, j)

    for k in range(1, 8):
        hcopy(k).start()

    def xcopy(k, part, block, dp, seq, src=None):
        piece = pl.ds(part * (rows // CK), rows // CK)
        source = xg.at[block, piece] if src is None else x_ref.at[src, piece]
        return remote(source, xg.at[block, piece], xsend.at[k, part], xrecv.at[block, part], dp, seq)

    def xarrive(block):
        for part in range(CK):
            xcopy(0, part, block, d, pj).wait_recv()

    jn = 2 * (2 - g) + c
    for part in range(CK):
        xcopy(0, part, j, d, ja, g).start()
        xcopy(1, part, j, d, pj, g).start()
    for part in range(CK):
        xcopy(2, part, j, d, jn, 1 - g).start()
    keep_h = pltpu.make_async_copy(mine(j), hg.at[me], lsem.at[1])
    keep_h.start()
    for copy in loads[3:]:
        copy.wait()
    keep = pltpu.make_async_copy(sv, wg.at[me], lsem.at[0])
    keep.start()
    weights.in_plane(sv)

    weights.along([sv] * 3)
    keep_h.wait()
    for k in range(1, 8):
        seq = (j + k) % 8
        remote(mine(seq), hg.at[d * 8 + seq], hsend.at[k], hrecv.at[seq], d, seq).wait_recv()
    for k, dp in enumerate((dx, dy, dxy)):
        lcopy(k, dp).start()
    for k, dp in enumerate((dx, dy, dxy)):
        line = hg.at[pl.ds(dp * 8, 8)]
        remote(line, line, hsend.at[8 + k], hrecv.at[8 + k], dp, j).wait_recv()

    vecs = jnp.zeros((16, LANES), F32)
    for k in range(32):
        vecs += hg[k, 3 * per :].astype(F32)
    for k in range(4):
        vec_ref[:, k * LANES : (k + 1) * LANES] = vecs[4 * k : 4 * k + 4]
    for k in range(3):
        w_ref[:, k * LANES : (k + 1) * LANES] = hg[:, k * per : (k + 1) * per, :].reshape(width, LANES)

    off = doc_off[g, 0, 0]
    end = off + doc_len[g, 0, 0]
    lane = lane_of(rows)
    up = lax.broadcasted_iota(jnp.int32, (rows, 1), 0)
    along = lax.broadcasted_iota(jnp.int32, (1, rows), 1)
    tall = lax.broadcasted_iota(jnp.int32, (16, rows), 0)
    ones = jnp.where(tall == 0, 1.0, 0.0).astype(BF)

    def project(b):
        x = xg[b].astype(F32)
        n = (x * lax.rsqrt(jnp.mean(x * x, -1, keepdims=True) + EPS) * vec_ref[0:1]).astype(BF)
        p = nn(n, w_ref[...])
        pos = b * rows + up
        bad = jnp.where(jnp.logical_and(pos >= off, pos < end), 0.0, NEG)
        q = p[:, :LANES] * (HEAD_DIM ** (-0.5) * LOG2E)
        k = p[:, LANES : 2 * LANES]
        v = p[:, 2 * LANES :]
        for h in range(2):
            qa[h, b] = beside(h, lane, q, (1.0,))
            ka[h, b] = beside(h, lane, k, (bad, 1.0, 1.0, 1.0))
            va[h, b] = beside(h, lane, v, (None, 1.0, 1.0, 1.0))
        turned = v.astype(BF).T
        for h in range(2):
            vt[h, b, :SIDE] = turned[h * SIDE : (h + 1) * SIDE]
            vt[h, b, SIDE:] = ones

    def project_two(base):
        def body(k, _):
            project(base + k)
            return 0

        lax.fori_loop(0, 2, body, 0)

    z1 = 2 - g
    z2 = 3 * (1 - g)
    b1, b2 = 2 * z1 + c, 2 * z2 + c
    own.wait()
    xarrive(pj)
    project_two(2 * z)
    for part in range(CK):
        xcopy(0, part, ja, d, pj).wait_recv()
        xcopy(3, part, ja, d, pj).start()

        @pl.when(near)
        def _():
            xcopy(0, part, b1, d, pj).wait_recv()
            xcopy(6, part, b1, d, ja).start()
            xcopy(4, part, b1, d, pj).start()

    xarrive(ja + 1 - 2 * c)
    project_two(2 * za)

    keep_low = upper(rows)
    sub = lax.broadcasted_iota(jnp.int32, (SIDE, rows), 0)

    def scores(q, k):
        return [nt(ka[h, k], qa[h, q]) for h in range(2)]

    def first(q):
        ss = [jnp.where(keep_low, s, NEG) for s in scores(q, q)]
        new = [jnp.max(s, 0, keepdims=True) for s in ss]
        ps = [jnp.exp2(s - n).astype(BF) for s, n in zip(ss, new)]
        for h in range(2):
            top[h, q] = new[h]
            acc[h, q] = nn(vt[h, q], ps[h])

    def pair(q, k):
        ss = scores(q, k)
        old = [top[h, q] for h in range(2)]
        new = [jnp.maximum(old[h], jnp.max(ss[h], 0, keepdims=True)) for h in range(2)]
        ps = [jnp.exp2(ss[h] - new[h]).astype(BF) for h in range(2)]
        for h in range(2):
            top[h, q] = new[h]
            acc[h, q] = acc[h, q] * jnp.exp2(old[h] - new[h]) + nn(vt[h, k], ps[h])

    def acopy(q):
        return remote(ov.at[q], att.at[j], ssend.at[q], srecv.at[j], d, q)

    def finish(b):
        pos = b * rows + along
        live = jnp.logical_and(pos >= off, pos < end)
        outs = []
        for h in range(2):
            total = acc[h, b, SIDE : SIDE + 1]
            lse = jnp.where(live, top[h, b] + jnp.log2(total), -NEG)
            mine = jnp.where(live, acc[h, b, :SIDE] / total, 0.0)
            parts = three(lse)
            beyond = jnp.zeros((SIDE, rows), F32)
            for k in range(3):
                beyond = jnp.where(sub == k + 1, -parts[k], beyond)
            both = (mine, beyond) if h == 0 else (beyond, mine)
            out = jnp.concatenate(both, axis=0).T
            start = SIDE * (1 - h)
            aug = jnp.logical_and(lane > start, lane < start + 4)
            qa[h, b] = jnp.where(aug, out, qa[h, b].astype(F32)).astype(BF)
            outs.append(out)
        out = jnp.where(lane < SIDE, outs[0], outs[1])
        o32_ref[b] = out
        ov[b] = out.astype(BF)

        @pl.when(b != j)
        def _():
            acopy(b).start()

    def outer(i, _):
        @pl.when(i == 1)
        def _():
            weights.from_plane(0)

        @pl.when(i == 3)
        def _():
            @pl.when(near)
            def _():
                for part in range(CK):
                    xcopy(0, part, b2, d, pj).wait_recv()
                    xcopy(7, part, b2, d, ja).start()
                    xcopy(5, part, b2, d, pj).start()

            weights.from_line(1)

        @pl.when(i == 4)
        def _():
            @pl.when(far)
            def _():
                for part in range(CK):
                    xcopy(0, part, b1, d, pj).wait_recv()
                    xcopy(4, part, b1, d, pj).start()

            xarrive(b1 + 1 - 2 * c)

        pl.when(i == 5)(partial(weights.from_plane, 1))

        @pl.when(i == 6)
        def _():
            weights.from_line(2)

            @pl.when(far)
            def _():
                for part in range(CK):
                    xcopy(0, part, b2, d, pj).wait_recv()
                    xcopy(5, part, b2, d, pj).start()

            xarrive(b2 + 1 - 2 * c)
            weights.from_line(3)

        @pl.when(jnp.logical_or(i == 4, i == 6))
        def _():
            project_two(2 * (z1 + (z2 - z1) * ((i - 4) // 2)))

        pl.when(i == 7)(partial(weights.from_plane, 2))
        pl.when(i == 8)(partial(weights.from_plane, 3))
        pl.when(i == 10)(weights.from_corner)
        tail = i >= blocks
        o = jnp.where(g == 0, i, jnp.where(tail, i - 4, blocks - 1 - i))
        early = jnp.where(jnp.logical_or(g == 0, i < 4), i, i - 4)
        count = jnp.where(tail, 4 * g, early)
        out_now = jnp.logical_and(g == 1, i == blocks - 1)

        @pl.when(jnp.logical_not(tail))
        def _():
            first(o)

        pl.when(i == 7 * g)(lambda: finish(o))

        def inner(t, _):
            q = jnp.where(jnp.logical_or(g == 0, tail), o, o + 1 + t)
            k = jnp.where(g == 0, o - 1 - t, jnp.where(tail, t, o))
            pair(q, k)
            ends = jnp.logical_and(jnp.logical_or(g == 0, tail), t == count - 1)
            pl.when(jnp.logical_or(out_now, ends))(lambda: finish(q))
            return 0

        lax.fori_loop(0, count, inner, 0)
        return 0

    lax.fori_loop(0, blocks + 4, outer, 0)
    att[j] = ov[j]
    weights.from_core()
    for k in range(1, 8):
        q = (j + k) % 8
        remote(ov.at[q], att.at[q], ssend.at[q], srecv.at[q], d, q).wait_recv()
    for k in range(1, 8):
        hcopy(k).wait_send()
    for k, dp in enumerate((dx, dy, dxy)):
        lcopy(k, dp).wait_send()
    weights.wait_sent()
    for k in range(6):
        for part in range(CK):
            xcopy(k, part, j, d, pj).wait_send()

    @pl.when(near)
    def _():
        for k in (6, 7):
            for part in range(CK):
                xcopy(k, part, j, d, pj).wait_send()

    for k in range(1, 8):
        acopy((j + k) % 8).wait_send()
    keep.wait()


def front(doc_len, doc_off, x, mats, small):
    _, rows, width = x.shape
    per = mats[0].shape[0]
    blocks = 8
    tall = sum(m.shape[0] * (m.shape[1] // width) for m in mats[3:])
    side = jax.ShapeDtypeStruct((2, blocks, rows, LANES), BF)
    dma = pltpu.SemaphoreType.DMA
    return pl.pallas_call(
        front_kernel,
        out_shape=(
            jax.ShapeDtypeStruct((blocks, rows, width), BF),
            jax.ShapeDtypeStruct((32, tall, width), BF),
            jax.ShapeDtypeStruct((width, 3 * LANES), BF),
            jax.ShapeDtypeStruct((4, width), F32),
            jax.ShapeDtypeStruct((blocks, rows, LANES), BF),
            jax.ShapeDtypeStruct((blocks, rows, LANES), F32),
            side, side, side,
        ),
        in_specs=[INSM, INSM] + [ANY] * 9 + [INVM],
        out_specs=(INVM, ANY) + (INVM,) * 7,
        scratch_shapes=[
            pltpu.VMEM((3 * per + 16, width), BF),
            pltpu.VMEM((32, 3 * per + 16, LANES), BF),
            pltpu.VMEM((tall, width), BF),
            pltpu.VMEM((2, blocks, SIDE + 16, rows), BF),
            pltpu.VMEM((2, blocks, 1, rows), F32),
            pltpu.VMEM((2, blocks, SIDE + 16, rows), F32),
            pltpu.VMEM((blocks, rows, LANES), BF),
            dma((12,)), dma, dma((11,)), dma((11,)), dma((32,)), dma((32,)),
            dma((8, CK)), dma((8, CK)), dma((8,)), dma((8,)),
        ],
        compiler_params=pltpu.CompilerParams(
            collective_id=0, has_side_effects=True, vmem_limit_bytes=VMEM_LIMIT
        ),
        name="front",
    )(doc_len, doc_off, x, *mats, small)


def token_kernel(
    x_ref, c_ref, a_ref, wg, vec, out_ref, do_ref, dh_ref, dn_ref, g_ref, v_ref,
    gp, act, da, dpres, g_out, g_ga, g_gf, g_in, g_back, send, recv,
):
    d, j = lax.axis_index("dp"), lax.axis_index("seq")
    g = j // 4
    rows, width = x_ref.shape[1:]
    ff = gp.shape[0]
    per = width // 32

    def weight(lo):
        return wg[:, lo : lo + per, :].reshape(width, width)

    def back(k):
        n = wg.shape[0] // ff
        return wg[k * n : (k + 1) * n, 7 * per : 7 * per + ff * per, :].reshape(width, width)

    for ref in (g_out, g_ga, g_gf, g_in, g_back, v_ref):
        ref[...] = jnp.zeros_like(ref)
    greet([(d, (j + k) % 8) for k in range(1, 8)])

    def dcopy(q):
        return remote(da.at[q], do_ref.at[j], send.at[q], recv.at[j], d, q)

    def one(t, _):
        m = (1 - g) * (1 - t) + g * t
        x = x_ref[m].astype(F32)
        gain_a, gain_f = vec[0:1].astype(F32), vec[1:2].astype(F32)
        shift_a, shift_f = vec[2:3].astype(F32), vec[3:4].astype(F32)
        n1 = x * lax.rsqrt(jnp.mean(x * x, -1, keepdims=True) + EPS)
        na = (n1 * gain_a).astype(BF)
        ga = jax.nn.sigmoid(nn(na, weight(per)) + shift_a)
        att = jnp.concatenate([a_ref[4 * m + i] for i in range(4)], axis=1)
        br = nn(att, weight(0))
        hid = ga * br + (1.0 - ga) * x
        r2 = lax.rsqrt(jnp.mean(hid * hid, -1, keepdims=True) + EPS)
        n2 = hid * r2
        nf = (n2 * gain_f).astype(BF)
        bf = jnp.zeros((rows, width), F32)
        for k in range(ff):
            pre = nn(nf, weight((3 + k) * per))
            sq = pre * pre
            t = jnp.tanh(GELU_C * pre * (1.0 + GELU_A * sq))
            half = 0.5 * (1.0 + t)
            act[k] = (pre * half).astype(BF)
            gp[k] = half + 0.5 * pre * (1.0 - t * t) * (GELU_C * (1.0 + 3.0 * GELU_A * sq))
            bf += nn(act[k], back(k))
        gf = jax.nn.sigmoid(nn(nf, weight(2 * per)) + shift_f)
        out_ref[m] = (gf * bf + (1.0 - gf) * hid).astype(BF)
        c = c_ref[m].astype(F32)
        dlf = (c * (bf - hid) * gf * (1.0 - gf)).astype(BF)
        dbf = (c * gf).astype(BF)
        dnf = nt(dlf, weight(2 * per))
        for k in range(ff):
            dpre = (nt(dbf, back(k)) * gp[k]).astype(BF)
            dpres[k] = dpre
            dnf += nt(dpre, weight((3 + k) * per))
        g2 = dnf * gain_f
        dh = c * (1.0 - gf) + r2 * (g2 - n2 * jnp.mean(g2 * n2, -1, keepdims=True))
        dba = (dh * ga).astype(BF)
        dla = (dh * (br - x) * ga * (1.0 - ga)).astype(BF)
        datt = nt(dba, weight(0)).astype(BF)
        for i in range(4):
            da[4 * m + i] = datt[:, i * LANES : (i + 1) * LANES]

            @pl.when(j != 4 * m + i)
            def _():
                dcopy(4 * m + i).start()

        dna = nt(dla, weight(per))
        g_out[...] += tn(att, dba)
        g_ga[...] += tn(na, dla)
        g_gf[...] += tn(nf, dlf)
        for k in range(ff):
            g_back[k] += tn(act[k], dbf)
            g_in[k] += tn(nf, dpres[k])
        dh_ref[m] = dh * (1.0 - ga)
        dn_ref[m] = dna
        v_ref[0:1] += jnp.sum(dna * n1, 0, keepdims=True)
        v_ref[1:2] += jnp.sum(dnf * n2, 0, keepdims=True)
        v_ref[2:3] += jnp.sum(dla.astype(F32), 0, keepdims=True)
        v_ref[3:4] += jnp.sum(dlf.astype(F32), 0, keepdims=True)
        return 0

    lax.fori_loop(0, 2, one, 0)

    def put(lo, value):
        g_ref[:, lo : lo + per, :] = value.astype(BF).reshape(32, per, width)

    put(0, g_out[...])
    put(per, g_ga[...])
    put(2 * per, g_gf[...])
    for k in range(ff):
        put((3 + k) * per, g_in[k])
        n = 32 // ff
        g_ref[k * n : (k + 1) * n, (3 + ff) * per :, :] = (
            g_back[k].astype(BF).reshape(n, ff * per, width)
        )
    do_ref[j] = da[j]
    for k in range(1, 8):
        q = (j + k) % 8
        remote(da.at[q], do_ref.at[q], send.at[q], recv.at[q], d, q).wait_recv()
        dcopy(q).wait_send()


def tokens(x, cot, att, wg, vec):
    micro, rows, width = x.shape
    ff = 4
    per = width // 32
    grads = (32, (3 + 2 * ff) * per, width)
    return pl.pallas_call(
        token_kernel,
        out_shape=(
            jax.ShapeDtypeStruct((micro, rows, width), BF),
            jax.ShapeDtypeStruct((4 * micro, rows, LANES), BF),
            jax.ShapeDtypeStruct((micro, rows, width), F32),
            jax.ShapeDtypeStruct((micro, rows, width), F32),
            jax.ShapeDtypeStruct(grads, BF),
            jax.ShapeDtypeStruct((8, width), F32),
        ),
        in_specs=[INVM] * 5,
        out_specs=(INVM,) * 6,
        scratch_shapes=[
            pltpu.VMEM((ff, rows, width), F32),
            pltpu.VMEM((ff, rows, width), BF),
            pltpu.VMEM((4 * micro, rows, LANES), BF),
            pltpu.VMEM((ff, rows, width), BF),
            pltpu.VMEM((width, width), F32),
            pltpu.VMEM((width, width), F32),
            pltpu.VMEM((width, width), F32),
            pltpu.VMEM((ff, width, width), F32),
            pltpu.VMEM((ff, width, width), F32),
            pltpu.SemaphoreType.DMA((8,)),
            pltpu.SemaphoreType.DMA((8,)),
        ],
        compiler_params=pltpu.CompilerParams(
            collective_id=1, has_side_effects=True, vmem_limit_bytes=VMEM_LIMIT
        ),
        name="tokens",
    )(x, cot, att, wg, vec)


def add_into(dst, src):
    rows = dst.shape[0]
    n = rows // 16
    per = 16 * max(k for k in range(1, 9) if n % k == 0)

    def body(i, _):
        piece = pl.ds(i * per, per)
        dst[piece, :] = (dst[piece, :].astype(F32) + src[piece, :].astype(F32)).astype(BF)
        return 0

    lax.fori_loop(0, rows // per, body, 0)


def attend_back_kernel(
    x_ref, w_ref, gain_ref, o32_ref, do_ref, qa, ka, va, sum_ref, g_ref,
    dn_ref, gf_ref, gq_ref, gv_ref,
    da, qt, kt, dot, dq, dk, dv, dw, pb, hs_buf, vs_buf,
    acc, b1, b2, b3, b4, q1, q2, hb, vb, own,
    l2, lo, s1, r1, s2, r2, s3, r3, s4, r4, ps, pr, ts, tr, us, ur, hs, hr, vs, vr,
):
    blocks, rows, width = x_ref.shape
    per = width // 32
    d, j, z, c, dx, dy, dxy = place()
    me = d * 8 + j
    g = z // 2
    pj = j + 1 - 2 * c
    za, zb, zc = z + 1 - 2 * (z % 2), (z + 2) % 4, 3 - z
    ja, jb, jc = 2 * za + c, 2 * zb + c, 2 * zc + c
    near = jnp.logical_or(z == 1, z == 2)
    far = jnp.logical_or(z == 0, z == 3)
    w3, w2, wn, wf = 3 * (1 - g), 2 - g, 1 + g, 3 * g
    first = [(zz, dp) for zz in range(4) for dp in ((dx, dxy) if zz % 2 == 0 else (dy, dxy))]
    rest = [(zz, dp) for zz in range(4) for dp in ((d, dy) if zz % 2 == 0 else (d, dx))]

    gloads = []
    for k, (zz, dp) in enumerate(first + rest):
        copy = pltpu.make_async_copy(g_ref.at[dp * 8 + 2 * zz + c], acc.at[dp * 4 + zz], l2.at[k])
        copy.start()
        gloads.append(copy)

    barrier = pltpu.get_barrier_semaphore()

    def hello(k, _):
        slot = (me + k) % 32
        pl.semaphore_signal(
            barrier, inc=1, device_id=(slot // 8, slot % 8), device_id_type=MESH
        )
        return 0

    lax.fori_loop(1, 32, hello, 0)
    pl.semaphore_wait(barrier, 31)

    def gcopy(zz, dp):
        i = dp * 4 + zz
        return remote(g_ref.at[dp * 8 + 2 * zz + 1 - c], b1.at[i], s1.at[i], r1.at[i], d, pj)

    def stage2(zz, dp):
        i = dp * 4 + zz
        to = dx if zz % 2 == 0 else dy
        return remote(acc.at[i], b2.at[i], s2.at[i], r2.at[i], to, j)

    def stage3(zz):
        to = dy if zz % 2 == 0 else dx
        return remote(acc.at[to * 4 + zz], b3.at[zz], s3.at[zz], r3.at[zz], to, j)

    def stage4(k, zz, jz):
        return remote(acc.at[d * 4 + zz], b4.at[z], s4.at[k], r4.at[z], d, jz)

    def pcopy(zz):
        return remote(pb.at[2 * zz + 1 - c], q1.at[zz], ps.at[zz], pr.at[zz], d, pj)

    def tcopy(zz):
        return remote(pb.at[2 * zz + c], q2.at[zz], ts.at[zz], tr.at[zz], d, ja)

    def ucopy(k, zz):
        return remote(pb.at[2 * zz + c], dn_ref.at[g], us.at[k], ur.at[0], d, 2 * zz + c)

    def hcopy(k):
        slot = (me + k) % 32
        return remote(hs_buf.at[slot], hb.at[me], hs.at[k], hr.at[me], slot // 8, slot % 8)

    def vcopy(k):
        slot = (me + k) % 32
        return remote(vs_buf, vb.at[me], vs.at[k], vr.at[me], slot // 8, slot % 8)

    for zz, dp in first + rest:
        gcopy(zz, dp).start()

    def sums1():
        for k, (zz, dp) in enumerate(first + rest):
            gloads[k].wait()
            gcopy(zz, dp).wait_recv()
            add_into(acc.at[dp * 4 + zz], b1.at[dp * 4 + zz])
            if k < len(first):
                stage2(zz, dp).start()

    def sums2():
        for pick in (1, 0):
            for zz in range(4):
                dp = (d, dy if zz % 2 == 0 else dx)[pick]
                stage2(zz, dp).wait_recv()
                add_into(acc.at[dp * 4 + zz], b2.at[dp * 4 + zz])
                if pick:
                    stage3(zz).start()

    def sums3():
        for zz in range(4):
            stage3(zz).wait_recv()
            add_into(acc.at[d * 4 + zz], b3.at[zz])
        for k, (zz, jz) in enumerate(((za, ja), (zb, jb), (zc, jc))):
            stage4(k, zz, jz).start()

    def both_cores(zz):
        pcopy(zz).wait_recv()
        add_into(pb.at[2 * zz + c], q1.at[zz])

    def pass_on(k, zz):
        @pl.when(near)
        def _():
            tcopy(zz).wait_recv()
            add_into(pb.at[2 * zz + c], q2.at[zz])
            ucopy(k, zz).start()

    def to_near(zz):
        @pl.when(far)
        def _():
            tcopy(zz).start()

    def event0():
        both_cores(w3)
        to_near(w3)

    def event1():
        both_cores(w2)
        to_near(w2)
        pass_on(0, w3)

    def event2():
        both_cores(wn)
        to_near(wn)
        pass_on(1, w2)

    events = {(0, 3): sums1, (1, 4): sums2, (2, 0): event0, (2, 3): sums3, (4, 0): event1, (6, 0): event2}

    lane = lane_of(rows)
    low = upper(rows)
    left = lane < SIDE

    def prepare(b, _):
        do = do_ref[b].astype(F32)
        both = do * o32_ref[b]
        for h in range(2):
            mine = left if h == 0 else jnp.logical_not(left)
            delta = jnp.sum(jnp.where(mine, both, 0.0), -1, keepdims=True)
            a, bb, cc = three(delta)
            da[h, b] = beside(h, lane, do, (None, -a, -bb, -cc))
        qt[b] = jnp.where(left, qa[0, b], qa[1, b]).T
        kt[b] = jnp.where(left, ka[0, b], ka[1, b]).T
        dot[b] = do_ref[b].T
        dq[b] = jnp.zeros((LANES, rows), F32)
        dk[b] = jnp.zeros((LANES, rows), F32)
        dv[b] = jnp.zeros((LANES, rows), F32)
        return 0

    lax.fori_loop(0, blocks, prepare, 0)
    gain = gain_ref[...].astype(F32)
    dw[...] = jnp.zeros_like(dw)
    vs_buf[...] = sum_ref[...]

    def finish(b):
        x = x_ref[b].astype(F32)
        n1 = x * lax.rsqrt(jnp.mean(x * x, -1, keepdims=True) + EPS)
        n = (n1 * gain).astype(BF)
        q = (dq[b] * HEAD_DIM ** (-0.5)).astype(BF)
        k = (dk[b] * (1.0 / LOG2E)).astype(BF)
        pt = jnp.concatenate([q, k, dv[b].astype(BF)], axis=0)
        dw[...] += nn(pt, n)
        dn = nt(pt.T, w_ref[...])
        pb[b] = dn.astype(BF)
        vs_buf[0:1] += jnp.sum(dn * n1, 0, keepdims=True)

    def pair(kb, b, masked=False):
        for h in range(2):
            part = slice(h * SIDE, (h + 1) * SIDE)
            p = jnp.exp2(nt(ka[h, kb], qa[h, b]))
            if masked:
                p = jnp.where(low, p, 0.0)
            ds = (p * nt(va[h, kb], da[h, b])).astype(BF)
            dv[kb, part] += nt(dot[b, part], p.astype(BF))
            dk[kb, part] += nt(qt[b, part], ds)
            dq[b, part] += nn(kt[kb, part], ds)

    def outer(i, _):
        o = g * i + (1 - g) * (blocks - 1 - i)
        pair(o, o, True)

        def inner(t, _):
            pair(g * o + (1 - g) * (o - 1 - t), g * (o + 1 + t) + (1 - g) * o)
            for (ei, et), event in events.items():
                pl.when(jnp.logical_and(i == ei, t == et))(event)
            return 0

        lax.fori_loop(0, blocks - 1 - i, inner, 0)
        finish(o)

        @pl.when(o % 2 != c)
        def _():
            pcopy(o // 2).start()

        return 0

    lax.fori_loop(0, blocks, outer, 0)
    wide = dw[...].T.astype(BF)
    hs_buf[...] = wide.reshape(32, per, 3 * LANES)
    keep_h = pltpu.make_async_copy(hs_buf.at[me], hb.at[me], lo.at[0])
    keep_v = pltpu.make_async_copy(vs_buf, vb.at[me], lo.at[1])
    keep_h.start()
    keep_v.start()

    def hstart(k, _):
        hcopy(k).start()
        vcopy(k).start()
        return 0

    both_cores(wf)

    @pl.when(near)
    def _():
        tcopy(wf).start()

    lax.fori_loop(1, 32, hstart, 0)
    for zz in (za, zb, zc):
        remote(acc.at[0], b4.at[zz], s4.at[0], r4.at[zz], d, ja).wait_recv()
    gf_ref[...] = (
        acc[d * 4 + z].astype(F32)
        + b4[za].astype(F32) + b4[zb].astype(F32) + b4[zc].astype(F32)
    )
    keep_h.wait()
    keep_v.wait()

    def harrive(k, _):
        slot = (me + k) % 32
        remote(hs_buf.at[0], hb.at[slot], hs.at[0], hr.at[slot], d, pj).wait_recv()
        remote(vs_buf, vb.at[slot], vs.at[0], vr.at[slot], d, pj).wait_recv()
        return 0

    lax.fori_loop(1, 32, harrive, 0)
    total = jnp.zeros(gv_ref.shape, F32)
    for hi in range(4):
        part = jnp.zeros((per, 3 * LANES), F32)
        for k in range(8):
            slot = (k // 2) * 8 + (k % 2) * 4 + hi
            part += hb[slot].astype(F32)
            total += vb[slot]
        for m in range(3):
            gq_ref[m, :, hi * LANES : (hi + 1) * LANES] = part[:, m * LANES : (m + 1) * LANES]
    gv_ref[...] = total
    tcopy(z).wait_recv()

    def mine(i, _):
        piece = pl.ds(i * 128, 128)
        own[piece, :] = (pb[j, piece, :].astype(F32) + q2[z, piece, :].astype(F32)).astype(BF)
        return 0

    lax.fori_loop(0, rows // 128, mine, 0)
    keep = pltpu.make_async_copy(own, dn_ref.at[g], lo.at[2])
    keep.start()
    ucopy(0, w3).wait_recv()
    for zz, dp in first + rest:
        gcopy(zz, dp).wait_send()
    for zz, dp in first:
        stage2(zz, dp).wait_send()
    for zz in range(4):
        stage3(zz).wait_send()
        pcopy(zz).wait_send()
    for k, (zz, jz) in enumerate(((za, ja), (zb, jb), (zc, jc))):
        stage4(k, zz, jz).wait_send()

    def hsent(k, _):
        hcopy(k).wait_send()
        vcopy(k).wait_send()
        return 0

    lax.fori_loop(1, 32, hsent, 0)

    @pl.when(near)
    def _():
        tcopy(wf).wait_send()
        ucopy(0, w3).wait_send()
        ucopy(1, w2).wait_send()

    @pl.when(far)
    def _():
        for zz in (w3, w2, wn):
            tcopy(zz).wait_send()

    keep.wait()


def attend_back(xg, w, gain, o32, do, qa, ka, va, sums, grads):
    blocks, rows, width = xg.shape
    g = grads.shape[1:]
    per = width // 32
    dma = pltpu.SemaphoreType.DMA
    turned = pltpu.VMEM((blocks, LANES, rows), BF)
    total = pltpu.VMEM((blocks, LANES, rows), F32)
    return pl.pallas_call(
        attend_back_kernel,
        out_shape=(
            jax.ShapeDtypeStruct((2, rows, width), BF),
            jax.ShapeDtypeStruct(g, F32),
            jax.ShapeDtypeStruct((3, per, width), F32),
            jax.ShapeDtypeStruct(sums.shape, F32),
        ),
        in_specs=[INVM] * 9 + [ANY],
        out_specs=(ANY, INVM, INVM, INVM),
        scratch_shapes=[
            pltpu.VMEM((2, blocks, rows, LANES), BF), turned, turned, turned, total, total, total,
            pltpu.VMEM((3 * LANES, width), F32),
            pltpu.VMEM((blocks, rows, width), BF),
            pltpu.VMEM((32, per, 3 * LANES), BF),
            pltpu.VMEM(sums.shape, F32),
            pltpu.VMEM((16,) + g, BF),
            pltpu.VMEM((16,) + g, BF),
            pltpu.VMEM((16,) + g, BF),
            pltpu.VMEM((4,) + g, BF),
            pltpu.VMEM((4,) + g, BF),
            pltpu.VMEM((4, rows, width), BF),
            pltpu.VMEM((4, rows, width), BF),
            pltpu.VMEM((32, per, 3 * LANES), BF),
            pltpu.VMEM((32,) + sums.shape, F32),
            pltpu.VMEM((rows, width), BF),
            dma((16,)), dma((3,)),
            dma((16,)), dma((16,)), dma((16,)), dma((16,)), dma((4,)), dma((4,)), dma((4,)), dma((4,)),
            dma((4,)), dma((4,)), dma((4,)), dma((4,)), dma((2,)), dma((1,)),
            dma((32,)), dma((32,)), dma((32,)), dma((32,)),
        ],
        compiler_params=pltpu.CompilerParams(
            collective_id=3, has_side_effects=True, vmem_limit_bytes=VMEM_LIMIT
        ),
        name="attend_back",
    )(xg, w, gain, o32, do, qa, ka, va, sums, grads)


def by_heads(
    layer_input, cotangent, doc_len, doc_offset,
    w_query, w_key, w_value, w_out, w_gate_attn, w_gate_ffn, w_in, w_back,
    norm_attn, norm_ffn, bias_attn, bias_ffn,
):
    micro, _, rows, width = layer_input.shape
    per = w_query.shape[0]
    ff = w_in.shape[1] // width
    j = lax.axis_index("seq")
    x = layer_input[:, 0]
    cot = cotangent[:, 0]
    small = jnp.pad(
        jnp.stack([norm_attn, norm_ffn, bias_attn, bias_ffn] * 4), ((0, 0), (0, LANES - per))
    )
    mats = (w_query, w_key, w_value, w_out, w_gate_attn, w_gate_ffn, w_in, w_back)
    xg, wg, w, vecs, att, o32, qa, ka, va = front(doc_len, doc_offset, x, mats, small)
    gain = vecs[0:1]
    out, do, dh, dna, grads, sums = tokens(x, cot, att, wg, vecs)
    dn, gf, gq, gv = attend_back(xg, w, gain, o32, do, qa, ka, va, sums, grads)
    x32 = x.astype(F32)
    r1 = lax.rsqrt(jnp.mean(x32 * x32, -1, keepdims=True) + EPS)
    n1 = x32 * r1
    g1 = (dna + dn.astype(F32)) * gain.astype(F32)
    grad = dh + r1 * (g1 - n1 * jnp.mean(g1 * n1, -1, keepdims=True))
    gv = lax.dynamic_slice(gv, (0, (lax.axis_index("dp") * 8 + j) * per), (4, per))
    return (
        out[:, None],
        grad[:, None],
        gq[0], gq[1], gq[2],
        gf[:per], gf[per : 2 * per], gf[2 * per : 3 * per],
        gf[3 * per : (3 + ff) * per].reshape(ff, per, width).transpose(1, 0, 2).reshape(per, ff * width),
        gf[(3 + ff) * per :],
        gv[0], gv[1], gv[2], gv[3],
    )


def from_behind(x, axis, by):
    count = lax.axis_size(axis)
    pairs = [(i, i + by) for i in range(count) if 0 <= i + by < count]
    return lax.ppermute(x, axis, pairs)


def passed_along(value, axis, steps):
    count = lax.axis_size(axis)
    pairs = [(source, (source + steps) % count) for source in range(count)]
    return lax.ppermute(value, axis, pairs)


def rms_norm(values, gain):
    return values * lax.rsqrt(jnp.mean(values * values, -1, keepdims=True) + EPS) * gain


def dense(left, right):
    return jnp.dot(left, right, preferred_element_type=jnp.float32)


def dense_tn(left, right):
    return lax.dot_general(
        left, right, (((0,), (0,)), ((), ())), preferred_element_type=jnp.float32
    )


def dense_nt(left, right):
    return lax.dot_general(
        left, right, (((1,), (1,)), ((), ())), preferred_element_type=jnp.float32
    )


def layout_of(lengths, offsets, source, rows, filler):
    positions = source * rows + jnp.arange(rows, dtype=jnp.int32)
    region = positions // DOC_MAX
    inside = positions - region * DOC_MAX
    members = (region[:, None] == jnp.arange(lengths.shape[1], dtype=jnp.int32)[None, :]).astype(
        jnp.int32
    )
    begins = jnp.sum(members[None] * offsets[:, None, :], axis=2)
    spans = jnp.sum(members[None] * lengths[:, None, :], axis=2)
    inside_doc = (inside[None] >= begins) & (inside[None] < begins + spans)
    labels = jnp.where(inside_doc, region[None], filler)
    return (positions, labels, inside_doc)


def allowed_pairs(query_side, key_side):
    same_doc = query_side[1][:, :, None] == key_side[1][:, None, :]
    causal = key_side[0][None, None, :] <= query_side[0][None, :, None]
    return same_doc & causal


def absorb(carry, query, key_piece, value_piece, allowed):
    run_max, run_sum, totals = carry
    scores = jnp.einsum(
        "mqhd,mkhd->mhqk", query, key_piece, preferred_element_type=jnp.float32
    ) * HEAD_DIM ** (-0.5)
    scores = jnp.where(allowed[:, None], scores, -1e30)
    new_max = jnp.maximum(run_max, jnp.max(scores, axis=-1))
    factor = jnp.exp(run_max - new_max)
    weights = jnp.where(allowed[:, None], jnp.exp(scores - new_max[..., None]), 0.0)
    run_sum = run_sum * factor + jnp.sum(weights, axis=-1)
    totals = totals * factor[..., None] + jnp.einsum(
        "mhqk,mkhd->mhqd", weights, value_piece.astype(jnp.float32)
    )
    return (new_max, run_sum, totals)


def hop_grads(query, grad_att, lse, delta, key_piece, value_piece, allowed):
    scores = jnp.einsum(
        "mqhd,mkhd->mhqk", query, key_piece, preferred_element_type=jnp.float32
    ) * HEAD_DIM ** (-0.5)
    probs = jnp.where(allowed[:, None], jnp.exp(scores - lse[..., None]), 0.0)
    grad_value = jnp.einsum("mhqk,mqhd->mkhd", probs, grad_att.astype(jnp.float32))
    grad_probs = jnp.einsum(
        "mqhd,mkhd->mhqk", grad_att, value_piece, preferred_element_type=jnp.float32
    )
    grad_scores = probs * (grad_probs - delta[..., None]) * HEAD_DIM ** (-0.5)
    grad_query = jnp.einsum("mhqk,mkhd->mqhd", grad_scores, key_piece.astype(jnp.float32))
    grad_key = jnp.einsum("mhqk,mqhd->mkhd", grad_scores, query.astype(jnp.float32))
    return (grad_query, grad_key, grad_value)


def shards(
    layer_input,
    cotangent,
    doc_len,
    doc_offset,
    w_query,
    w_key,
    w_value,
    w_out,
    w_gate_attn,
    w_gate_ffn,
    w_in,
    w_back,
    norm_attn,
    norm_ffn,
    bias_attn,
    bias_ffn,
):
    gathered = (
        lax.all_gather(w_query, ("dp", "seq"), axis=0, tiled=True),
        lax.all_gather(w_key, ("dp", "seq"), axis=0, tiled=True),
        lax.all_gather(w_value, ("dp", "seq"), axis=0, tiled=True),
        lax.all_gather(w_out, ("dp", "seq"), axis=0, tiled=True),
        lax.all_gather(w_gate_attn, ("dp", "seq"), axis=0, tiled=True),
        lax.all_gather(w_gate_ffn, ("dp", "seq"), axis=0, tiled=True),
        lax.all_gather(w_in, ("dp", "seq"), axis=0, tiled=True),
        lax.all_gather(w_back, ("dp", "seq"), axis=0, tiled=True),
        lax.all_gather(norm_attn, ("dp", "seq"), axis=0, tiled=True),
        lax.all_gather(norm_ffn, ("dp", "seq"), axis=0, tiled=True),
        lax.all_gather(bias_attn, ("dp", "seq"), axis=0, tiled=True),
        lax.all_gather(bias_ffn, ("dp", "seq"), axis=0, tiled=True),
    )
    (
        full_query,
        full_key,
        full_value,
        full_out,
        full_gate_attn,
        full_gate_ffn,
        full_in,
        full_back,
        gain_attn,
        gain_ffn,
        shift_attn,
        shift_ffn,
    ) = gathered
    micro = layer_input.shape[0]
    rows = layer_input.shape[2]
    width = layer_input.shape[3]
    tokens = micro * rows
    nseq = lax.axis_size("seq")
    me_index = lax.axis_index("seq")
    hops = min(max(DOC_MAX // rows, 1), nseq) - 1
    lengths = doc_len[:, 0]
    offsets = doc_offset[:, 0]

    def key_side(source):
        positions, labels, _ = layout_of(lengths, offsets, source, rows, -2)
        return (positions, labels)

    own_layout = layout_of(lengths, offsets, me_index, rows, -1)
    query_side = (own_layout[0], own_layout[1])
    own_keys = key_side(me_index)
    inputs = layer_input[:, 0].reshape(tokens, width).astype(jnp.float32)
    normed_attn, pull_attn = jax.vjp(rms_norm, inputs, gain_attn.astype(jnp.float32))
    normed_low = normed_attn.astype(jnp.bfloat16)
    query = dense(normed_low, full_query).astype(jnp.bfloat16)
    keys = dense(normed_low, full_key).astype(jnp.bfloat16)
    values = dense(normed_low, full_value).astype(jnp.bfloat16)
    gate_attn = jax.nn.sigmoid(dense(normed_low, full_gate_attn) + shift_attn.astype(jnp.float32))
    head_shape = (micro, rows, HEADS, HEAD_DIM)
    query_h = query.reshape(head_shape)
    keys_h = keys.reshape(head_shape)
    values_h = values.reshape(head_shape)
    start_carry = (
        jnp.full((micro, HEADS, rows), -1e30, jnp.float32),
        jnp.zeros((micro, HEADS, rows), jnp.float32),
        jnp.zeros((micro, HEADS, rows, HEAD_DIM), jnp.float32),
    )
    carry = absorb(start_carry, query_h, keys_h, values_h, allowed_pairs(query_side, own_keys))

    def forward_hop(hop, state):
        pieces, inner = state
        pieces = from_behind((pieces[0], pieces[1]), "seq", 1)
        source = me_index - hop
        inner = absorb(
            inner, query_h, pieces[0], pieces[1], allowed_pairs(query_side, key_side(source))
        )
        return (pieces, inner)

    _, (run_max, run_sum, totals) = lax.fori_loop(
        1, hops + 1, forward_hop, ((keys_h, values_h), carry)
    )
    live = own_layout[2][:, None, :]
    safe_sum = jnp.where(live, run_sum, 1.0)
    attended_h = jnp.where(live[..., None], totals / safe_sum[..., None], 0.0)
    lse = jnp.where(live, run_max + jnp.log(safe_sum), 0.0)
    attended32 = attended_h.transpose(0, 2, 1, 3).reshape(tokens, width)
    attended = attended32.astype(jnp.bfloat16)
    branch_attn = dense(attended, full_out)
    hidden = gate_attn * branch_attn + (1.0 - gate_attn) * inputs
    normed_ffn, pull_ffn = jax.vjp(rms_norm, hidden, gain_ffn.astype(jnp.float32))
    normed_ffn_low = normed_ffn.astype(jnp.bfloat16)
    pre = dense(normed_ffn_low, full_in)
    act32, pull_gelu = jax.vjp(partial(jax.nn.gelu, approximate=True), pre)
    act = act32.astype(jnp.bfloat16)
    branch_ffn = dense(act, full_back)
    gate_ffn = jax.nn.sigmoid(dense(normed_ffn_low, full_gate_ffn) + shift_ffn.astype(jnp.float32))
    output = gate_ffn * branch_ffn + (1.0 - gate_ffn) * hidden
    again = (
        lax.all_gather(w_query, ("dp", "seq"), axis=0, tiled=True),
        lax.all_gather(w_key, ("dp", "seq"), axis=0, tiled=True),
        lax.all_gather(w_value, ("dp", "seq"), axis=0, tiled=True),
        lax.all_gather(w_out, ("dp", "seq"), axis=0, tiled=True),
        lax.all_gather(w_gate_attn, ("dp", "seq"), axis=0, tiled=True),
        lax.all_gather(w_gate_ffn, ("dp", "seq"), axis=0, tiled=True),
        lax.all_gather(w_in, ("dp", "seq"), axis=0, tiled=True),
        lax.all_gather(w_back, ("dp", "seq"), axis=0, tiled=True),
        lax.all_gather(norm_attn, ("dp", "seq"), axis=0, tiled=True),
        lax.all_gather(norm_ffn, ("dp", "seq"), axis=0, tiled=True),
        lax.all_gather(bias_attn, ("dp", "seq"), axis=0, tiled=True),
        lax.all_gather(bias_ffn, ("dp", "seq"), axis=0, tiled=True),
    )
    (
        back_query,
        back_key,
        back_value,
        back_out,
        back_gate_attn,
        back_gate_ffn,
        back_in,
        back_back,
        _,
        _,
        _,
        _,
    ) = again
    upstream = cotangent[:, 0].reshape(tokens, width).astype(jnp.float32)
    d_logit_ffn = (upstream * (branch_ffn - hidden) * gate_ffn * (1.0 - gate_ffn)).astype(
        jnp.bfloat16
    )
    d_branch_ffn = (upstream * gate_ffn).astype(jnp.bfloat16)
    grad_back = dense_tn(act, d_branch_ffn)
    (d_pre32,) = pull_gelu(dense_nt(d_branch_ffn, back_back))
    d_pre = d_pre32.astype(jnp.bfloat16)
    grad_in = dense_tn(normed_ffn_low, d_pre)
    grad_gate_ffn = dense_tn(normed_ffn_low, d_logit_ffn)
    grad_bias_ffn = jnp.sum(d_logit_ffn.astype(jnp.float32), axis=0)
    d_normed_ffn = dense_nt(d_pre, back_in) + dense_nt(d_logit_ffn, back_gate_ffn)
    d_hidden_norm, grad_gain_ffn = pull_ffn(d_normed_ffn)
    d_hidden = upstream * (1.0 - gate_ffn) + d_hidden_norm
    d_branch_attn = (d_hidden * gate_attn).astype(jnp.bfloat16)
    d_logit_attn = (d_hidden * (branch_attn - inputs) * gate_attn * (1.0 - gate_attn)).astype(
        jnp.bfloat16
    )
    grad_out = dense_tn(attended, d_branch_attn)
    d_attended = dense_nt(d_branch_attn, back_out).astype(jnp.bfloat16)
    grad_att = d_attended.reshape(head_shape)
    delta = jnp.einsum(
        "mqhd,mqhd->mhq", grad_att.astype(jnp.float32), attended32.reshape(head_shape)
    )
    first_q, first_k, first_v = hop_grads(
        query_h, grad_att, lse, delta, keys_h, values_h, allowed_pairs(query_side, own_keys)
    )

    def backward_hop(hop, state):
        pieces, moving, grad_q = state
        pieces = from_behind((pieces[0], pieces[1]), "seq", 1)
        moving = (
            passed_along(moving[0].astype(jnp.bfloat16), "seq", 1).astype(jnp.float32),
            passed_along(moving[1].astype(jnp.bfloat16), "seq", 1).astype(jnp.float32),
        )
        source = me_index - hop
        step_q, step_k, step_v = hop_grads(
            query_h,
            grad_att,
            lse,
            delta,
            pieces[0],
            pieces[1],
            allowed_pairs(query_side, key_side(source)),
        )
        return (pieces, (moving[0] + step_k, moving[1] + step_v), grad_q + step_q)

    _, moving, grad_q = lax.fori_loop(
        1, hops + 1, backward_hop, ((keys_h, values_h), (first_k, first_v), first_q)
    )
    moving = (
        passed_along(moving[0].astype(jnp.bfloat16), "seq", -hops).astype(jnp.float32),
        passed_along(moving[1].astype(jnp.bfloat16), "seq", -hops).astype(jnp.float32),
    )
    grad_k, grad_v = moving
    d_query = grad_q.reshape(tokens, width).astype(jnp.bfloat16)
    d_key = grad_k.reshape(tokens, width).astype(jnp.bfloat16)
    d_value = grad_v.reshape(tokens, width).astype(jnp.bfloat16)
    grad_query = dense_tn(normed_low, d_query)
    grad_key = dense_tn(normed_low, d_key)
    grad_value = dense_tn(normed_low, d_value)
    grad_gate_attn = dense_tn(normed_low, d_logit_attn)
    grad_bias_attn = jnp.sum(d_logit_attn.astype(jnp.float32), axis=0)
    d_normed_attn = (
        dense_nt(d_query, back_query)
        + dense_nt(d_key, back_key)
        + dense_nt(d_value, back_value)
        + dense_nt(d_logit_attn, back_gate_attn)
    )
    d_inputs_norm, grad_gain_attn = pull_attn(d_normed_attn)
    grad_input = d_hidden * (1.0 - gate_attn) + d_inputs_norm
    owned = (
        lax.psum_scatter(grad_query, ("dp", "seq"), scatter_dimension=0, tiled=True),
        lax.psum_scatter(grad_key, ("dp", "seq"), scatter_dimension=0, tiled=True),
        lax.psum_scatter(grad_value, ("dp", "seq"), scatter_dimension=0, tiled=True),
        lax.psum_scatter(grad_out, ("dp", "seq"), scatter_dimension=0, tiled=True),
        lax.psum_scatter(grad_gate_attn, ("dp", "seq"), scatter_dimension=0, tiled=True),
        lax.psum_scatter(grad_gate_ffn, ("dp", "seq"), scatter_dimension=0, tiled=True),
        lax.psum_scatter(grad_in, ("dp", "seq"), scatter_dimension=0, tiled=True),
        lax.psum_scatter(grad_back, ("dp", "seq"), scatter_dimension=0, tiled=True),
        lax.psum_scatter(grad_gain_attn, ("dp", "seq"), scatter_dimension=0, tiled=True),
        lax.psum_scatter(grad_gain_ffn, ("dp", "seq"), scatter_dimension=0, tiled=True),
        lax.psum_scatter(grad_bias_attn, ("dp", "seq"), scatter_dimension=0, tiled=True),
        lax.psum_scatter(grad_bias_ffn, ("dp", "seq"), scatter_dimension=0, tiled=True),
    )
    return (
        output.reshape(micro, 1, rows, width).astype(jnp.bfloat16),
        grad_input.reshape(micro, 1, rows, width),
        owned[0],
        owned[1],
        owned[2],
        owned[3],
        owned[4],
        owned[5],
        owned[6],
        owned[7],
        owned[8],
        owned[9],
        owned[10],
        owned[11],
    )


def solution(mesh):
    placed = (
        P(None, "dp", "seq", None),
        P(None, "dp", "seq", None),
        P(None, "dp", None),
        P(None, "dp", None),
        P(("dp", "seq"), None),
        P(("dp", "seq"), None),
        P(("dp", "seq"), None),
        P(("dp", "seq"), None),
        P(("dp", "seq"), None),
        P(("dp", "seq"), None),
        P(("dp", "seq"), None),
        P(("dp", "seq"), None),
        P(("dp", "seq")),
        P(("dp", "seq")),
        P(("dp", "seq")),
        P(("dp", "seq")),
    )
    def pick(layer_input, *others):
        micro, _, rows, width = layer_input.shape
        fits = (
            dict(mesh.shape) == {"dp": 4, "seq": 8}
            and micro == 2
            and others[1].shape[2] == 1
            and width == HEADS * HEAD_DIM
            and width == 4 * LANES
            and rows % 128 == 0
            and others[10].shape == (width // 8, width)
        )
        return (by_heads if fits else shards)(layer_input, *others)

    return jax.shard_map(
        pick,
        mesh=mesh,
        in_specs=placed,
        out_specs=(
            P(None, "dp", "seq", None),
            P(None, "dp", "seq", None),
            P(("dp", "seq"), None),
            P(("dp", "seq"), None),
            P(("dp", "seq"), None),
            P(("dp", "seq"), None),
            P(("dp", "seq"), None),
            P(("dp", "seq"), None),
            P(("dp", "seq"), None),
            P(("dp", "seq"), None),
            P(("dp", "seq")),
            P(("dp", "seq")),
            P(("dp", "seq")),
            P(("dp", "seq")),
        ),
        check_vma=False,
    )
```

```python
from functools import partial

import jax
import jax.numpy as jnp
from jax import lax
from jax.experimental import pallas as pl
from jax.experimental.pallas import tpu as pltpu
from jax.sharding import PartitionSpec as P

HEADS = 8
HEAD_DIM = 64
DOC_MAX = 4096

EPS = 1e-05
MESH = pl.DeviceIdType.MESH
BF = jnp.bfloat16
F32 = jnp.float32
VMEM_LIMIT = 66_000_000
LANES = 128
SIDE = 64
GELU_C = 0.7978845608028654
GELU_A = 0.044715
NEG = -1e30
ANY = pl.BlockSpec(memory_space=pl.ANY)
INVM = pl.BlockSpec(memory_space=pltpu.VMEM)
INSM = pl.BlockSpec(memory_space=pltpu.SMEM)


def nn(a, b):
    return lax.dot_general(a, b, (((1,), (0,)), ((), ())), preferred_element_type=F32)


def nt(a, b):
    return lax.dot_general(a, b, (((1,), (1,)), ((), ())), preferred_element_type=F32)


def tn(a, b):
    return lax.dot_general(a, b, (((0,), (0,)), ((), ())), preferred_element_type=F32)


def remote(src, dst, send, recv, dp, seq):
    return pltpu.make_async_remote_copy(
        src_ref=src, dst_ref=dst, send_sem=send, recv_sem=recv,
        device_id=(dp, seq), device_id_type=MESH,
    )


def greet(peers):
    barrier = pltpu.get_barrier_semaphore()
    for dp, seq in peers:
        pl.semaphore_signal(barrier, inc=1, device_id=(dp, seq), device_id_type=MESH)
    pl.semaphore_wait(barrier, len(peers))


def place():
    d = lax.axis_index("dp")
    j = lax.axis_index("seq")
    z = j // 2
    c = j % 2
    dx = d + 1 - 2 * (d % 2)
    dy = (d + 2) % 4
    dxy = 3 - d
    return d, j, z, c, dx, dy, dxy


CK = 4


class Spread:
    def __init__(self, dst, send, recv):
        self.dst, self.send, self.recv = dst, send, recv
        self.at = place()
        self.count = 0
        self.sent = []
        d, j, z, c, dx, dy, dxy = self.at
        self.pj = j + 1 - 2 * c
        self.lines = (z, z + 1 - 2 * (z % 2), (z + 2) % 4, 3 - z)
        self.slots = {
            dp: [where * 8 + 2 * zz + c for zz in self.lines]
            for dp, where in (("d", d), ("x", dx), ("y", dy), ("xy", dxy))
        }

    def make(self, slot, i, dp, seq, src=None):
        return remote(
            self.dst.at[slot] if src is None else src, self.dst.at[slot],
            self.send.at[i], self.recv.at[slot], dp, seq,
        )

    def put(self, slot, dp, seq, src=None):
        i = self.count
        self.count += 1
        self.make(slot, i, dp, seq, src).start()
        self.sent.append((slot, i))

    def arrive(self, slot):
        self.make(slot, 0, self.at[0], self.pj).wait_recv()

    def in_plane(self, src):
        d, j, z, c, dx, dy, dxy = self.at
        for dp, seq in ((dx, j), (dy, j), (d, self.pj)):
            self.put(self.slots["d"][0], dp, seq, src)

    def along(self, srcs):
        d, j, z, c, dx, dy, dxy = self.at
        for zz, src in zip(self.lines[1:], srcs):
            self.put(self.slots["d"][0], d, 2 * zz + c, src)

    def from_line(self, k):
        d, j, z, c, dx, dy, dxy = self.at
        slot = self.slots["d"][k]
        self.arrive(slot)
        for dp, seq in ((dx, j), (dy, j), (d, self.pj)):
            self.put(slot, dp, seq)

    def from_plane(self, k):
        d, j, z, c, dx, dy, dxy = self.at
        sx, sy = self.slots["x"][k], self.slots["y"][k]
        for slot in (sx, sy):
            self.arrive(slot)
            self.put(slot, d, self.pj)
        even = self.lines[k] % 2 == 0
        i = self.count
        self.count += 1
        self.sent.append((sx, i))

        @pl.when(even)
        def _():
            self.make(sx, i, dy, j).start()

        @pl.when(jnp.logical_not(even))
        def _():
            self.make(sy, i, dx, j).start()

    def from_corner(self):
        for slot in self.slots["xy"]:
            self.arrive(slot)
            self.put(slot, self.at[0], self.pj)

    def from_core(self):
        c = self.at[3]
        for slots in self.slots.values():
            for slot in slots:
                self.arrive(slot + 1 - 2 * c)

    def wait_sent(self):
        for slot, i in self.sent:
            self.make(slot, i, self.at[0], self.pj).wait_send()


LOG2E = 1.4426950408889634


def lane_of(rows):
    return lax.broadcasted_iota(jnp.int32, (rows, LANES), 1)


def three(v):
    a = v.astype(BF).astype(F32)
    b = (v - a).astype(BF).astype(F32)
    return a, b, v - a - b


def beside(h, lane, values, parts):
    first = SIDE * (1 - h)
    own = (lane < SIDE) if h == 0 else (lane >= SIDE)
    out = jnp.where(own, values, 0.0)
    for k, part in enumerate(parts):
        if part is not None:
            out = jnp.where(lane == first + k, part, out)
    return out.astype(BF)


def upper(rows):
    return lax.broadcasted_iota(jnp.int32, (rows, rows), 0) <= lax.broadcasted_iota(
        jnp.int32, (rows, rows), 1
    )


def front_kernel(
    doc_len, doc_off, x_ref, wq, wk, wv, wo, wga, wgf, win, wback, small_ref,
    xg, wg, w_ref, vec_ref, att, o32_ref, qa, ka, va,
    hv, hg, sv, vt, top, acc, ov,
    lsem, xsem, hsend, hrecv, wsend, wrecv, xsend, xrecv, ssend, srecv,
):
    blocks, rows, width = xg.shape
    per = wq.shape[0]
    d, j, z, c, dx, dy, dxy = place()
    me = d * 8 + j
    g = z // 2
    pj = j + 1 - 2 * c
    za, zb, zc = z + 1 - 2 * (z % 2), (z + 2) % 4, 3 - z
    ja = 2 * za + c
    near = jnp.logical_or(z == 1, z == 2)
    far = jnp.logical_or(z == 0, z == 3)
    loads = []
    pieces = [(m, hv.at[k * per : (k + 1) * per]) for k, m in enumerate((wq, wk, wv))]
    pieces += [(m, sv.at[k * per : (k + 1) * per]) for k, m in enumerate((wo, wga, wgf))]
    ff = win.shape[1] // width
    for k in range(ff):
        pieces.append((win.at[:, k * width : (k + 1) * width], sv.at[(3 + k) * per : (4 + k) * per]))
    pieces.append((wback, sv.at[(3 + ff) * per :]))
    for k, (src, dst) in enumerate(pieces):
        loads.append(pltpu.make_async_copy(src, dst, lsem.at[k]))
        loads[-1].start()
    own = pltpu.make_async_copy(x_ref.at[g], xg.at[j], xsem)
    own.start()
    lanes = lax.broadcasted_iota(jnp.int32, (LANES, LANES), 1)
    subs = lax.broadcasted_iota(jnp.int32, (LANES, LANES), 0)
    row = lax.broadcasted_iota(jnp.int32, (16, LANES), 0)
    tile = jnp.zeros((16, LANES), F32)
    for k in range(4):
        spot = jnp.where(lanes + k * LANES == me * per + subs, 1.0, 0.0).astype(BF)
        tile = jnp.where(row // 4 == k, nn(small_ref[...], spot), tile)
    for k in range(4):
        hv[3 * per :, k * LANES : (k + 1) * LANES] = tile.astype(BF)
    for k in range(3):
        loads[k].wait()
    greet([(d, (j + k) % 8) for k in range(1, 8)] + [(dx, j), (dy, j), (dxy, j)])

    weights = Spread(wg, wsend, wrecv)

    def mine(seq):
        return hv.at[:, pl.ds(pl.multiple_of(LANES * (seq % 4), LANES), LANES)]

    def hcopy(k):
        seq = (j + k) % 8
        return remote(mine(seq), hg.at[me], hsend.at[k], hrecv.at[j], d, seq)

    def lcopy(k, dp):
        line = hg.at[pl.ds(d * 8, 8)]
        return remote(line, line, hsend.at[8 + k], hrecv.at[8 + k], dp, j)

    for k in range(1, 8):
        hcopy(k).start()

    def xcopy(k, part, block, dp, seq, src=None):
        piece = pl.ds(part * (rows // CK), rows // CK)
        source = xg.at[block, piece] if src is None else x_ref.at[src, piece]
        return remote(source, xg.at[block, piece], xsend.at[k, part], xrecv.at[block, part], dp, seq)

    def xarrive(block):
        for part in range(CK):
            xcopy(0, part, block, d, pj).wait_recv()

    jn = 2 * (2 - g) + c
    for part in range(CK):
        xcopy(0, part, j, d, ja, g).start()
        xcopy(1, part, j, d, pj, g).start()
    for part in range(CK):
        xcopy(2, part, j, d, jn, 1 - g).start()
    keep_h = pltpu.make_async_copy(mine(j), hg.at[me], lsem.at[1])
    keep_h.start()
    for copy in loads[3:]:
        copy.wait()
    keep = pltpu.make_async_copy(sv, wg.at[me], lsem.at[0])
    keep.start()
    weights.in_plane(sv)

    weights.along([sv] * 3)
    keep_h.wait()
    for k in range(1, 8):
        seq = (j + k) % 8
        remote(mine(seq), hg.at[d * 8 + seq], hsend.at[k], hrecv.at[seq], d, seq).wait_recv()
    for k, dp in enumerate((dx, dy, dxy)):
        lcopy(k, dp).start()
    for k, dp in enumerate((dx, dy, dxy)):
        line = hg.at[pl.ds(dp * 8, 8)]
        remote(line, line, hsend.at[8 + k], hrecv.at[8 + k], dp, j).wait_recv()

    vecs = jnp.zeros((16, LANES), F32)
    for k in range(32):
        vecs += hg[k, 3 * per :].astype(F32)
    for k in range(4):
        vec_ref[:, k * LANES : (k + 1) * LANES] = vecs[4 * k : 4 * k + 4]
    for k in range(3):
        w_ref[:, k * LANES : (k + 1) * LANES] = hg[:, k * per : (k + 1) * per, :].reshape(width, LANES)

    off = doc_off[g, 0, 0]
    end = off + doc_len[g, 0, 0]
    lane = lane_of(rows)
    up = lax.broadcasted_iota(jnp.int32, (rows, 1), 0)
    along = lax.broadcasted_iota(jnp.int32, (1, rows), 1)
    tall = lax.broadcasted_iota(jnp.int32, (16, rows), 0)
    ones = jnp.where(tall == 0, 1.0, 0.0).astype(BF)

    def project(b):
        x = xg[b].astype(F32)
        n = (x * lax.rsqrt(jnp.mean(x * x, -1, keepdims=True) + EPS) * vec_ref[0:1]).astype(BF)
        p = nn(n, w_ref[...])
        pos = b * rows + up
        bad = jnp.where(jnp.logical_and(pos >= off, pos < end), 0.0, NEG)
        q = p[:, :LANES] * (HEAD_DIM ** (-0.5) * LOG2E)
        k = p[:, LANES : 2 * LANES]
        v = p[:, 2 * LANES :]
        for h in range(2):
            qa[h, b] = beside(h, lane, q, (1.0,))
            ka[h, b] = beside(h, lane, k, (bad, 1.0, 1.0, 1.0))
            va[h, b] = beside(h, lane, v, (None, 1.0, 1.0, 1.0))
        turned = v.astype(BF).T
        for h in range(2):
            vt[h, b, :SIDE] = turned[h * SIDE : (h + 1) * SIDE]
            vt[h, b, SIDE:] = ones

    def project_two(base):
        def body(k, _):
            project(base + k)
            return 0

        lax.fori_loop(0, 2, body, 0)

    z1 = 2 - g
    z2 = 3 * (1 - g)
    b1, b2 = 2 * z1 + c, 2 * z2 + c
    own.wait()
    xarrive(pj)
    project_two(2 * z)
    for part in range(CK):
        xcopy(0, part, ja, d, pj).wait_recv()
        xcopy(3, part, ja, d, pj).start()

        @pl.when(near)
        def _():
            xcopy(0, part, b1, d, pj).wait_recv()
            xcopy(6, part, b1, d, ja).start()
            xcopy(4, part, b1, d, pj).start()

    xarrive(ja + 1 - 2 * c)
    project_two(2 * za)

    keep_low = upper(rows)
    sub = lax.broadcasted_iota(jnp.int32, (SIDE, rows), 0)

    def scores(q, k):
        return [nt(ka[h, k], qa[h, q]) for h in range(2)]

    def first(q):
        ss = [jnp.where(keep_low, s, NEG) for s in scores(q, q)]
        new = [jnp.max(s, 0, keepdims=True) for s in ss]
        ps = [jnp.exp2(s - n).astype(BF) for s, n in zip(ss, new)]
        for h in range(2):
            top[h, q] = new[h]
            acc[h, q] = nn(vt[h, q], ps[h])

    def pair(q, k):
        ss = scores(q, k)
        old = [top[h, q] for h in range(2)]
        new = [jnp.maximum(old[h], jnp.max(ss[h], 0, keepdims=True)) for h in range(2)]
        ps = [jnp.exp2(ss[h] - new[h]).astype(BF) for h in range(2)]
        for h in range(2):
            top[h, q] = new[h]
            acc[h, q] = acc[h, q] * jnp.exp2(old[h] - new[h]) + nn(vt[h, k], ps[h])

    def acopy(q):
        return remote(ov.at[q], att.at[j], ssend.at[q], srecv.at[j], d, q)

    def finish(b):
        pos = b * rows + along
        live = jnp.logical_and(pos >= off, pos < end)
        outs = []
        for h in range(2):
            total = acc[h, b, SIDE : SIDE + 1]
            lse = jnp.where(live, top[h, b] + jnp.log2(total), -NEG)
            mine = jnp.where(live, acc[h, b, :SIDE] / total, 0.0)
            parts = three(lse)
            beyond = jnp.zeros((SIDE, rows), F32)
            for k in range(3):
                beyond = jnp.where(sub == k + 1, -parts[k], beyond)
            both = (mine, beyond) if h == 0 else (beyond, mine)
            out = jnp.concatenate(both, axis=0).T
            start = SIDE * (1 - h)
            aug = jnp.logical_and(lane > start, lane < start + 4)
            qa[h, b] = jnp.where(aug, out, qa[h, b].astype(F32)).astype(BF)
            outs.append(out)
        out = jnp.where(lane < SIDE, outs[0], outs[1])
        o32_ref[b] = out
        ov[b] = out.astype(BF)

        @pl.when(b != j)
        def _():
            acopy(b).start()

    def outer(i, _):
        @pl.when(i == 1)
        def _():
            weights.from_plane(0)

        @pl.when(i == 3)
        def _():
            @pl.when(near)
            def _():
                for part in range(CK):
                    xcopy(0, part, b2, d, pj).wait_recv()
                    xcopy(7, part, b2, d, ja).start()
                    xcopy(5, part, b2, d, pj).start()

            weights.from_line(1)

        @pl.when(i == 4)
        def _():
            @pl.when(far)
            def _():
                for part in range(CK):
                    xcopy(0, part, b1, d, pj).wait_recv()
                    xcopy(4, part, b1, d, pj).start()

            xarrive(b1 + 1 - 2 * c)

        pl.when(i == 5)(partial(weights.from_plane, 1))

        @pl.when(i == 6)
        def _():
            weights.from_line(3)

            @pl.when(far)
            def _():
                for part in range(CK):
                    xcopy(0, part, b2, d, pj).wait_recv()
                    xcopy(5, part, b2, d, pj).start()

            xarrive(b2 + 1 - 2 * c)
            weights.from_plane(2)

        @pl.when(jnp.logical_or(i == 4, i == 6))
        def _():
            project_two(2 * (z1 + (z2 - z1) * ((i - 4) // 2)))

        pl.when(i == 5)(partial(weights.from_line, 2))
        pl.when(i == 7)(partial(weights.from_plane, 3))
        pl.when(i == 8)(weights.from_corner)
        tail = i >= blocks
        o = jnp.where(g == 0, i, jnp.where(tail, i - 4, blocks - 1 - i))
        early = jnp.where(jnp.logical_or(g == 0, i < 4), i, i - 4)
        count = jnp.where(tail, 4 * g, early)
        out_now = jnp.logical_and(g == 1, i == blocks - 1)

        @pl.when(jnp.logical_not(tail))
        def _():
            first(o)

        pl.when(i == 7 * g)(lambda: finish(o))

        def inner(t, _):
            q = jnp.where(jnp.logical_or(g == 0, tail), o, o + 1 + t)
            k = jnp.where(g == 0, o - 1 - t, jnp.where(tail, t, o))
            pair(q, k)
            ends = jnp.logical_and(jnp.logical_or(g == 0, tail), t == count - 1)
            pl.when(jnp.logical_or(out_now, ends))(lambda: finish(q))
            return 0

        lax.fori_loop(0, count, inner, 0)
        return 0

    lax.fori_loop(0, blocks + 4, outer, 0)
    att[j] = ov[j]
    weights.from_core()
    for k in range(1, 8):
        q = (j + k) % 8
        remote(ov.at[q], att.at[q], ssend.at[q], srecv.at[q], d, q).wait_recv()
    for k in range(1, 8):
        hcopy(k).wait_send()
    for k, dp in enumerate((dx, dy, dxy)):
        lcopy(k, dp).wait_send()
    weights.wait_sent()
    for k in range(6):
        for part in range(CK):
            xcopy(k, part, j, d, pj).wait_send()

    @pl.when(near)
    def _():
        for k in (6, 7):
            for part in range(CK):
                xcopy(k, part, j, d, pj).wait_send()

    for k in range(1, 8):
        acopy((j + k) % 8).wait_send()
    keep.wait()


def front(doc_len, doc_off, x, mats, small):
    _, rows, width = x.shape
    per = mats[0].shape[0]
    blocks = 8
    tall = sum(m.shape[0] * (m.shape[1] // width) for m in mats[3:])
    side = jax.ShapeDtypeStruct((2, blocks, rows, LANES), BF)
    dma = pltpu.SemaphoreType.DMA
    return pl.pallas_call(
        front_kernel,
        out_shape=(
            jax.ShapeDtypeStruct((blocks, rows, width), BF),
            jax.ShapeDtypeStruct((32, tall, width), BF),
            jax.ShapeDtypeStruct((width, 3 * LANES), BF),
            jax.ShapeDtypeStruct((4, width), F32),
            jax.ShapeDtypeStruct((blocks, rows, LANES), BF),
            jax.ShapeDtypeStruct((blocks, rows, LANES), F32),
            side, side, side,
        ),
        in_specs=[INSM, INSM] + [ANY] * 9 + [INVM],
        out_specs=(INVM, ANY) + (INVM,) * 7,
        scratch_shapes=[
            pltpu.VMEM((3 * per + 16, width), BF),
            pltpu.VMEM((32, 3 * per + 16, LANES), BF),
            pltpu.VMEM((tall, width), BF),
            pltpu.VMEM((2, blocks, SIDE + 16, rows), BF),
            pltpu.VMEM((2, blocks, 1, rows), F32),
            pltpu.VMEM((2, blocks, SIDE + 16, rows), F32),
            pltpu.VMEM((blocks, rows, LANES), BF),
            dma((12,)), dma, dma((11,)), dma((11,)), dma((32,)), dma((32,)),
            dma((8, CK)), dma((8, CK)), dma((8,)), dma((8,)),
        ],
        compiler_params=pltpu.CompilerParams(
            collective_id=0, has_side_effects=True, vmem_limit_bytes=VMEM_LIMIT
        ),
        name="front",
    )(doc_len, doc_off, x, *mats, small)


def token_kernel(
    x_ref, c_ref, a_ref, wg, vec, out_ref, do_ref, dh_ref, dn_ref, g_ref, v_ref,
    gp, act, da, dpres, g_out, g_ga, g_gf, g_in, g_back, send, recv,
):
    d, j = lax.axis_index("dp"), lax.axis_index("seq")
    g = j // 4
    rows, width = x_ref.shape[1:]
    ff = gp.shape[0]
    per = width // 32

    def weight(lo):
        return wg[:, lo : lo + per, :].reshape(width, width)

    def back(k):
        n = wg.shape[0] // ff
        return wg[k * n : (k + 1) * n, 7 * per : 7 * per + ff * per, :].reshape(width, width)

    for ref in (g_out, g_ga, g_gf, g_in, g_back, v_ref):
        ref[...] = jnp.zeros_like(ref)
    greet([(d, (j + k) % 8) for k in range(1, 8)])

    def dcopy(q):
        return remote(da.at[q], do_ref.at[j], send.at[q], recv.at[j], d, q)

    def one(t, _):
        m = (1 - g) * (1 - t) + g * t
        x = x_ref[m].astype(F32)
        gain_a, gain_f = vec[0:1].astype(F32), vec[1:2].astype(F32)
        shift_a, shift_f = vec[2:3].astype(F32), vec[3:4].astype(F32)
        n1 = x * lax.rsqrt(jnp.mean(x * x, -1, keepdims=True) + EPS)
        na = (n1 * gain_a).astype(BF)
        ga = jax.nn.sigmoid(nn(na, weight(per)) + shift_a)
        att = jnp.concatenate([a_ref[4 * m + i] for i in range(4)], axis=1)
        br = nn(att, weight(0))
        hid = ga * br + (1.0 - ga) * x
        r2 = lax.rsqrt(jnp.mean(hid * hid, -1, keepdims=True) + EPS)
        n2 = hid * r2
        nf = (n2 * gain_f).astype(BF)
        bf = jnp.zeros((rows, width), F32)
        for k in range(ff):
            pre = nn(nf, weight((3 + k) * per))
            sq = pre * pre
            t = jnp.tanh(GELU_C * pre * (1.0 + GELU_A * sq))
            half = 0.5 * (1.0 + t)
            act[k] = (pre * half).astype(BF)
            gp[k] = half + 0.5 * pre * (1.0 - t * t) * (GELU_C * (1.0 + 3.0 * GELU_A * sq))
            bf += nn(act[k], back(k))
        gf = jax.nn.sigmoid(nn(nf, weight(2 * per)) + shift_f)
        out_ref[m] = (gf * bf + (1.0 - gf) * hid).astype(BF)
        c = c_ref[m].astype(F32)
        dlf = (c * (bf - hid) * gf * (1.0 - gf)).astype(BF)
        dbf = (c * gf).astype(BF)
        dnf = nt(dlf, weight(2 * per))
        for k in range(ff):
            dpre = (nt(dbf, back(k)) * gp[k]).astype(BF)
            dpres[k] = dpre
            dnf += nt(dpre, weight((3 + k) * per))
        g2 = dnf * gain_f
        dh = c * (1.0 - gf) + r2 * (g2 - n2 * jnp.mean(g2 * n2, -1, keepdims=True))
        dba = (dh * ga).astype(BF)
        dla = (dh * (br - x) * ga * (1.0 - ga)).astype(BF)
        datt = nt(dba, weight(0)).astype(BF)
        for i in range(4):
            da[4 * m + i] = datt[:, i * LANES : (i + 1) * LANES]

            @pl.when(j != 4 * m + i)
            def _():
                dcopy(4 * m + i).start()

        dna = nt(dla, weight(per))
        g_out[...] += tn(att, dba)
        g_ga[...] += tn(na, dla)
        g_gf[...] += tn(nf, dlf)
        for k in range(ff):
            g_back[k] += tn(act[k], dbf)
            g_in[k] += tn(nf, dpres[k])
        dh_ref[m] = dh * (1.0 - ga)
        dn_ref[m] = dna
        v_ref[0:1] += jnp.sum(dna * n1, 0, keepdims=True)
        v_ref[1:2] += jnp.sum(dnf * n2, 0, keepdims=True)
        v_ref[2:3] += jnp.sum(dla.astype(F32), 0, keepdims=True)
        v_ref[3:4] += jnp.sum(dlf.astype(F32), 0, keepdims=True)
        return 0

    lax.fori_loop(0, 2, one, 0)

    def put(lo, value):
        g_ref[:, lo : lo + per, :] = value.astype(BF).reshape(32, per, width)

    put(0, g_out[...])
    put(per, g_ga[...])
    put(2 * per, g_gf[...])
    for k in range(ff):
        put((3 + k) * per, g_in[k])
        n = 32 // ff
        g_ref[k * n : (k + 1) * n, (3 + ff) * per :, :] = (
            g_back[k].astype(BF).reshape(n, ff * per, width)
        )
    do_ref[j] = da[j]
    for k in range(1, 8):
        q = (j + k) % 8
        remote(da.at[q], do_ref.at[q], send.at[q], recv.at[q], d, q).wait_recv()
        dcopy(q).wait_send()


def tokens(x, cot, att, wg, vec):
    micro, rows, width = x.shape
    ff = 4
    per = width // 32
    grads = (32, (3 + 2 * ff) * per, width)
    return pl.pallas_call(
        token_kernel,
        out_shape=(
            jax.ShapeDtypeStruct((micro, rows, width), BF),
            jax.ShapeDtypeStruct((4 * micro, rows, LANES), BF),
            jax.ShapeDtypeStruct((micro, rows, width), F32),
            jax.ShapeDtypeStruct((micro, rows, width), F32),
            jax.ShapeDtypeStruct(grads, BF),
            jax.ShapeDtypeStruct((8, width), F32),
        ),
        in_specs=[INVM] * 5,
        out_specs=(INVM,) * 6,
        scratch_shapes=[
            pltpu.VMEM((ff, rows, width), F32),
            pltpu.VMEM((ff, rows, width), BF),
            pltpu.VMEM((4 * micro, rows, LANES), BF),
            pltpu.VMEM((ff, rows, width), BF),
            pltpu.VMEM((width, width), F32),
            pltpu.VMEM((width, width), F32),
            pltpu.VMEM((width, width), F32),
            pltpu.VMEM((ff, width, width), F32),
            pltpu.VMEM((ff, width, width), F32),
            pltpu.SemaphoreType.DMA((8,)),
            pltpu.SemaphoreType.DMA((8,)),
        ],
        compiler_params=pltpu.CompilerParams(
            collective_id=1, has_side_effects=True, vmem_limit_bytes=VMEM_LIMIT
        ),
        name="tokens",
    )(x, cot, att, wg, vec)


def add_into(dst, src):
    rows = dst.shape[0]
    n = rows // 16
    per = 16 * max(k for k in range(1, 9) if n % k == 0)

    def body(i, _):
        piece = pl.ds(i * per, per)
        dst[piece, :] += src[piece, :]
        return 0

    lax.fori_loop(0, rows // per, body, 0)


def attend_back_kernel(
    x_ref, w_ref, gain_ref, o32_ref, do_ref, qa, ka, va, sum_ref, g_ref,
    dn_ref, gf_ref, gq_ref, gv_ref,
    da, qt, kt, dot, dq, dk, dv, dw, pb, hs_buf, vs_buf,
    acc, b1, b2, b3, b4, q1, q2, hb, vb, own,
    l2, lo, s1, r1, s2, r2, s3, r3, s4, r4, ps, pr, ts, tr, us, ur, hs, hr, vs, vr,
):
    blocks, rows, width = x_ref.shape
    per = width // 32
    d, j, z, c, dx, dy, dxy = place()
    me = d * 8 + j
    g = z // 2
    pj = j + 1 - 2 * c
    za, zb, zc = z + 1 - 2 * (z % 2), (z + 2) % 4, 3 - z
    ja, jb, jc = 2 * za + c, 2 * zb + c, 2 * zc + c
    near = jnp.logical_or(z == 1, z == 2)
    far = jnp.logical_or(z == 0, z == 3)
    w3, w2, wn, wf = 3 * (1 - g), 2 - g, 1 + g, 3 * g
    first = [(zz, dp) for zz in range(4) for dp in ((dx, dxy) if zz % 2 == 0 else (dy, dxy))]
    rest = [(zz, dp) for zz in range(4) for dp in ((d, dy) if zz % 2 == 0 else (d, dx))]

    gloads = []
    for k, (zz, dp) in enumerate(first + rest):
        copy = pltpu.make_async_copy(g_ref.at[dp * 8 + 2 * zz + c], acc.at[dp * 4 + zz], l2.at[k])
        copy.start()
        gloads.append(copy)

    barrier = pltpu.get_barrier_semaphore()

    def hello(k, _):
        slot = (me + k) % 32
        pl.semaphore_signal(
            barrier, inc=1, device_id=(slot // 8, slot % 8), device_id_type=MESH
        )
        return 0

    lax.fori_loop(1, 32, hello, 0)
    pl.semaphore_wait(barrier, 31)

    def gcopy(zz, dp):
        i = dp * 4 + zz
        return remote(g_ref.at[dp * 8 + 2 * zz + 1 - c], b1.at[i], s1.at[i], r1.at[i], d, pj)

    def stage2(zz, dp):
        i = dp * 4 + zz
        to = dx if zz % 2 == 0 else dy
        return remote(acc.at[i], b2.at[i], s2.at[i], r2.at[i], to, j)

    def stage3(zz):
        to = dy if zz % 2 == 0 else dx
        return remote(acc.at[to * 4 + zz], b3.at[zz], s3.at[zz], r3.at[zz], to, j)

    def stage4(k, zz, jz):
        return remote(acc.at[d * 4 + zz], b4.at[z], s4.at[k], r4.at[z], d, jz)

    def pcopy(zz):
        return remote(pb.at[2 * zz + 1 - c], q1.at[zz], ps.at[zz], pr.at[zz], d, pj)

    def tcopy(zz):
        return remote(pb.at[2 * zz + c], q2.at[zz], ts.at[zz], tr.at[zz], d, ja)

    def ucopy(k, zz):
        return remote(pb.at[2 * zz + c], dn_ref.at[g], us.at[k], ur.at[0], d, 2 * zz + c)

    def hcopy(k):
        slot = (me + k) % 32
        return remote(hs_buf.at[slot], hb.at[me], hs.at[k], hr.at[me], slot // 8, slot % 8)

    def part_of(dp):
        return vs_buf.at[:, pl.ds(pl.multiple_of(dp * LANES, LANES), LANES)]

    def vcopy(k):
        slot = (me + k) % 32
        return remote(part_of(slot // 8), vb.at[me], vs.at[k], vr.at[me], slot // 8, slot % 8)

    for zz, dp in first + rest:
        gcopy(zz, dp).start()

    def sums1():
        for k, (zz, dp) in enumerate(first + rest):
            gloads[k].wait()
            gcopy(zz, dp).wait_recv()
            add_into(acc.at[dp * 4 + zz], b1.at[dp * 4 + zz])
            if k < len(first):
                stage2(zz, dp).start()

    def sums2():
        for pick in (1, 0):
            for zz in range(4):
                dp = (d, dy if zz % 2 == 0 else dx)[pick]
                stage2(zz, dp).wait_recv()
                add_into(acc.at[dp * 4 + zz], b2.at[dp * 4 + zz])
                if pick:
                    stage3(zz).start()

    def sums3():
        for zz in range(4):
            stage3(zz).wait_recv()
            add_into(acc.at[d * 4 + zz], b3.at[zz])
        for k, (zz, jz) in enumerate(((za, ja), (zb, jb), (zc, jc))):
            stage4(k, zz, jz).start()

    def both_cores(zz):
        pcopy(zz).wait_recv()
        add_into(pb.at[2 * zz + c], q1.at[zz])

    def pass_on(k, zz):
        @pl.when(near)
        def _():
            tcopy(zz).wait_recv()
            add_into(pb.at[2 * zz + c], q2.at[zz])
            ucopy(k, zz).start()

    def to_near(zz):
        @pl.when(far)
        def _():
            tcopy(zz).start()

    def event0():
        both_cores(w3)
        to_near(w3)

    def event1():
        both_cores(w2)
        to_near(w2)
        pass_on(0, w3)

    def event2():
        both_cores(wn)
        to_near(wn)
        pass_on(1, w2)

    events = {(0, 3): sums1, (1, 4): sums2, (2, 0): event0, (2, 3): sums3, (4, 0): event1, (6, 0): event2}

    lane = lane_of(rows)
    low = upper(rows)
    left = lane < SIDE

    def prepare(b, _):
        do = do_ref[b].astype(F32)
        both = do * o32_ref[b]
        for h in range(2):
            mine = left if h == 0 else jnp.logical_not(left)
            delta = jnp.sum(jnp.where(mine, both, 0.0), -1, keepdims=True)
            a, bb, cc = three(delta)
            da[h, b] = beside(h, lane, do, (None, -a, -bb, -cc))
        qt[b] = jnp.where(left, qa[0, b], qa[1, b]).T
        kt[b] = jnp.where(left, ka[0, b], ka[1, b]).T
        dot[b] = do_ref[b].T
        dq[b] = jnp.zeros((LANES, rows), F32)
        dk[b] = jnp.zeros((LANES, rows), F32)
        dv[b] = jnp.zeros((LANES, rows), F32)
        return 0

    lax.fori_loop(0, blocks, prepare, 0)
    gain = gain_ref[...].astype(F32)
    dw[...] = jnp.zeros_like(dw)
    vs_buf[...] = sum_ref[...]

    def finish(b):
        x = x_ref[b].astype(F32)
        n1 = x * lax.rsqrt(jnp.mean(x * x, -1, keepdims=True) + EPS)
        n = (n1 * gain).astype(BF)
        q = (dq[b] * HEAD_DIM ** (-0.5)).astype(BF)
        k = (dk[b] * (1.0 / LOG2E)).astype(BF)
        pt = jnp.concatenate([q, k, dv[b].astype(BF)], axis=0)
        dw[...] += nn(pt, n)
        dn = nt(pt.T, w_ref[...])
        pb[b] = dn.astype(BF)
        vs_buf[0:1] += jnp.sum(dn * n1, 0, keepdims=True)

    def pair(kb, b, masked=False):
        for h in range(2):
            part = slice(h * SIDE, (h + 1) * SIDE)
            p = jnp.exp2(nt(ka[h, kb], qa[h, b]))
            if masked:
                p = jnp.where(low, p, 0.0)
            ds = (p * nt(va[h, kb], da[h, b])).astype(BF)
            dv[kb, part] += nt(dot[b, part], p.astype(BF))
            dk[kb, part] += nt(qt[b, part], ds)
            dq[b, part] += nn(kt[kb, part], ds)

    def outer(i, _):
        o = g * i + (1 - g) * (blocks - 1 - i)
        pair(o, o, True)

        def inner(t, _):
            pair(g * o + (1 - g) * (o - 1 - t), g * (o + 1 + t) + (1 - g) * o)
            for (ei, et), event in events.items():
                pl.when(jnp.logical_and(i == ei, t == et))(event)
            return 0

        lax.fori_loop(0, blocks - 1 - i, inner, 0)
        finish(o)

        @pl.when(o % 2 != c)
        def _():
            pcopy(o // 2).start()

        return 0

    lax.fori_loop(0, blocks, outer, 0)
    wide = dw[...].T.astype(BF)
    hs_buf[...] = wide.reshape(32, per, 3 * LANES)
    keep_h = pltpu.make_async_copy(hs_buf.at[me], hb.at[me], lo.at[0])
    keep_v = pltpu.make_async_copy(part_of(d), vb.at[me], lo.at[1])
    keep_h.start()
    keep_v.start()

    def hstart(k, _):
        hcopy(k).start()
        vcopy(k).start()
        return 0

    lax.fori_loop(1, 32, hstart, 0)
    both_cores(wf)

    @pl.when(near)
    def _():
        tcopy(wf).start()

    for zz in (za, zb, zc):
        remote(acc.at[0], b4.at[zz], s4.at[0], r4.at[zz], d, ja).wait_recv()
    gf_ref[...] = (
        acc[d * 4 + z].astype(F32)
        + b4[za].astype(F32) + b4[zb].astype(F32) + b4[zc].astype(F32)
    )
    keep_h.wait()
    keep_v.wait()

    def harrive(k, _):
        slot = (me + k) % 32
        remote(hs_buf.at[0], hb.at[slot], hs.at[0], hr.at[slot], d, pj).wait_recv()
        remote(part_of(d), vb.at[slot], vs.at[0], vr.at[slot], d, pj).wait_recv()
        return 0

    lax.fori_loop(1, 32, harrive, 0)
    total = jnp.zeros(gv_ref.shape, F32)
    for hi in range(4):
        part = jnp.zeros((per, 3 * LANES), F32)
        for k in range(8):
            slot = (k // 2) * 8 + (k % 2) * 4 + hi
            part += hb[slot].astype(F32)
            total += vb[slot]
        for m in range(3):
            gq_ref[m, :, hi * LANES : (hi + 1) * LANES] = part[:, m * LANES : (m + 1) * LANES]
    gv_ref[...] = total
    tcopy(z).wait_recv()

    def mine(i, _):
        piece = pl.ds(i * 128, 128)
        own[piece, :] = pb[j, piece, :] + q2[z, piece, :]
        return 0

    lax.fori_loop(0, rows // 128, mine, 0)
    keep = pltpu.make_async_copy(own, dn_ref.at[g], lo.at[2])
    keep.start()
    ucopy(0, w3).wait_recv()
    for zz, dp in first + rest:
        gcopy(zz, dp).wait_send()
    for zz, dp in first:
        stage2(zz, dp).wait_send()
    for zz in range(4):
        stage3(zz).wait_send()
        pcopy(zz).wait_send()
    for k, (zz, jz) in enumerate(((za, ja), (zb, jb), (zc, jc))):
        stage4(k, zz, jz).wait_send()

    def hsent(k, _):
        hcopy(k).wait_send()
        vcopy(k).wait_send()
        return 0

    lax.fori_loop(1, 32, hsent, 0)

    @pl.when(near)
    def _():
        tcopy(wf).wait_send()
        ucopy(0, w3).wait_send()
        ucopy(1, w2).wait_send()

    @pl.when(far)
    def _():
        for zz in (w3, w2, wn):
            tcopy(zz).wait_send()

    keep.wait()


def attend_back(xg, w, gain, o32, do, qa, ka, va, sums, grads):
    blocks, rows, width = xg.shape
    g = grads.shape[1:]
    per = width // 32
    dma = pltpu.SemaphoreType.DMA
    turned = pltpu.VMEM((blocks, LANES, rows), BF)
    total = pltpu.VMEM((blocks, LANES, rows), F32)
    return pl.pallas_call(
        attend_back_kernel,
        out_shape=(
            jax.ShapeDtypeStruct((2, rows, width), BF),
            jax.ShapeDtypeStruct(g, F32),
            jax.ShapeDtypeStruct((3, per, width), F32),
            jax.ShapeDtypeStruct((sums.shape[0], LANES), F32),
        ),
        in_specs=[INVM] * 9 + [ANY],
        out_specs=(ANY, INVM, INVM, INVM),
        scratch_shapes=[
            pltpu.VMEM((2, blocks, rows, LANES), BF), turned, turned, turned, total, total, total,
            pltpu.VMEM((3 * LANES, width), F32),
            pltpu.VMEM((blocks, rows, width), BF),
            pltpu.VMEM((32, per, 3 * LANES), BF),
            pltpu.VMEM(sums.shape, F32),
            pltpu.VMEM((16,) + g, BF),
            pltpu.VMEM((16,) + g, BF),
            pltpu.VMEM((16,) + g, BF),
            pltpu.VMEM((4,) + g, BF),
            pltpu.VMEM((4,) + g, BF),
            pltpu.VMEM((4, rows, width), BF),
            pltpu.VMEM((4, rows, width), BF),
            pltpu.VMEM((32, per, 3 * LANES), BF),
            pltpu.VMEM((32, sums.shape[0], LANES), F32),
            pltpu.VMEM((rows, width), BF),
            dma((16,)), dma((3,)),
            dma((16,)), dma((16,)), dma((16,)), dma((16,)), dma((4,)), dma((4,)), dma((4,)), dma((4,)),
            dma((4,)), dma((4,)), dma((4,)), dma((4,)), dma((2,)), dma((1,)),
            dma((32,)), dma((32,)), dma((32,)), dma((32,)),
        ],
        compiler_params=pltpu.CompilerParams(
            collective_id=3, has_side_effects=True, vmem_limit_bytes=VMEM_LIMIT
        ),
        name="attend_back",
    )(xg, w, gain, o32, do, qa, ka, va, sums, grads)


def by_heads(
    layer_input, cotangent, doc_len, doc_offset,
    w_query, w_key, w_value, w_out, w_gate_attn, w_gate_ffn, w_in, w_back,
    norm_attn, norm_ffn, bias_attn, bias_ffn,
):
    micro, _, rows, width = layer_input.shape
    per = w_query.shape[0]
    ff = w_in.shape[1] // width
    j = lax.axis_index("seq")
    x = layer_input[:, 0]
    cot = cotangent[:, 0]
    small = jnp.pad(
        jnp.stack([norm_attn, norm_ffn, bias_attn, bias_ffn] * 4), ((0, 0), (0, LANES - per))
    )
    mats = (w_query, w_key, w_value, w_out, w_gate_attn, w_gate_ffn, w_in, w_back)
    xg, wg, w, vecs, att, o32, qa, ka, va = front(doc_len, doc_offset, x, mats, small)
    gain = vecs[0:1]
    out, do, dh, dna, grads, sums = tokens(x, cot, att, wg, vecs)
    dn, gf, gq, gv = attend_back(xg, w, gain, o32, do, qa, ka, va, sums, grads)
    x32 = x.astype(F32)
    r1 = lax.rsqrt(jnp.mean(x32 * x32, -1, keepdims=True) + EPS)
    n1 = x32 * r1
    g1 = (dna + dn.astype(F32)) * gain.astype(F32)
    grad = dh + r1 * (g1 - n1 * jnp.mean(g1 * n1, -1, keepdims=True))
    gv = lax.dynamic_slice(gv, (0, lax.axis_index("seq") * per), (4, per))
    return (
        out[:, None],
        grad[:, None],
        gq[0], gq[1], gq[2],
        gf[:per], gf[per : 2 * per], gf[2 * per : 3 * per],
        gf[3 * per : (3 + ff) * per].reshape(ff, per, width).transpose(1, 0, 2).reshape(per, ff * width),
        gf[(3 + ff) * per :],
        gv[0], gv[1], gv[2], gv[3],
    )


def from_behind(x, axis, by):
    count = lax.axis_size(axis)
    pairs = [(i, i + by) for i in range(count) if 0 <= i + by < count]
    return lax.ppermute(x, axis, pairs)


def passed_along(value, axis, steps):
    count = lax.axis_size(axis)
    pairs = [(source, (source + steps) % count) for source in range(count)]
    return lax.ppermute(value, axis, pairs)


def rms_norm(values, gain):
    return values * lax.rsqrt(jnp.mean(values * values, -1, keepdims=True) + EPS) * gain


def dense(left, right):
    return jnp.dot(left, right, preferred_element_type=jnp.float32)


def dense_tn(left, right):
    return lax.dot_general(
        left, right, (((0,), (0,)), ((), ())), preferred_element_type=jnp.float32
    )


def dense_nt(left, right):
    return lax.dot_general(
        left, right, (((1,), (1,)), ((), ())), preferred_element_type=jnp.float32
    )


def layout_of(lengths, offsets, source, rows, filler):
    positions = source * rows + jnp.arange(rows, dtype=jnp.int32)
    region = positions // DOC_MAX
    inside = positions - region * DOC_MAX
    members = (region[:, None] == jnp.arange(lengths.shape[1], dtype=jnp.int32)[None, :]).astype(
        jnp.int32
    )
    begins = jnp.sum(members[None] * offsets[:, None, :], axis=2)
    spans = jnp.sum(members[None] * lengths[:, None, :], axis=2)
    inside_doc = (inside[None] >= begins) & (inside[None] < begins + spans)
    labels = jnp.where(inside_doc, region[None], filler)
    return (positions, labels, inside_doc)


def allowed_pairs(query_side, key_side):
    same_doc = query_side[1][:, :, None] == key_side[1][:, None, :]
    causal = key_side[0][None, None, :] <= query_side[0][None, :, None]
    return same_doc & causal


def absorb(carry, query, key_piece, value_piece, allowed):
    run_max, run_sum, totals = carry
    scores = jnp.einsum(
        "mqhd,mkhd->mhqk", query, key_piece, preferred_element_type=jnp.float32
    ) * HEAD_DIM ** (-0.5)
    scores = jnp.where(allowed[:, None], scores, -1e30)
    new_max = jnp.maximum(run_max, jnp.max(scores, axis=-1))
    factor = jnp.exp(run_max - new_max)
    weights = jnp.where(allowed[:, None], jnp.exp(scores - new_max[..., None]), 0.0)
    run_sum = run_sum * factor + jnp.sum(weights, axis=-1)
    totals = totals * factor[..., None] + jnp.einsum(
        "mhqk,mkhd->mhqd", weights, value_piece.astype(jnp.float32)
    )
    return (new_max, run_sum, totals)


def hop_grads(query, grad_att, lse, delta, key_piece, value_piece, allowed):
    scores = jnp.einsum(
        "mqhd,mkhd->mhqk", query, key_piece, preferred_element_type=jnp.float32
    ) * HEAD_DIM ** (-0.5)
    probs = jnp.where(allowed[:, None], jnp.exp(scores - lse[..., None]), 0.0)
    grad_value = jnp.einsum("mhqk,mqhd->mkhd", probs, grad_att.astype(jnp.float32))
    grad_probs = jnp.einsum(
        "mqhd,mkhd->mhqk", grad_att, value_piece, preferred_element_type=jnp.float32
    )
    grad_scores = probs * (grad_probs - delta[..., None]) * HEAD_DIM ** (-0.5)
    grad_query = jnp.einsum("mhqk,mkhd->mqhd", grad_scores, key_piece.astype(jnp.float32))
    grad_key = jnp.einsum("mhqk,mqhd->mkhd", grad_scores, query.astype(jnp.float32))
    return (grad_query, grad_key, grad_value)


def shards(
    layer_input,
    cotangent,
    doc_len,
    doc_offset,
    w_query,
    w_key,
    w_value,
    w_out,
    w_gate_attn,
    w_gate_ffn,
    w_in,
    w_back,
    norm_attn,
    norm_ffn,
    bias_attn,
    bias_ffn,
):
    gathered = (
        lax.all_gather(w_query, ("dp", "seq"), axis=0, tiled=True),
        lax.all_gather(w_key, ("dp", "seq"), axis=0, tiled=True),
        lax.all_gather(w_value, ("dp", "seq"), axis=0, tiled=True),
        lax.all_gather(w_out, ("dp", "seq"), axis=0, tiled=True),
        lax.all_gather(w_gate_attn, ("dp", "seq"), axis=0, tiled=True),
        lax.all_gather(w_gate_ffn, ("dp", "seq"), axis=0, tiled=True),
        lax.all_gather(w_in, ("dp", "seq"), axis=0, tiled=True),
        lax.all_gather(w_back, ("dp", "seq"), axis=0, tiled=True),
        lax.all_gather(norm_attn, ("dp", "seq"), axis=0, tiled=True),
        lax.all_gather(norm_ffn, ("dp", "seq"), axis=0, tiled=True),
        lax.all_gather(bias_attn, ("dp", "seq"), axis=0, tiled=True),
        lax.all_gather(bias_ffn, ("dp", "seq"), axis=0, tiled=True),
    )
    (
        full_query,
        full_key,
        full_value,
        full_out,
        full_gate_attn,
        full_gate_ffn,
        full_in,
        full_back,
        gain_attn,
        gain_ffn,
        shift_attn,
        shift_ffn,
    ) = gathered
    micro = layer_input.shape[0]
    rows = layer_input.shape[2]
    width = layer_input.shape[3]
    tokens = micro * rows
    nseq = lax.axis_size("seq")
    me_index = lax.axis_index("seq")
    hops = min(max(DOC_MAX // rows, 1), nseq) - 1
    lengths = doc_len[:, 0]
    offsets = doc_offset[:, 0]

    def key_side(source):
        positions, labels, _ = layout_of(lengths, offsets, source, rows, -2)
        return (positions, labels)

    own_layout = layout_of(lengths, offsets, me_index, rows, -1)
    query_side = (own_layout[0], own_layout[1])
    own_keys = key_side(me_index)
    inputs = layer_input[:, 0].reshape(tokens, width).astype(jnp.float32)
    normed_attn, pull_attn = jax.vjp(rms_norm, inputs, gain_attn.astype(jnp.float32))
    normed_low = normed_attn.astype(jnp.bfloat16)
    query = dense(normed_low, full_query).astype(jnp.bfloat16)
    keys = dense(normed_low, full_key).astype(jnp.bfloat16)
    values = dense(normed_low, full_value).astype(jnp.bfloat16)
    gate_attn = jax.nn.sigmoid(dense(normed_low, full_gate_attn) + shift_attn.astype(jnp.float32))
    head_shape = (micro, rows, HEADS, HEAD_DIM)
    query_h = query.reshape(head_shape)
    keys_h = keys.reshape(head_shape)
    values_h = values.reshape(head_shape)
    start_carry = (
        jnp.full((micro, HEADS, rows), -1e30, jnp.float32),
        jnp.zeros((micro, HEADS, rows), jnp.float32),
        jnp.zeros((micro, HEADS, rows, HEAD_DIM), jnp.float32),
    )
    carry = absorb(start_carry, query_h, keys_h, values_h, allowed_pairs(query_side, own_keys))

    def forward_hop(hop, state):
        pieces, inner = state
        pieces = from_behind((pieces[0], pieces[1]), "seq", 1)
        source = me_index - hop
        inner = absorb(
            inner, query_h, pieces[0], pieces[1], allowed_pairs(query_side, key_side(source))
        )
        return (pieces, inner)

    _, (run_max, run_sum, totals) = lax.fori_loop(
        1, hops + 1, forward_hop, ((keys_h, values_h), carry)
    )
    live = own_layout[2][:, None, :]
    safe_sum = jnp.where(live, run_sum, 1.0)
    attended_h = jnp.where(live[..., None], totals / safe_sum[..., None], 0.0)
    lse = jnp.where(live, run_max + jnp.log(safe_sum), 0.0)
    attended32 = attended_h.transpose(0, 2, 1, 3).reshape(tokens, width)
    attended = attended32.astype(jnp.bfloat16)
    branch_attn = dense(attended, full_out)
    hidden = gate_attn * branch_attn + (1.0 - gate_attn) * inputs
    normed_ffn, pull_ffn = jax.vjp(rms_norm, hidden, gain_ffn.astype(jnp.float32))
    normed_ffn_low = normed_ffn.astype(jnp.bfloat16)
    pre = dense(normed_ffn_low, full_in)
    act32, pull_gelu = jax.vjp(partial(jax.nn.gelu, approximate=True), pre)
    act = act32.astype(jnp.bfloat16)
    branch_ffn = dense(act, full_back)
    gate_ffn = jax.nn.sigmoid(dense(normed_ffn_low, full_gate_ffn) + shift_ffn.astype(jnp.float32))
    output = gate_ffn * branch_ffn + (1.0 - gate_ffn) * hidden
    again = (
        lax.all_gather(w_query, ("dp", "seq"), axis=0, tiled=True),
        lax.all_gather(w_key, ("dp", "seq"), axis=0, tiled=True),
        lax.all_gather(w_value, ("dp", "seq"), axis=0, tiled=True),
        lax.all_gather(w_out, ("dp", "seq"), axis=0, tiled=True),
        lax.all_gather(w_gate_attn, ("dp", "seq"), axis=0, tiled=True),
        lax.all_gather(w_gate_ffn, ("dp", "seq"), axis=0, tiled=True),
        lax.all_gather(w_in, ("dp", "seq"), axis=0, tiled=True),
        lax.all_gather(w_back, ("dp", "seq"), axis=0, tiled=True),
        lax.all_gather(norm_attn, ("dp", "seq"), axis=0, tiled=True),
        lax.all_gather(norm_ffn, ("dp", "seq"), axis=0, tiled=True),
        lax.all_gather(bias_attn, ("dp", "seq"), axis=0, tiled=True),
        lax.all_gather(bias_ffn, ("dp", "seq"), axis=0, tiled=True),
    )
    (
        back_query,
        back_key,
        back_value,
        back_out,
        back_gate_attn,
        back_gate_ffn,
        back_in,
        back_back,
        _,
        _,
        _,
        _,
    ) = again
    upstream = cotangent[:, 0].reshape(tokens, width).astype(jnp.float32)
    d_logit_ffn = (upstream * (branch_ffn - hidden) * gate_ffn * (1.0 - gate_ffn)).astype(
        jnp.bfloat16
    )
    d_branch_ffn = (upstream * gate_ffn).astype(jnp.bfloat16)
    grad_back = dense_tn(act, d_branch_ffn)
    (d_pre32,) = pull_gelu(dense_nt(d_branch_ffn, back_back))
    d_pre = d_pre32.astype(jnp.bfloat16)
    grad_in = dense_tn(normed_ffn_low, d_pre)
    grad_gate_ffn = dense_tn(normed_ffn_low, d_logit_ffn)
    grad_bias_ffn = jnp.sum(d_logit_ffn.astype(jnp.float32), axis=0)
    d_normed_ffn = dense_nt(d_pre, back_in) + dense_nt(d_logit_ffn, back_gate_ffn)
    d_hidden_norm, grad_gain_ffn = pull_ffn(d_normed_ffn)
    d_hidden = upstream * (1.0 - gate_ffn) + d_hidden_norm
    d_branch_attn = (d_hidden * gate_attn).astype(jnp.bfloat16)
    d_logit_attn = (d_hidden * (branch_attn - inputs) * gate_attn * (1.0 - gate_attn)).astype(
        jnp.bfloat16
    )
    grad_out = dense_tn(attended, d_branch_attn)
    d_attended = dense_nt(d_branch_attn, back_out).astype(jnp.bfloat16)
    grad_att = d_attended.reshape(head_shape)
    delta = jnp.einsum(
        "mqhd,mqhd->mhq", grad_att.astype(jnp.float32), attended32.reshape(head_shape)
    )
    first_q, first_k, first_v = hop_grads(
        query_h, grad_att, lse, delta, keys_h, values_h, allowed_pairs(query_side, own_keys)
    )

    def backward_hop(hop, state):
        pieces, moving, grad_q = state
        pieces = from_behind((pieces[0], pieces[1]), "seq", 1)
        moving = (
            passed_along(moving[0].astype(jnp.bfloat16), "seq", 1).astype(jnp.float32),
            passed_along(moving[1].astype(jnp.bfloat16), "seq", 1).astype(jnp.float32),
        )
        source = me_index - hop
        step_q, step_k, step_v = hop_grads(
            query_h,
            grad_att,
            lse,
            delta,
            pieces[0],
            pieces[1],
            allowed_pairs(query_side, key_side(source)),
        )
        return (pieces, (moving[0] + step_k, moving[1] + step_v), grad_q + step_q)

    _, moving, grad_q = lax.fori_loop(
        1, hops + 1, backward_hop, ((keys_h, values_h), (first_k, first_v), first_q)
    )
    moving = (
        passed_along(moving[0].astype(jnp.bfloat16), "seq", -hops).astype(jnp.float32),
        passed_along(moving[1].astype(jnp.bfloat16), "seq", -hops).astype(jnp.float32),
    )
    grad_k, grad_v = moving
    d_query = grad_q.reshape(tokens, width).astype(jnp.bfloat16)
    d_key = grad_k.reshape(tokens, width).astype(jnp.bfloat16)
    d_value = grad_v.reshape(tokens, width).astype(jnp.bfloat16)
    grad_query = dense_tn(normed_low, d_query)
    grad_key = dense_tn(normed_low, d_key)
    grad_value = dense_tn(normed_low, d_value)
    grad_gate_attn = dense_tn(normed_low, d_logit_attn)
    grad_bias_attn = jnp.sum(d_logit_attn.astype(jnp.float32), axis=0)
    d_normed_attn = (
        dense_nt(d_query, back_query)
        + dense_nt(d_key, back_key)
        + dense_nt(d_value, back_value)
        + dense_nt(d_logit_attn, back_gate_attn)
    )
    d_inputs_norm, grad_gain_attn = pull_attn(d_normed_attn)
    grad_input = d_hidden * (1.0 - gate_attn) + d_inputs_norm
    owned = (
        lax.psum_scatter(grad_query, ("dp", "seq"), scatter_dimension=0, tiled=True),
        lax.psum_scatter(grad_key, ("dp", "seq"), scatter_dimension=0, tiled=True),
        lax.psum_scatter(grad_value, ("dp", "seq"), scatter_dimension=0, tiled=True),
        lax.psum_scatter(grad_out, ("dp", "seq"), scatter_dimension=0, tiled=True),
        lax.psum_scatter(grad_gate_attn, ("dp", "seq"), scatter_dimension=0, tiled=True),
        lax.psum_scatter(grad_gate_ffn, ("dp", "seq"), scatter_dimension=0, tiled=True),
        lax.psum_scatter(grad_in, ("dp", "seq"), scatter_dimension=0, tiled=True),
        lax.psum_scatter(grad_back, ("dp", "seq"), scatter_dimension=0, tiled=True),
        lax.psum_scatter(grad_gain_attn, ("dp", "seq"), scatter_dimension=0, tiled=True),
        lax.psum_scatter(grad_gain_ffn, ("dp", "seq"), scatter_dimension=0, tiled=True),
        lax.psum_scatter(grad_bias_attn, ("dp", "seq"), scatter_dimension=0, tiled=True),
        lax.psum_scatter(grad_bias_ffn, ("dp", "seq"), scatter_dimension=0, tiled=True),
    )
    return (
        output.reshape(micro, 1, rows, width).astype(jnp.bfloat16),
        grad_input.reshape(micro, 1, rows, width),
        owned[0],
        owned[1],
        owned[2],
        owned[3],
        owned[4],
        owned[5],
        owned[6],
        owned[7],
        owned[8],
        owned[9],
        owned[10],
        owned[11],
    )


def solution(mesh):
    placed = (
        P(None, "dp", "seq", None),
        P(None, "dp", "seq", None),
        P(None, "dp", None),
        P(None, "dp", None),
        P(("dp", "seq"), None),
        P(("dp", "seq"), None),
        P(("dp", "seq"), None),
        P(("dp", "seq"), None),
        P(("dp", "seq"), None),
        P(("dp", "seq"), None),
        P(("dp", "seq"), None),
        P(("dp", "seq"), None),
        P(("dp", "seq")),
        P(("dp", "seq")),
        P(("dp", "seq")),
        P(("dp", "seq")),
    )
    def pick(layer_input, *others):
        micro, _, rows, width = layer_input.shape
        fits = (
            dict(mesh.shape) == {"dp": 4, "seq": 8}
            and micro == 2
            and others[1].shape[2] == 1
            and width == HEADS * HEAD_DIM
            and width == 4 * LANES
            and rows % 128 == 0
            and others[10].shape == (width // 8, width)
        )
        return (by_heads if fits else shards)(layer_input, *others)

    return jax.shard_map(
        pick,
        mesh=mesh,
        in_specs=placed,
        out_specs=(
            P(None, "dp", "seq", None),
            P(None, "dp", "seq", None),
            P(("dp", "seq"), None),
            P(("dp", "seq"), None),
            P(("dp", "seq"), None),
            P(("dp", "seq"), None),
            P(("dp", "seq"), None),
            P(("dp", "seq"), None),
            P(("dp", "seq"), None),
            P(("dp", "seq"), None),
            P(("dp", "seq")),
            P(("dp", "seq")),
            P(("dp", "seq")),
            P(("dp", "seq")),
        ),
        check_vma=False,
    )
```
